128 devices in a mesh: depth: 32 (over z, x, core), batch: 4 (over y).
Axes of the slice: x: 4, y: 4, z: 4, core: 2. Of those that a mesh axis runs over, the one named last changes fastest.
Arguments:
- cpoint_guess: float32 [32, 4, 32, 4096], P('depth', 'batch'), may hold values from -6 to 6
- adjoint_guess: float32 [32, 4, 32, 4096], P('depth', 'batch'), may hold values from -6 to 6
- weights: float32 [256, 32, 32], P('depth'), may hold values from -0.5 to 0.5
- biases: float32 [256, 32], P('depth'), may hold values from -3 to 3
- diffusion: float32 [32], replicated, may hold values from 0.02 to 0.25
- section_len: int32 [32], replicated, may hold values from 1 to 8, 96 in all
Outputs:
- states_out: float32 [32, 4, 32, 4096], P('depth', 'batch')
- adjoint_out: float32 [32, 4, 32, 4096], P('depth', 'batch')
- grad_weights: float32 [256, 32, 32], P('depth')
- grad_biases: float32 [256, 32], P('depth')
The draws below stay inside these ranges and needn't reach their ends.
Inputs may be any that keep to these rules, and one draw needn't show every extreme that they name: `section_len`: each of the 32 sections holds 1 to 8 layers, 96 in all, and one section holds exactly 8.
All inputs are finite; a program needn't handle non-finite values.
Results may differ from the reference program's by a relative error of at most 0.0003.
Values sent between devices are 32-bit elements; how exact they have to be, the bound alone decides.
A program may use at most 128 MiB of HBM per device.

```python
import math
import jax
import jax.numpy as jnp
import numpy as np
from jax import lax

C = 32
IMG_H = 64
IMG_W = 64
PIX = 4096
MOST = 8
LAYERS = 96
IMAGES = 4
N_DEPTH = 32


def steps_of(stream_key, shape, shards, smallest, top_value):
    gain, own = 1.0, jax.random.fold_in(stream_key, 6)
    for axis_at, parts in shards:
        steps = jnp.exp(jax.random.uniform(jax.random.fold_in(own, axis_at), (parts,), jnp.float32, smallest / len(shards), top_value / len(shards)))
        gain = gain * jnp.repeat(steps, shape[axis_at] // parts).reshape([-1 if axis == axis_at else 1 for axis in range(len(shape))])
    return gain


def length_profile(count, total, bound, slope):
    weights = [(1 << 20) // math.isqrt(rank ** slope) + 1 for rank in range(2, count + 1)]
    surplus, holding = total - bound - (count - 1), [1] * (count - 1)
    while surplus > 0:
        free = [i for i in range(count - 1) if holding[i] < bound]
        pool, budget = sum([weights[i] for i in free]), surplus
        for i in free:
            addition = min(bound - holding[i], max(1, budget * weights[i] // pool), surplus)
            holding[i] = holding[i] + addition
            surplus = surplus - addition
    return np.array([bound] + holding)


def uneven(key, number_of, total, reach, slope):
    if number_of == 2:
        one = jax.random.randint(key, (), max(1, total - reach), min(reach, total - 1) + 1)
        return jnp.stack([one, total - one])
    tallies = jnp.asarray(length_profile(number_of, total, reach, slope), jnp.int32)
    couples = (number_of - 1) // 2
    giver, taker = tallies[1:1 + 2 * couples:2], tallies[2:2 + 2 * couples:2]
    slack = jnp.minimum(giver - 1, reach - taker)
    moved = jax.random.randint(jax.random.fold_in(key, 1), (couples,), 0, 1 << 20) % (slack + 1)
    tallies = tallies.at[1:1 + 2 * couples:2].set(giver - moved).at[2:2 + 2 * couples:2].set(taker + moved)
    return tallies[jax.random.permutation(jax.random.fold_in(key, 2), number_of)]


def normal_values(stream_key, dims, scale, reach, cuts=(), dtype=jnp.bfloat16):
    array = scale * jax.random.normal(stream_key, dims, jnp.float32)
    if cuts:
        array = array * steps_of(stream_key, dims, cuts, -0.22, 0.18)
    return jnp.clip(array, -reach, reach).astype(dtype)


def setup_inputs(seed: int = 0) -> dict:
    arg_keys = jax.random.split(jax.random.key(seed), 7)
    cpoint_guess = normal_values(arg_keys[0], (N_DEPTH, IMAGES, C, PIX), 1.0, 6.0, ((0, 32), (1, 4)), jnp.float32)
    adjoint_guess = normal_values(arg_keys[1], (N_DEPTH, IMAGES, C, PIX), 1.0, 6.0, ((0, 32), (1, 4)), jnp.float32)
    weights = normal_values(arg_keys[2], (N_DEPTH * MOST, C, C), (4 * C) ** -0.5, 0.5, ((0, 32),), jnp.float32)
    biases = normal_values(arg_keys[3], (N_DEPTH * MOST, C), 0.5, 3.0, ((0, 32),), jnp.float32)
    diffusion = jnp.clip(jnp.exp(jax.random.uniform(arg_keys[4], (C,), jnp.float32, math.log(0.02), math.log(0.25))), 0.02, 0.25)
    section_len = uneven(arg_keys[5], N_DEPTH, LAYERS, MOST, 2).astype(jnp.int32)
    return dict(cpoint_guess=cpoint_guess, adjoint_guess=adjoint_guess, weights=weights, biases=biases, diffusion=diffusion, section_len=section_len)


def laplace(states):
    shaped = states.reshape(states.shape[:-1] + (IMG_H, IMG_W))
    padded = jnp.pad(shaped, [(0, 0)] * (shaped.ndim - 2) + [(1, 1), (1, 1)])
    beside_all = padded[..., 2:, 1:-1] + padded[..., :-2, 1:-1] + padded[..., 1:-1, 2:] + padded[..., 1:-1, :-2]
    return (beside_all - 4.0 * shaped).reshape(states.shape)

def apply_layer(states, matrix, offset, diffusion, factor):
    pre_act = jnp.einsum('ij,bjp->bip', matrix, states, precision=lax.Precision.HIGHEST) + offset[None, :, None]
    mixed = jnp.einsum('ji,bjp->bip', matrix, jnp.tanh(pre_act), precision=lax.Precision.HIGHEST)
    return states + (factor * diffusion)[None, :, None] * laplace(states) - factor * mixed

def fine_factor():
    return jnp.asarray(1.0, jnp.float32) / MOST

def section(states, matrices, offsets, diffusion, layer_count):
    factor = fine_factor()

    def advance(position, current):
        changed = apply_layer(current, matrices[position], offsets[position], diffusion, factor)
        return jnp.where(position < layer_count - 1, changed, current)
    relaxed = lax.fori_loop(0, MOST - 1, advance, states)
    final_slot = layer_count - 1
    return apply_layer(relaxed, matrices[final_slot], offsets[final_slot], diffusion, factor)

def coarse(states, matrix, offset, diffusion, layer_count):
    factor = layer_count.astype(jnp.float32) / MOST
    return apply_layer(states, matrix, offset, diffusion, factor)

def reference(cpoint_guess, adjoint_guess, weights, biases, diffusion, section_len):
    sections = N_DEPTH
    matrices = weights.reshape(sections, MOST, C, C)
    offsets = biases.reshape(sections, MOST, C)

    def forward_one(packed):
        states, mats, offs, layer_count = packed
        return section(states, mats, offs, diffusion, layer_count)
    pushed = lax.map(forward_one, (cpoint_guess, matrices, offsets, section_len))
    cpoints = jnp.concatenate([cpoint_guess[:1], pushed[:-1]], 0)
    second = lax.map(forward_one, (cpoints, matrices, offsets, section_len))

    def tau_one(packed):
        states, mat, off, layer_count = packed
        return coarse(states, mat, off, diffusion, layer_count)
    anchors = lax.map(tau_one, (cpoints, matrices[:, 0], offsets[:, 0], section_len))
    taus = second - anchors

    def coarse_step(current, packed):
        mat, off, layer_count, tau_here = packed
        return (coarse(current, mat, off, diffusion, layer_count) + tau_here, current)
    _, states_out = lax.scan(coarse_step, cpoints[0], (matrices[:, 0], offsets[:, 0], section_len, taus))

    def back_start(packed):
        states, mats, offs, layer_count, cotangent = packed
        _, pullback = jax.vjp(lambda start_state: section(start_state, mats, offs, diffusion, layer_count), states)
        return pullback(cotangent)[0]
    lam_start = lax.map(back_start, (cpoints, matrices, offsets, section_len, adjoint_guess))
    lam_end = jnp.concatenate([lam_start[1:], adjoint_guess[-1:]], 0)

    def back_full(packed):
        states, mats, offs, layer_count, cotangent = packed
        _, pullback = jax.vjp(lambda start_state, mat_all, off_all: section(start_state, mat_all, off_all, diffusion, layer_count), states, mats, offs)
        return pullback(cotangent)
    adjoint_out, grad_mats, grad_offs = lax.map(back_full, (cpoints, matrices, offsets, section_len, lam_end))
    return (states_out, adjoint_out, grad_mats.reshape(sections * MOST, C, C), grad_offs.reshape(sections * MOST, C))
```

```python
import jax
import jax.numpy as jnp
from jax import lax
from jax.experimental import pallas as pl
from jax.experimental.pallas import tpu as pltpu
from jax.sharding import PartitionSpec as P

MOST = 8
C = 32
LANES = 128
F = jnp.float32
BF = jnp.bfloat16
NT = (((1,), (1,)), ((), ()))


def split2(x):
    hi = x.astype(BF)
    return hi, (x - hi.astype(F)).astype(BF)


def dot3(packed, x):
    hi, lo = split2(x)
    return jnp.dot(packed, jnp.concatenate([hi, lo, hi], axis=0), preferred_element_type=F)


def pack3(matrix):
    hi, lo = split2(matrix)
    return jnp.concatenate([hi, hi, lo], axis=1)


def lane_masks():
    lane = lax.broadcasted_iota(jnp.int32, (C, LANES), 1)
    return lane < 64, lane % 64 == 0, lane % 64 == 63


def beside(x, masks):
    zero = jnp.zeros_like(x)
    return jnp.where(masks[1], zero, pltpu.roll(x, 1, 1)) + jnp.where(masks[2], zero, pltpu.roll(x, 127, 1))


def chunk_laps(chunks, count, masks):
    turned = [pltpu.roll(x, 64, 1) for x in chunks]
    laps = []
    for k in range(1, count + 1):
        above_below = turned[k] + jnp.where(masks[0], turned[k - 1], turned[k + 1])
        laps.append((above_below + beside(chunks[k], masks)) - 4.0 * chunks[k])
    return laps


def column_of(row, eye):
    return jnp.sum(jnp.where(eye, jnp.broadcast_to(row, (C, C)), 0.0), axis=1, keepdims=True)


def row_of(column, eye):
    return jnp.sum(jnp.where(eye, jnp.broadcast_to(column, (C, C)), 0.0), axis=0, keepdims=True)


def spread(matrix, out_ref):
    for k in range(C):
        out_ref[k] = jnp.broadcast_to(matrix[:, k : k + 1], (C, LANES))


def mix(spread_ref, x, first):
    sums = [first, None]
    for k in range(C):
        term = spread_ref[k] * jnp.broadcast_to(x[k : k + 1, :], (C, LANES))
        sums[k % 2] = term if sums[k % 2] is None else sums[k % 2] + term
    return sums[0] + sums[1]


def kernel(
    guess_ref, adj_ref, w_ref, b_ref, d_ref, n_ref,
    s_out, a_out, gw_out, gb_out,
    A, T, G, LR, PUSH, LSEND, S, S1, S2, TAU_S, TAU_B,
    WC, WT, BB, FD, WP, BP, SPA, SPAT, SPB, SPBT, CB, GB, GR,
    push_s, push_r, lam_s, lam_r, tau_s, tau_r, par_s, par_r, one_s, two_s, st_r, grad_s, grad_r,
):
    sections, images = lax.axis_size("depth"), lax.axis_size("batch")
    d, image = lax.axis_index("depth"), lax.axis_index("batch")
    chunks = guess_ref.shape[1] // LANES
    NB = min(16, chunks)
    blocks = chunks // NB
    core, chip, chips = d % 2, d // 2, sections // 2
    has_prev, has_next = d > 0, d < sections - 1
    even = core == 0
    odd = core == 1
    early, middle = chips // 4, (9 * chips) // 16
    masks = lane_masks()
    eye = lax.broadcasted_iota(jnp.int32, (C, C), 0) == lax.broadcasted_iota(jnp.int32, (C, C), 1)

    def at(c):
        return pl.ds(pl.multiple_of(c * LANES, LANES), LANES)

    def copy(src, dst, ssem, rsem, depth_to, image_to=None):
        return pltpu.make_async_remote_copy(
            src_ref=src, dst_ref=dst, send_sem=ssem, recv_sem=rsem,
            device_id=(depth_to, image if image_to is None else image_to),
            device_id_type=pl.DeviceIdType.MESH,
        )

    barrier = pltpu.get_barrier_semaphore()

    def greet(cond, depth_to, image_to):
        @pl.when(cond)
        def _():
            pl.semaphore_signal(barrier, inc=1, device_id=(depth_to, image_to), device_id_type=pl.DeviceIdType.MESH)

    up2, down2 = jnp.logical_and(even, chip < chips - 1), jnp.logical_and(even, chip > 0)
    greet(has_prev, d - 1, image)
    greet(has_next, d + 1, image)
    greet(up2, d + 2, image)
    greet(down2, d - 2, image)
    for o in range(1, images):
        pl.semaphore_signal(
            barrier, inc=1, device_id=(d, (image + o) % images), device_id_type=pl.DeviceIdType.MESH
        )
    partners = (
        has_prev.astype(jnp.int32) + has_next.astype(jnp.int32) + up2.astype(jnp.int32)
        + down2.astype(jnp.int32) + (images - 1)
    )

    n = n_ref[d]
    diff_col = column_of(d_ref[...], eye)
    diff = jnp.broadcast_to(diff_col, (C, LANES))

    def prepare(i, _):
        factor = jnp.where(i < n, 1.0 / MOST, 0.0)
        WC[i] = pack3(w_ref[i])
        WT[i] = pack3(w_ref[i].T * factor)
        BB[i] = jnp.broadcast_to(column_of(b_ref[pl.ds(i, 1), :], eye), (C, LANES))
        FD[i] = diff * factor
        return 0

    lax.fori_loop(0, MOST, prepare, 0)
    zero_chunk = jnp.zeros((C, LANES), F)
    for l in range(MOST + 1):
        A[l, 0] = zero_chunk
        A[l, chunks + 1] = zero_chunk
    for ref in (G.at[0], G.at[1], LR):
        ref[0] = zero_chunk
        ref[chunks + 1] = zero_chunk
    S[chunks] = zero_chunk
    for c in range(chunks):
        G[0, c + 1] = guess_ref[:, c * LANES : (c + 1) * LANES]

    def forward_block(src, i, j, store, keep):
        u = [src[j * NB + k] for k in range(NB + 2)]
        laps = chunk_laps(u, NB, masks)
        bias = jnp.concatenate([BB[i]] * NB, axis=1)
        act = jnp.tanh(dot3(WC[i], jnp.concatenate(u[1:-1], axis=1)) + bias)
        mixed = dot3(WT[i], act)
        fd = FD[i]
        for k in range(NB):
            store(j * NB + k, u[k + 1] + fd * laps[k] - mixed[:, k * LANES : (k + 1) * LANES])
            if keep is not None:
                keep[j * NB + k] = act[:, k * LANES : (k + 1) * LANES]

    def into(ref, shift):
        def store(c, value):
            ref[c + shift] = value
        return store

    def forward_layer(src, i, store, keep=None, unroll=True):
        def block(j, _):
            forward_block(src, i, j, store, keep)
            return 0
        lax.fori_loop(0, blocks, block, 0, unroll=unroll)

    def first_pass(i, _):
        forward_layer(G.at[i % 2], i, into(G.at[(i + 1) % 2], 1))
        return 0

    lax.fori_loop(0, MOST - 1, first_pass, 0)
    pl.semaphore_wait(barrier, partners)

    def push_copy(j):
        return copy(
            PUSH.at[pl.ds(j * NB, NB)], A.at[0, pl.ds(1 + j * NB, NB)], push_s.at[j], push_r.at[j], d + 1
        )

    def push_block(j, _):
        forward_block(G.at[(MOST - 1) % 2], MOST - 1, j, into(PUSH, 0), None)

        @pl.when(has_next)
        def _():
            push_copy(j).start()
        return 0

    lax.fori_loop(0, blocks, push_block, 0)

    weight_copy = copy(w_ref.at[0], WP, par_s.at[0], par_r.at[0], d - 1)
    bias_copy = copy(b_ref, BP, par_s.at[1], par_r.at[1], d - 1)

    @pl.when(odd)
    def _():
        weight_copy.start()
        bias_copy.start()

    @pl.when(even)
    def _():
        coarse_a = n.astype(F) / MOST
        spread(w_ref[0], SPA)
        spread(w_ref[0].T * coarse_a, SPAT)
        CB[0] = BB[0]
        CB[1] = diff * coarse_a
        weight_copy.wait_recv()
        bias_copy.wait_recv()
        coarse_b = n_ref[d + 1 - core].astype(F) / MOST
        spread(WP[...], SPB)
        spread(WP[...].T * coarse_b, SPBT)
        CB[2] = jnp.broadcast_to(column_of(BP[0:1, :], eye), (C, LANES))
        CB[3] = diff * coarse_b

    @pl.when(has_prev)
    def _():
        for j in range(blocks):
            push_copy(j).wait_recv()

    @pl.when(jnp.logical_not(has_prev))
    def _():
        for c in range(chunks):
            A[0, c + 1] = guess_ref[:, c * LANES : (c + 1) * LANES]

    def second_pass(i, _):
        forward_layer(A.at[i], i, into(A.at[i + 1], 1), T.at[i])
        return 0

    lax.fori_loop(0, MOST, second_pass, 0)

    layers = n.astype(F)

    def tau_of(c):
        start = A[0, c + 1]
        return A[MOST, c + 1] - (start + layers * (A[1, c + 1] - start))

    def tau_copy(j):
        return copy(PUSH2.at[pl.ds(j * NB, NB)], TAU_B.at[pl.ds(j * NB, NB)], tau_s.at[j], tau_r.at[j], d - 1)

    PUSH2 = TAU_S
    sends_tau = jnp.logical_and(odd, has_next)

    @pl.when(sends_tau)
    def _():
        def tau_block(j, _):
            for k in range(NB):
                PUSH2[j * NB + k] = tau_of(j * NB + k)
            tau_copy(j).start()
            return 0
        lax.fori_loop(0, blocks, tau_block, 0)

    @pl.when(even)
    def _():
        before = zero_chunk
        for c in range(chunks):
            turned = pltpu.roll(tau_of(c), 64, 1)
            TAU_S[c] = jnp.where(masks[0], before, turned)
            before = turned
        TAU_S[chunks] = jnp.where(masks[0], before, 0.0)

    def one_copy(c):
        return copy(S1.at[c], S.at[c], one_s.at[c], st_r.at[c], d + 1)

    def two_copy(c):
        return copy(S2.at[c], S.at[c], two_s.at[c], st_r.at[c], d + 2)

    def relay():
        @pl.when(chip == 0)
        def _():
            for c in range(chunks):
                S[c] = guess_ref[:, c * LANES : (c + 1) * LANES]

        @pl.when(chip < chips - 1)
        def _():
            for j in range(blocks):
                tau_copy(j).wait_recv()

        bias_a, fd_a, bias_b, fd_b = CB[0], CB[1], CB[2], CB[3]

        def step(c, carry, first=False, last=False):
            prev, prev_turned, one_prev, one_turned = carry
            if not last:
                @pl.when(chip > 0)
                def _():
                    two_copy(c).wait_recv()
            now = S[c]
            turned = pltpu.roll(now, 64, 1)
            mid = jnp.where(masks[0], prev_turned, turned)
            act = jnp.tanh(mix(SPA, mid, bias_a))
            lap = ((prev + now) + beside(mid, masks)) - 4.0 * mid
            one = (mid + fd_a * lap + TAU_S[c]) - mix(SPAT, act, None)
            if first:
                one = jnp.where(masks[0], 0.0, one)
            if last:
                one = jnp.where(masks[0], one, 0.0)
            turned_one = pltpu.roll(one, 64, 1)
            if not first:
                mid_one = jnp.where(masks[0], one_turned, turned_one)
                S1[c - 1] = mid_one
                one_copy(c - 1).start()

                @pl.when(chip < chips - 1)
                def _():
                    act_b = jnp.tanh(mix(SPB, mid_one, bias_b))
                    lap_b = ((one_prev + one) + beside(mid_one, masks)) - 4.0 * mid_one
                    S2[c - 1] = (mid_one + fd_b * lap_b + TAU_B[c - 1]) - mix(SPBT, act_b, None)
                    two_copy(c - 1).start()
            return now, turned, one, turned_one

        carry = step(0, (zero_chunk,) * 4, first=True)
        carry = lax.fori_loop(1, chunks, step, carry)
        step(chunks, carry, last=True)

    def backward_block(src, i, j, store, with_grads):
        g = [src[j * NB + k] for k in range(NB + 2)]
        laps = chunk_laps(g, NB, masks)
        act = jnp.concatenate([T[i, j * NB + k] for k in range(NB)], axis=1)
        g_hi, g_lo = split2(jnp.concatenate(g[1:-1], axis=1))
        pulled = jnp.dot(WC_T(i), jnp.concatenate([g_hi, g_lo, g_hi], axis=0), preferred_element_type=F)
        pre = (1.0 - act * act) * pulled
        p_hi, p_lo = split2(pre)
        back = jnp.dot(WT[i], jnp.concatenate([p_hi, p_lo, p_hi], axis=0), preferred_element_type=F)
        fd = FD[i]
        for k in range(NB):
            store(j * NB + k, g[k + 1] + fd * laps[k] - back[:, k * LANES : (k + 1) * LANES])
        if not with_grads:
            return None
        t_hi, t_lo = split2(act)
        u_hi, u_lo = split2(jnp.concatenate([A[i, j * NB + k + 1] for k in range(NB)], axis=1))
        left = jnp.concatenate(
            [jnp.concatenate([t_hi, p_hi], axis=1), jnp.concatenate([t_lo, p_lo], axis=1)], axis=0
        )
        right = jnp.concatenate(
            [jnp.concatenate([g_hi, u_hi], axis=1), jnp.concatenate([g_lo, u_lo], axis=1)], axis=0
        )
        prod = lax.dot_general(left, right, NT, preferred_element_type=F)
        bias_sum = pre[:, :LANES]
        for k in range(1, NB):
            bias_sum = bias_sum + pre[:, k * LANES : (k + 1) * LANES]
        return prod, bias_sum

    def WC_T(i):
        return WC[i]

    def lam_copy(j):
        return copy(LSEND.at[pl.ds(j * NB, NB)], LR.at[pl.ds(1 + j * NB, NB)], lam_s.at[j], lam_r.at[j], d - 1)

    def backward_start():
        for c in range(chunks):
            G[0, c + 1] = adj_ref[:, c * LANES : (c + 1) * LANES]

        def layer(i, _):
            def block(j, _):
                backward_block(G.at[i % 2], MOST - 1 - i, j, into(G.at[(i + 1) % 2], 1), False)
                return 0
            lax.fori_loop(0, blocks, block, 0, unroll=True)
            return 0

        lax.fori_loop(0, MOST - 1, layer, 0)

        def block(j, _):
            backward_block(G.at[(MOST - 1) % 2], 0, j, into(LSEND, 0), False)

            @pl.when(has_prev)
            def _():
                lam_copy(j).start()
            return 0

        lax.fori_loop(0, blocks, block, 0)

    def backward_full():
        @pl.when(has_next)
        def _():
            for j in range(blocks):
                lam_copy(j).wait_recv()

        @pl.when(jnp.logical_not(has_next))
        def _():
            for c in range(chunks):
                LR[c + 1] = adj_ref[:, c * LANES : (c + 1) * LANES]

        for c in range(chunks):
            G[0, c + 1] = LR[c + 1]
        GB[MOST] = jnp.zeros((C, C), F)

        def layer(i, _):
            slot = MOST - 1 - i
            factor = jnp.where(slot < n, 1.0 / MOST, 0.0)
            start = (jnp.zeros((2 * C, 2 * C), F), jnp.zeros((C, LANES), F))

            def block(j, sums):
                prod, bias_sum = backward_block(G.at[i % 2], slot, j, into(G.at[(i + 1) % 2], 1), True)
                return sums[0] + prod, sums[1] + bias_sum
            prod, bias_sum = lax.fori_loop(0, blocks, block, start, unroll=True)
            GB[slot] = -factor * (prod[:C, :C] + (prod[:C, C:] + prod[C:, :C]))
            column = jnp.sum(bias_sum, axis=1, keepdims=True)
            GB[MOST, pl.ds(slot, 1), :] = -factor * row_of(column, eye)
            return 0

        lax.fori_loop(0, MOST, layer, 0)
        for c in range(chunks):
            a_out[:, c * LANES : (c + 1) * LANES] = G[0, c + 1]
        GR[image] = GB[...]
        for o in range(1, images):
            grad_copy(o).start()

    def grad_copy(o):
        return copy(GB, GR.at[image], grad_s.at[o - 1], grad_r.at[o - 1], d, (image + o) % images)

    def turn(order, _):
        relay_at = jnp.where(chip < early, 0, jnp.where(chip < middle, 1, 2))
        start_at = jnp.where(jnp.logical_and(even, chip < early), 1, 0)
        full_at = jnp.where(jnp.logical_and(even, chip >= middle), 1, 2)

        @pl.when(jnp.logical_and(even, order == relay_at))
        def _():
            relay()

        @pl.when(order == start_at)
        def _():
            backward_start()

        @pl.when(order == full_at)
        def _():
            backward_full()
        return 0

    lax.fori_loop(0, 3, turn, 0)

    for o in range(1, images):
        grad_copy(o).wait_recv()
    for i in range(MOST + 1):
        total = GR[0, i]
        for b in range(1, images):
            total = total + GR[b, i]
        if i < MOST:
            gw_out[i] = total
        else:
            gb_out[...] = total[:MOST]

    @pl.when(odd)
    def _():
        def take(c, _):
            one_copy(c).wait_recv()
            s_out[:, at(c)] = S[c]
            return 0
        lax.fori_loop(0, chunks, take, 0)

    @pl.when(even)
    def _():
        for c in range(chunks):
            s_out[:, c * LANES : (c + 1) * LANES] = S[c]

    for o in range(1, images):
        grad_copy(o).wait_send()

    @pl.when(has_next)
    def _():
        for j in range(blocks):
            push_copy(j).wait_send()

    @pl.when(has_prev)
    def _():
        for j in range(blocks):
            lam_copy(j).wait_send()

    @pl.when(odd)
    def _():
        weight_copy.wait_send()
        bias_copy.wait_send()

    @pl.when(sends_tau)
    def _():
        for j in range(blocks):
            tau_copy(j).wait_send()

    @pl.when(even)
    def _():
        def sent(c, _):
            one_copy(c).wait_send()
            return 0
        lax.fori_loop(0, chunks, sent, 0)

    @pl.when(up2)
    def _():
        def sent(c, _):
            two_copy(c).wait_send()
            return 0
        lax.fori_loop(0, chunks, sent, 0)


def body(cpoint_guess, adjoint_guess, weights, biases, diffusion, section_len):
    pixels = cpoint_guess.shape[-1]
    images = lax.axis_size("batch")
    chunks = pixels // LANES
    NB = min(16, chunks)
    blocks = chunks // NB
    vmem = pl.BlockSpec(memory_space=pltpu.VMEM)
    image_shape = jax.ShapeDtypeStruct((C, pixels), F)
    dma = pltpu.SemaphoreType.DMA

    def stack(*lead):
        return pltpu.VMEM(lead + (C, LANES), F)

    outs = pl.pallas_call(
        kernel,
        out_shape=(
            image_shape, image_shape,
            jax.ShapeDtypeStruct((MOST, C, C), F), jax.ShapeDtypeStruct((MOST, C), F),
        ),
        in_specs=[vmem] * 5 + [pl.BlockSpec(memory_space=pltpu.SMEM)],
        out_specs=(vmem,) * 4,
        scratch_shapes=[
            stack(MOST + 1, chunks + 2), stack(MOST, chunks), stack(2, chunks + 2), stack(chunks + 2),
            stack(chunks), stack(chunks), stack(chunks + 1), stack(chunks), stack(chunks),
            stack(chunks + 1), stack(chunks),
            pltpu.VMEM((MOST, C, 3 * C), BF), pltpu.VMEM((MOST, C, 3 * C), BF), stack(MOST), stack(MOST),
            pltpu.VMEM((C, C), F), pltpu.VMEM((MOST, C), F),
            stack(C), stack(C), stack(C), stack(C), stack(4),
            pltpu.VMEM((MOST + 1, C, C), F), pltpu.VMEM((images, MOST + 1, C, C), F),
            dma((blocks,)), dma((blocks,)), dma((blocks,)), dma((blocks,)), dma((blocks,)), dma((blocks,)),
            dma((2,)), dma((2,)), dma((chunks,)), dma((chunks,)), dma((chunks,)),
            dma((images - 1,)), dma((images - 1,)),
        ],
        compiler_params=pltpu.CompilerParams(
            collective_id=0, has_side_effects=True, vmem_limit_bytes=56 << 20
        ),
        name="mgrit_cycle",
    )(
        cpoint_guess.reshape(C, pixels), adjoint_guess.reshape(C, pixels), weights, biases,
        diffusion.reshape(1, C), section_len,
    )
    states_out, adjoint_out, grad_weights, grad_biases = outs
    return states_out[None, None], adjoint_out[None, None], grad_weights, grad_biases


def solution(mesh):
    placed = (
        P("depth", "batch", None, None), P("depth", "batch", None, None), P("depth", None, None),
        P("depth", None), P(), P(),
    )
    return jax.shard_map(
        body, mesh=mesh, in_specs=placed,
        out_specs=(
            P("depth", "batch", None, None), P("depth", "batch", None, None), P("depth", None, None),
            P("depth", None),
        ),
        check_vma=False,
    )
```

```python
import jax
import jax.numpy as jnp
from jax import lax
from jax.experimental import pallas as pl
from jax.experimental.pallas import tpu as pltpu
from jax.sharding import PartitionSpec as P

MOST = 8
C = 32
LANES = 128
F = jnp.float32
BF = jnp.bfloat16
NT = (((1,), (1,)), ((), ()))


def split2(x):
    hi = x.astype(BF)
    return hi, (x - hi.astype(F)).astype(BF)


def dot3(packed, x):
    hi, lo = split2(x)
    return jnp.dot(packed, jnp.concatenate([hi, lo, hi], axis=0), preferred_element_type=F)


def pack3(matrix):
    hi, lo = split2(matrix)
    return jnp.concatenate([hi, hi, lo], axis=1)


def lane_masks():
    lane = lax.broadcasted_iota(jnp.int32, (C, LANES), 1)
    return lane < 64, lane % 64 == 0, lane % 64 == 63


def beside(x, masks):
    zero = jnp.zeros_like(x)
    return jnp.where(masks[1], zero, pltpu.roll(x, 1, 1)) + jnp.where(masks[2], zero, pltpu.roll(x, 127, 1))


def chunk_laps(chunks, count, masks):
    turned = [pltpu.roll(x, 64, 1) for x in chunks]
    laps = []
    for k in range(1, count + 1):
        above_below = turned[k] + jnp.where(masks[0], turned[k - 1], turned[k + 1])
        laps.append((above_below + beside(chunks[k], masks)) - 4.0 * chunks[k])
    return laps


def column_of(row, eye):
    return jnp.sum(jnp.where(eye, jnp.broadcast_to(row, (C, C)), 0.0), axis=1, keepdims=True)


def row_of(column, eye):
    return jnp.sum(jnp.where(eye, jnp.broadcast_to(column, (C, C)), 0.0), axis=0, keepdims=True)


def spread(matrix, out_ref):
    for k in range(C):
        out_ref[k] = jnp.broadcast_to(matrix[:, k : k + 1], (C, LANES))


def mix(spread_ref, x, first):
    sums = [first, None]
    for k in range(C):
        term = spread_ref[k] * jnp.broadcast_to(x[k : k + 1, :], (C, LANES))
        sums[k % 2] = term if sums[k % 2] is None else sums[k % 2] + term
    return sums[0] + sums[1]


def kernel(
    guess_ref, adj_ref, w_ref, b_ref, d_ref, n_ref,
    s_out, a_out, gw_out, gb_out,
    A, T, G, LR, PUSH, LSEND, S, S2, TAU, TAU_A,
    WC, WT, BB, FD, WP, BP, SPA, SPAT, SPB, SPBT, CB, GB, GR,
    push_s, push_r, lam_s, lam_r, tau_s, tau_r, par_s, par_r, one_s, two_s, st_r, grad_s, grad_r,
):
    sections, images = lax.axis_size("depth"), lax.axis_size("batch")
    d, image = lax.axis_index("depth"), lax.axis_index("batch")
    chunks = guess_ref.shape[1] // LANES
    NB = min(16, chunks)
    blocks = chunks // NB
    core, chip, chips = d % 2, d // 2, sections // 2
    has_prev, has_next = d > 0, d < sections - 1
    even = core == 0
    odd = core == 1
    early, middle = (3 * chips) // 16, (10 * chips) // 16
    masks = lane_masks()
    eye = lax.broadcasted_iota(jnp.int32, (C, C), 0) == lax.broadcasted_iota(jnp.int32, (C, C), 1)

    def at(c):
        return pl.ds(pl.multiple_of(c * LANES, LANES), LANES)

    def copy(src, dst, ssem, rsem, depth_to, image_to=None):
        return pltpu.make_async_remote_copy(
            src_ref=src, dst_ref=dst, send_sem=ssem, recv_sem=rsem,
            device_id=(depth_to, image if image_to is None else image_to),
            device_id_type=pl.DeviceIdType.MESH,
        )

    barrier = pltpu.get_barrier_semaphore()

    def greet(cond, depth_to, image_to):
        @pl.when(cond)
        def _():
            pl.semaphore_signal(barrier, inc=1, device_id=(depth_to, image_to), device_id_type=pl.DeviceIdType.MESH)

    up2, down2 = jnp.logical_and(odd, chip < chips - 1), jnp.logical_and(odd, chip > 0)
    greet(has_prev, d - 1, image)
    greet(has_next, d + 1, image)
    greet(up2, d + 2, image)
    greet(down2, d - 2, image)
    for o in range(1, images):
        pl.semaphore_signal(
            barrier, inc=1, device_id=(d, (image + o) % images), device_id_type=pl.DeviceIdType.MESH
        )
    partners = (
        has_prev.astype(jnp.int32) + has_next.astype(jnp.int32) + up2.astype(jnp.int32)
        + down2.astype(jnp.int32) + (images - 1)
    )

    n = n_ref[d]
    diff_col = column_of(d_ref[...], eye)
    diff = jnp.broadcast_to(diff_col, (C, LANES))

    def prepare(i, _):
        factor = jnp.where(i < n, 1.0 / MOST, 0.0)
        WC[i] = pack3(w_ref[i])
        WT[i] = pack3(w_ref[i].T * factor)
        BB[i] = jnp.broadcast_to(column_of(b_ref[pl.ds(i, 1), :], eye), (C, LANES))
        FD[i] = diff * factor
        return 0

    lax.fori_loop(0, MOST, prepare, 0)
    zero_chunk = jnp.zeros((C, LANES), F)
    for l in range(MOST + 1):
        A[l, 0] = zero_chunk
        A[l, chunks + 1] = zero_chunk
    for ref in (G.at[0], G.at[1], LR):
        ref[0] = zero_chunk
        ref[chunks + 1] = zero_chunk
    for c in range(chunks):
        G[0, c + 1] = guess_ref[:, c * LANES : (c + 1) * LANES]

    def forward_block(src, i, j, store, keep):
        u = [src[j * NB + k] for k in range(NB + 2)]
        laps = chunk_laps(u, NB, masks)
        bias = jnp.concatenate([BB[i]] * NB, axis=1)
        act = jnp.tanh(dot3(WC[i], jnp.concatenate(u[1:-1], axis=1)) + bias)
        mixed = dot3(WT[i], act)
        fd = FD[i]
        for k in range(NB):
            store(j * NB + k, u[k + 1] + fd * laps[k] - mixed[:, k * LANES : (k + 1) * LANES])
            if keep is not None:
                keep[j * NB + k] = act[:, k * LANES : (k + 1) * LANES]

    def into(ref, shift):
        def store(c, value):
            ref[c + shift] = value
        return store

    def forward_layer(src, i, store, keep=None, unroll=True):
        def block(j, _):
            forward_block(src, i, j, store, keep)
            return 0
        lax.fori_loop(0, blocks, block, 0, unroll=unroll)

    def first_pass(i, _):
        forward_layer(G.at[i % 2], i, into(G.at[(i + 1) % 2], 1))
        return 0

    lax.fori_loop(0, MOST - 1, first_pass, 0)
    pl.semaphore_wait(barrier, partners)

    def push_copy(j):
        return copy(
            PUSH.at[pl.ds(j * NB, NB)], A.at[0, pl.ds(1 + j * NB, NB)], push_s.at[j], push_r.at[j], d + 1
        )

    def push_block(j, _):
        forward_block(G.at[(MOST - 1) % 2], MOST - 1, j, into(PUSH, 0), None)

        @pl.when(has_next)
        def _():
            push_copy(j).start()
        return 0

    lax.fori_loop(0, blocks, push_block, 0)

    weight_copy = copy(w_ref.at[0], WP, par_s.at[0], par_r.at[0], d + 1)
    bias_copy = copy(b_ref, BP, par_s.at[1], par_r.at[1], d + 1)

    def first_copy(c):
        return copy(guess_ref.at[:, at(c)], S.at[c], one_s.at[c], st_r.at[c], d + 1)

    starts = jnp.logical_not(has_prev)

    @pl.when(even)
    def _():
        weight_copy.start()
        bias_copy.start()

    @pl.when(starts)
    def _():
        def send(c, _):
            first_copy(c).start()
            return 0
        lax.fori_loop(0, chunks, send, 0)

    @pl.when(odd)
    def _():
        coarse_b = n.astype(F) / MOST
        spread(w_ref[0], SPB)
        spread(w_ref[0].T * -coarse_b, SPBT)
        CB[2] = BB[0]
        CB[3] = diff * coarse_b
        weight_copy.wait_recv()
        bias_copy.wait_recv()
        coarse_a = n_ref[d - core].astype(F) / MOST
        spread(WP[...], SPA)
        spread(WP[...].T * -coarse_a, SPAT)
        CB[0] = jnp.broadcast_to(column_of(BP[0:1, :], eye), (C, LANES))
        CB[1] = diff * coarse_a

    @pl.when(has_prev)
    def _():
        for j in range(blocks):
            push_copy(j).wait_recv()

    @pl.when(jnp.logical_not(has_prev))
    def _():
        for c in range(chunks):
            A[0, c + 1] = guess_ref[:, c * LANES : (c + 1) * LANES]

    def second_pass(i, _):
        forward_layer(A.at[i], i, into(A.at[i + 1], 1), T.at[i])
        return 0

    lax.fori_loop(0, MOST, second_pass, 0)

    layers = n.astype(F)

    def tau_of(c):
        start = A[0, c + 1]
        return A[MOST, c + 1] - (start + layers * (A[1, c + 1] - start))

    def tau_copy(j):
        part = pl.ds(j * NB, NB) if j < blocks else pl.ds(chunks, 1)
        return copy(TAU.at[part], TAU_A.at[part], tau_s.at[j], tau_r.at[j], d + 1)

    @pl.when(even)
    def _():
        before = zero_chunk
        for c in range(chunks):
            here = tau_of(c)
            TAU[c] = jnp.where(masks[0], here, before)
            before = here
            if c % NB == NB - 1:
                tau_copy(c // NB).start()
        TAU[chunks] = jnp.where(masks[0], 0.0, before)
        tau_copy(blocks).start()

    @pl.when(odd)
    def _():
        for c in range(chunks):
            TAU[c] = tau_of(c)

    def one_copy(c):
        return copy(S.at[c], S.at[c], one_s.at[c], st_r.at[c], d - 1)

    def two_copy(c):
        return copy(S2.at[c], S.at[c], two_s.at[c], st_r.at[c], d + 2)

    def relay(both):
        for j in range(blocks + 1):
            tau_copy(j).wait_recv()
        bias_a, fd_a, bias_b, fd_b = CB[0], CB[1], CB[2], CB[3]
        lower = masks[0]

        def step(c, carry, first=False, last=False):
            prev, one_prev = carry
            if last:
                now = zero_chunk
            else:
                two_copy(c).wait_recv()
                one_copy(c).start()
                now = S[c]
            mid = jnp.where(lower, now, prev)
            lap = (pltpu.roll(prev + now, 64, 1) + beside(mid, masks)) - 4.0 * mid
            act = jnp.tanh(mix(SPA, mid, bias_a))
            one = mix(SPAT, act, mid + fd_a * lap + TAU_A[c])
            if first:
                one = jnp.where(lower, one, 0.0)
            if last:
                one = jnp.where(lower, 0.0, one)
            if not first:
                mid_one = jnp.where(lower, one_prev, one)
                if both:
                    lap_b = (pltpu.roll(one_prev + one, 64, 1) + beside(mid_one, masks)) - 4.0 * mid_one
                    act_b = jnp.tanh(mix(SPB, mid_one, bias_b))
                    S2[c - 1] = mix(SPBT, act_b, mid_one + fd_b * lap_b + TAU[c - 1])
                    two_copy(c - 1).start()
                s_out[:, at(c - 1)] = mid_one
            return now, one

        carry = step(0, (zero_chunk,) * 2, first=True)
        carry = lax.fori_loop(1, chunks, step, carry)
        step(chunks, carry, last=True)

    def backward_block(src, i, j, store, with_grads):
        g = [src[j * NB + k] for k in range(NB + 2)]
        laps = chunk_laps(g, NB, masks)
        act = jnp.concatenate([T[i, j * NB + k] for k in range(NB)], axis=1)
        g_hi, g_lo = split2(jnp.concatenate(g[1:-1], axis=1))
        pulled = jnp.dot(WC[i], jnp.concatenate([g_hi, g_lo, g_hi], axis=0), preferred_element_type=F)
        pre = (1.0 - act * act) * pulled
        p_hi, p_lo = split2(pre)
        back = jnp.dot(WT[i], jnp.concatenate([p_hi, p_lo, p_hi], axis=0), preferred_element_type=F)
        fd = FD[i]
        for k in range(NB):
            store(j * NB + k, g[k + 1] + fd * laps[k] - back[:, k * LANES : (k + 1) * LANES])
        if not with_grads:
            return None
        t_hi, t_lo = split2(act)
        u_hi, u_lo = split2(jnp.concatenate([A[i, j * NB + k + 1] for k in range(NB)], axis=1))
        left = jnp.concatenate(
            [jnp.concatenate([t_hi, p_hi], axis=1), jnp.concatenate([t_lo, p_lo], axis=1)], axis=0
        )
        right = jnp.concatenate(
            [jnp.concatenate([g_hi, u_hi], axis=1), jnp.concatenate([g_lo, u_lo], axis=1)], axis=0
        )
        prod = lax.dot_general(left, right, NT, preferred_element_type=F)
        bias_sum = pre[:, :LANES]
        for k in range(1, NB):
            bias_sum = bias_sum + pre[:, k * LANES : (k + 1) * LANES]
        return prod, bias_sum

    def lam_copy(j):
        return copy(LSEND.at[pl.ds(j * NB, NB)], LR.at[pl.ds(1 + j * NB, NB)], lam_s.at[j], lam_r.at[j], d - 1)

    def backward_start():
        for c in range(chunks):
            G[0, c + 1] = adj_ref[:, c * LANES : (c + 1) * LANES]

        def layer(i, _):
            def block(j, _):
                backward_block(G.at[i % 2], MOST - 1 - i, j, into(G.at[(i + 1) % 2], 1), False)
                return 0
            lax.fori_loop(0, blocks, block, 0, unroll=True)
            return 0

        lax.fori_loop(0, MOST - 1, layer, 0)

        def block(j, _):
            backward_block(G.at[(MOST - 1) % 2], 0, j, into(LSEND, 0), False)

            @pl.when(has_prev)
            def _():
                lam_copy(j).start()
            return 0

        lax.fori_loop(0, blocks, block, 0)

    def backward_full():
        @pl.when(has_next)
        def _():
            for j in range(blocks):
                lam_copy(j).wait_recv()

        @pl.when(jnp.logical_not(has_next))
        def _():
            for c in range(chunks):
                LR[c + 1] = adj_ref[:, c * LANES : (c + 1) * LANES]

        for c in range(chunks):
            G[0, c + 1] = LR[c + 1]
        GB[MOST] = jnp.zeros((C, C), F)

        def layer(i, _):
            slot = MOST - 1 - i
            factor = jnp.where(slot < n, 1.0 / MOST, 0.0)
            start = (jnp.zeros((2 * C, 2 * C), F), jnp.zeros((C, LANES), F))

            def block(j, sums):
                prod, bias_sum = backward_block(G.at[i % 2], slot, j, into(G.at[(i + 1) % 2], 1), True)
                return sums[0] + prod, sums[1] + bias_sum
            prod, bias_sum = lax.fori_loop(0, blocks, block, start, unroll=True)
            GB[slot] = -factor * (prod[:C, :C] + (prod[:C, C:] + prod[C:, :C]))
            column = jnp.sum(bias_sum, axis=1, keepdims=True)
            GB[MOST, pl.ds(slot, 1), :] = -factor * row_of(column, eye)
            return 0

        lax.fori_loop(0, MOST, layer, 0)
        for c in range(chunks):
            a_out[:, c * LANES : (c + 1) * LANES] = G[0, c + 1]
        GR[image] = GB[...]
        for o in range(1, images):
            grad_copy(o).start()

    def grad_copy(o):
        return copy(GB, GR.at[image], grad_s.at[o - 1], grad_r.at[o - 1], d, (image + o) % images)

    def turn(order, _):
        relay_at = jnp.where(chip < early, 0, jnp.where(chip < middle, 1, 2))
        start_at = jnp.where(jnp.logical_and(odd, chip < early), 1, 0)
        full_at = jnp.where(jnp.logical_and(odd, chip >= middle), 1, 2)
        here = jnp.logical_and(odd, order == relay_at)

        @pl.when(jnp.logical_and(here, chip < chips - 1))
        def _():
            relay(True)

        @pl.when(jnp.logical_and(here, chip == chips - 1))
        def _():
            relay(False)

        @pl.when(order == start_at)
        def _():
            backward_start()

        @pl.when(order == full_at)
        def _():
            backward_full()
        return 0

    lax.fori_loop(0, 3, turn, 0)

    for o in range(1, images):
        grad_copy(o).wait_recv()
    for i in range(MOST + 1):
        total = GR[0, i]
        for b in range(1, images):
            total = total + GR[b, i]
        if i < MOST:
            gw_out[i] = total
        else:
            gb_out[...] = total[:MOST]

    @pl.when(even)
    def _():
        def take(c, _):
            one_copy(c).wait_recv()
            s_out[:, at(c)] = S[c]
            return 0
        lax.fori_loop(0, chunks, take, 0)

    for o in range(1, images):
        grad_copy(o).wait_send()

    @pl.when(has_next)
    def _():
        for j in range(blocks):
            push_copy(j).wait_send()

    @pl.when(has_prev)
    def _():
        for j in range(blocks):
            lam_copy(j).wait_send()

    @pl.when(even)
    def _():
        weight_copy.wait_send()
        bias_copy.wait_send()
        for j in range(blocks + 1):
            tau_copy(j).wait_send()

    @pl.when(starts)
    def _():
        def sent(c, _):
            first_copy(c).wait_send()
            return 0
        lax.fori_loop(0, chunks, sent, 0)

    @pl.when(odd)
    def _():
        def sent(c, _):
            one_copy(c).wait_send()
            return 0
        lax.fori_loop(0, chunks, sent, 0)

    @pl.when(up2)
    def _():
        def sent(c, _):
            two_copy(c).wait_send()
            return 0
        lax.fori_loop(0, chunks, sent, 0)


def body(cpoint_guess, adjoint_guess, weights, biases, diffusion, section_len):
    pixels = cpoint_guess.shape[-1]
    images = lax.axis_size("batch")
    chunks = pixels // LANES
    NB = min(16, chunks)
    blocks = chunks // NB
    vmem = pl.BlockSpec(memory_space=pltpu.VMEM)
    image_shape = jax.ShapeDtypeStruct((C, pixels), F)
    dma = pltpu.SemaphoreType.DMA

    def stack(*lead):
        return pltpu.VMEM(lead + (C, LANES), F)

    outs = pl.pallas_call(
        kernel,
        out_shape=(
            image_shape, image_shape,
            jax.ShapeDtypeStruct((MOST, C, C), F), jax.ShapeDtypeStruct((MOST, C), F),
        ),
        in_specs=[vmem] * 5 + [pl.BlockSpec(memory_space=pltpu.SMEM)],
        out_specs=(vmem,) * 4,
        scratch_shapes=[
            stack(MOST + 1, chunks + 2), stack(MOST, chunks), stack(2, chunks + 2), stack(chunks + 2),
            stack(chunks), stack(chunks), stack(chunks), stack(chunks), stack(chunks + 1), stack(chunks + 1),
            pltpu.VMEM((MOST, C, 3 * C), BF), pltpu.VMEM((MOST, C, 3 * C), BF), stack(MOST), stack(MOST),
            pltpu.VMEM((C, C), F), pltpu.VMEM((MOST, C), F),
            stack(C), stack(C), stack(C), stack(C), stack(4),
            pltpu.VMEM((MOST + 1, C, C), F), pltpu.VMEM((images, MOST + 1, C, C), F),
            dma((blocks,)), dma((blocks,)), dma((blocks,)), dma((blocks,)), dma((blocks + 1,)), dma((blocks + 1,)),
            dma((2,)), dma((2,)), dma((chunks,)), dma((chunks,)), dma((chunks,)),
            dma((images - 1,)), dma((images - 1,)),
        ],
        compiler_params=pltpu.CompilerParams(
            collective_id=0, has_side_effects=True, vmem_limit_bytes=56 << 20
        ),
        name="mgrit_cycle",
    )(
        cpoint_guess.reshape(C, pixels), adjoint_guess.reshape(C, pixels), weights, biases,
        diffusion.reshape(1, C), section_len,
    )
    states_out, adjoint_out, grad_weights, grad_biases = outs
    return states_out[None, None], adjoint_out[None, None], grad_weights, grad_biases


def solution(mesh):
    placed = (
        P("depth", "batch", None, None), P("depth", "batch", None, None), P("depth", None, None),
        P("depth", None), P(), P(),
    )
    return jax.shard_map(
        body, mesh=mesh, in_specs=placed,
        out_specs=(
            P("depth", "batch", None, None), P("depth", "batch", None, None), P("depth", None, None),
            P("depth", None),
        ),
        check_vma=False,
    )
```

```python
import jax
import jax.numpy as jnp
from jax import lax
from jax.experimental import pallas as pl
from jax.experimental.pallas import tpu as pltpu
from jax.sharding import PartitionSpec as P

MOST = 8
C = 32
LANES = 128
F = jnp.float32
BF = jnp.bfloat16
NT = (((1,), (1,)), ((), ()))


def split2(x):
    hi = x.astype(BF)
    return hi, (x - hi.astype(F)).astype(BF)


def dot3(packed, x):
    hi, lo = split2(x)
    return jnp.dot(packed, jnp.concatenate([hi, lo, hi], axis=0), preferred_element_type=F)


def pack3(matrix):
    hi, lo = split2(matrix)
    return jnp.concatenate([hi, hi, lo], axis=1)


def lane_masks():
    lane = lax.broadcasted_iota(jnp.int32, (C, LANES), 1)
    return lane < 64, lane % 64 == 0, lane % 64 == 63


def beside(x, masks):
    zero = jnp.zeros_like(x)
    return jnp.where(masks[1], zero, pltpu.roll(x, 1, 1)) + jnp.where(masks[2], zero, pltpu.roll(x, 127, 1))


def chunk_laps(chunks, count, masks):
    turned = [pltpu.roll(x, 64, 1) for x in chunks]
    laps = []
    for k in range(1, count + 1):
        above_below = turned[k] + jnp.where(masks[0], turned[k - 1], turned[k + 1])
        laps.append((above_below + beside(chunks[k], masks)) - 4.0 * chunks[k])
    return laps


def column_of(row, eye):
    return jnp.sum(jnp.where(eye, jnp.broadcast_to(row, (C, C)), 0.0), axis=1, keepdims=True)


def row_of(column, eye):
    return jnp.sum(jnp.where(eye, jnp.broadcast_to(column, (C, C)), 0.0), axis=0, keepdims=True)


def spread(matrix, out_ref):
    for k in range(C):
        out_ref[k] = jnp.broadcast_to(matrix[:, k : k + 1], (C, LANES))


def mix(spread_ref, x, first):
    sums = [first, None]
    for k in range(C):
        term = spread_ref[k] * jnp.broadcast_to(x[k : k + 1, :], (C, LANES))
        sums[k % 2] = term if sums[k % 2] is None else sums[k % 2] + term
    return sums[0] + sums[1]


def kernel(
    guess_ref, adj_ref, w_ref, b_ref, d_ref, n_ref,
    s_out, a_out, gw_out, gb_out,
    A, T, G, LR, PUSH, LSEND, S, S2, TAU, TAU_A,
    WC, WT, BB, FD, WP, BP, SPA, SPAT, SPB, SPBT, CB, GB, GR,
    push_s, push_r, lam_s, lam_r, tau_s, tau_r, par_s, par_r, one_s, two_s, st_r, grad_s, grad_r,
):
    sections, images = lax.axis_size("depth"), lax.axis_size("batch")
    d, image = lax.axis_index("depth"), lax.axis_index("batch")
    chunks = guess_ref.shape[1] // LANES
    NB = min(16, chunks)
    blocks = chunks // NB
    core, chip, chips = d % 2, d // 2, sections // 2
    has_prev, has_next = d > 0, d < sections - 1
    even = core == 0
    odd = core == 1
    early, middle = (3 * chips) // 16, chips // 2
    masks = lane_masks()
    eye = lax.broadcasted_iota(jnp.int32, (C, C), 0) == lax.broadcasted_iota(jnp.int32, (C, C), 1)

    def at(c):
        return pl.ds(pl.multiple_of(c * LANES, LANES), LANES)

    def copy(src, dst, ssem, rsem, depth_to, image_to=None):
        return pltpu.make_async_remote_copy(
            src_ref=src, dst_ref=dst, send_sem=ssem, recv_sem=rsem,
            device_id=(depth_to, image if image_to is None else image_to),
            device_id_type=pl.DeviceIdType.MESH,
        )

    barrier = pltpu.get_barrier_semaphore()

    def greet(cond, depth_to, image_to):
        @pl.when(cond)
        def _():
            pl.semaphore_signal(barrier, inc=1, device_id=(depth_to, image_to), device_id_type=pl.DeviceIdType.MESH)

    up2, down2 = jnp.logical_and(odd, chip < chips - 1), jnp.logical_and(odd, chip > 0)
    greet(has_prev, d - 1, image)
    greet(has_next, d + 1, image)
    greet(up2, d + 2, image)
    greet(down2, d - 2, image)
    for o in range(1, images):
        pl.semaphore_signal(
            barrier, inc=1, device_id=(d, (image + o) % images), device_id_type=pl.DeviceIdType.MESH
        )
    partners = (
        has_prev.astype(jnp.int32) + has_next.astype(jnp.int32) + up2.astype(jnp.int32)
        + down2.astype(jnp.int32) + (images - 1)
    )

    n = n_ref[d]
    diff_col = column_of(d_ref[...], eye)
    diff = jnp.broadcast_to(diff_col, (C, LANES))

    def prepare(i, _):
        factor = jnp.where(i < n, 1.0 / MOST, 0.0)
        WC[i] = pack3(w_ref[i])
        WT[i] = pack3(w_ref[i].T * factor)
        BB[i] = jnp.broadcast_to(column_of(b_ref[pl.ds(i, 1), :], eye), (C, LANES))
        FD[i] = diff * factor
        return 0

    lax.fori_loop(0, MOST, prepare, 0)
    zero_chunk = jnp.zeros((C, LANES), F)
    for l in range(MOST + 1):
        A[l, 0] = zero_chunk
        A[l, chunks + 1] = zero_chunk
    for ref in (G.at[0], G.at[1], LR):
        ref[0] = zero_chunk
        ref[chunks + 1] = zero_chunk
    for c in range(chunks):
        G[0, c + 1] = guess_ref[:, c * LANES : (c + 1) * LANES]

    def forward_block(src, i, j, store, keep):
        u = [src[j * NB + k] for k in range(NB + 2)]
        laps = chunk_laps(u, NB, masks)
        bias = jnp.concatenate([BB[i]] * NB, axis=1)
        act = jnp.tanh(dot3(WC[i], jnp.concatenate(u[1:-1], axis=1)) + bias)
        mixed = dot3(WT[i], act)
        fd = FD[i]
        for k in range(NB):
            store(j * NB + k, u[k + 1] + fd * laps[k] - mixed[:, k * LANES : (k + 1) * LANES])
            if keep is not None:
                keep[j * NB + k] = act[:, k * LANES : (k + 1) * LANES]

    def into(ref, shift):
        def store(c, value):
            ref[c + shift] = value
        return store

    def forward_layer(src, i, store, keep=None, unroll=True):
        def block(j, _):
            forward_block(src, i, j, store, keep)
            return 0
        lax.fori_loop(0, blocks, block, 0, unroll=unroll)

    def first_pass(i, _):
        forward_layer(G.at[i % 2], i, into(G.at[(i + 1) % 2], 1))
        return 0

    lax.fori_loop(0, MOST - 1, first_pass, 0)
    pl.semaphore_wait(barrier, partners)

    def push_copy(j):
        return copy(
            PUSH.at[pl.ds(j * NB, NB)], A.at[0, pl.ds(1 + j * NB, NB)], push_s.at[j], push_r.at[j], d + 1
        )

    def push_block(j, _):
        forward_block(G.at[(MOST - 1) % 2], MOST - 1, j, into(PUSH, 0), None)

        @pl.when(has_next)
        def _():
            push_copy(j).start()
        return 0

    lax.fori_loop(0, blocks, push_block, 0)

    weight_copy = copy(w_ref.at[0], WP, par_s.at[0], par_r.at[0], d + 1)
    bias_copy = copy(b_ref, BP, par_s.at[1], par_r.at[1], d + 1)

    def first_copy(c):
        return copy(guess_ref.at[:, at(c)], S.at[c], one_s.at[c], st_r.at[c], d + 1)

    starts = jnp.logical_not(has_prev)

    @pl.when(even)
    def _():
        weight_copy.start()
        bias_copy.start()

    @pl.when(starts)
    def _():
        def send(c, _):
            first_copy(c).start()
            return 0
        lax.fori_loop(0, chunks, send, 0)

    @pl.when(odd)
    def _():
        coarse_b = n.astype(F) / MOST
        spread(w_ref[0], SPB)
        spread(w_ref[0].T * -coarse_b, SPBT)
        CB[2] = BB[0]
        CB[3] = diff * coarse_b
        weight_copy.wait_recv()
        bias_copy.wait_recv()
        coarse_a = n_ref[d - core].astype(F) / MOST
        spread(WP[...], SPA)
        spread(WP[...].T * -coarse_a, SPAT)
        CB[0] = jnp.broadcast_to(column_of(BP[0:1, :], eye), (C, LANES))
        CB[1] = diff * coarse_a

    @pl.when(has_prev)
    def _():
        for j in range(blocks):
            push_copy(j).wait_recv()

    @pl.when(jnp.logical_not(has_prev))
    def _():
        for c in range(chunks):
            A[0, c + 1] = guess_ref[:, c * LANES : (c + 1) * LANES]

    def second_pass(i, _):
        forward_layer(A.at[i], i, into(A.at[i + 1], 1), T.at[i])
        return 0

    lax.fori_loop(0, MOST, second_pass, 0)

    layers = n.astype(F)

    def tau_of(c):
        start = A[0, c + 1]
        return A[MOST, c + 1] - (start + layers * (A[1, c + 1] - start))

    def tau_copy(j):
        part = pl.ds(j * NB, NB) if j < blocks else pl.ds(chunks, 1)
        return copy(TAU.at[part], TAU_A.at[part], tau_s.at[j], tau_r.at[j], d + 1)

    @pl.when(even)
    def _():
        before = zero_chunk
        for c in range(chunks):
            here = tau_of(c)
            TAU[c] = jnp.where(masks[0], here, before)
            before = here
            if c % NB == NB - 1:
                tau_copy(c // NB).start()
        TAU[chunks] = jnp.where(masks[0], 0.0, before)
        tau_copy(blocks).start()

    @pl.when(odd)
    def _():
        for c in range(chunks):
            TAU[c] = tau_of(c)

    def one_copy(c):
        return copy(S.at[c], S.at[c], one_s.at[c], st_r.at[c], d - 1)

    def two_copy(c):
        return copy(S2.at[c], S.at[c], two_s.at[c], st_r.at[c], d + 2)

    def relay(both):
        for j in range(blocks + 1):
            tau_copy(j).wait_recv()
        bias_a, fd_a, bias_b, fd_b = CB[0], CB[1], CB[2], CB[3]
        lower = masks[0]

        def step(c, carry, first=False, last=False):
            prev, one_prev = carry
            if last:
                now = zero_chunk
            else:
                two_copy(c).wait_recv()
                one_copy(c).start()
                now = S[c]
            mid = jnp.where(lower, now, prev)
            lap = (pltpu.roll(prev + now, 64, 1) + beside(mid, masks)) - 4.0 * mid
            act = jnp.tanh(mix(SPA, mid, bias_a))
            one = mix(SPAT, act, mid + fd_a * lap + TAU_A[c])
            if first:
                one = jnp.where(lower, one, 0.0)
            if last:
                one = jnp.where(lower, 0.0, one)
            if not first:
                mid_one = jnp.where(lower, one_prev, one)
                if both:
                    lap_b = (pltpu.roll(one_prev + one, 64, 1) + beside(mid_one, masks)) - 4.0 * mid_one
                    act_b = jnp.tanh(mix(SPB, mid_one, bias_b))
                    S2[c - 1] = mix(SPBT, act_b, mid_one + fd_b * lap_b + TAU[c - 1])
                    two_copy(c - 1).start()
                s_out[:, at(c - 1)] = mid_one
            return now, one

        carry = step(0, (zero_chunk,) * 2, first=True)
        carry = lax.fori_loop(1, chunks, step, carry)
        step(chunks, carry, last=True)

    def backward_block(src, i, j, store, with_grads):
        g = [src[j * NB + k] for k in range(NB + 2)]
        laps = chunk_laps(g, NB, masks)
        act = jnp.concatenate([T[i, j * NB + k] for k in range(NB)], axis=1)
        g_hi, g_lo = split2(jnp.concatenate(g[1:-1], axis=1))
        pulled = jnp.dot(WC[i], jnp.concatenate([g_hi, g_lo, g_hi], axis=0), preferred_element_type=F)
        pre = (1.0 - act * act) * pulled
        p_hi, p_lo = split2(pre)
        back = jnp.dot(WT[i], jnp.concatenate([p_hi, p_lo, p_hi], axis=0), preferred_element_type=F)
        fd = FD[i]
        for k in range(NB):
            store(j * NB + k, g[k + 1] + fd * laps[k] - back[:, k * LANES : (k + 1) * LANES])
        if not with_grads:
            return None
        t_hi, t_lo = split2(act)
        u_hi, u_lo = split2(jnp.concatenate([A[i, j * NB + k + 1] for k in range(NB)], axis=1))
        left = jnp.concatenate(
            [jnp.concatenate([t_hi, p_hi], axis=1), jnp.concatenate([t_lo, p_lo], axis=1)], axis=0
        )
        right = jnp.concatenate(
            [jnp.concatenate([g_hi, u_hi], axis=1), jnp.concatenate([g_lo, u_lo], axis=1)], axis=0
        )
        prod = lax.dot_general(left, right, NT, preferred_element_type=F)
        bias_sum = pre[:, :LANES]
        for k in range(1, NB):
            bias_sum = bias_sum + pre[:, k * LANES : (k + 1) * LANES]
        return prod, bias_sum

    def lam_copy(j):
        return copy(LSEND.at[pl.ds(j * NB, NB)], LR.at[pl.ds(1 + j * NB, NB)], lam_s.at[j], lam_r.at[j], d - 1)

    def backward_start():
        for c in range(chunks):
            G[0, c + 1] = adj_ref[:, c * LANES : (c + 1) * LANES]

        def layer(i, _):
            def block(j, _):
                backward_block(G.at[i % 2], MOST - 1 - i, j, into(G.at[(i + 1) % 2], 1), False)
                return 0
            lax.fori_loop(0, blocks, block, 0, unroll=True)
            return 0

        lax.fori_loop(0, MOST - 1, layer, 0)

        def block(j, _):
            backward_block(G.at[(MOST - 1) % 2], 0, j, into(LSEND, 0), False)

            @pl.when(has_prev)
            def _():
                lam_copy(j).start()
            return 0

        lax.fori_loop(0, blocks, block, 0)

    def backward_full():
        @pl.when(has_next)
        def _():
            for j in range(blocks):
                lam_copy(j).wait_recv()

        @pl.when(jnp.logical_not(has_next))
        def _():
            for c in range(chunks):
                LR[c + 1] = adj_ref[:, c * LANES : (c + 1) * LANES]

        for c in range(chunks):
            G[0, c + 1] = LR[c + 1]
        GB[MOST] = jnp.zeros((C, C), F)

        def layer(i, _):
            slot = MOST - 1 - i
            factor = jnp.where(slot < n, 1.0 / MOST, 0.0)
            start = (jnp.zeros((2 * C, 2 * C), F), jnp.zeros((C, LANES), F))

            def block(j, sums):
                prod, bias_sum = backward_block(G.at[i % 2], slot, j, into(G.at[(i + 1) % 2], 1), True)
                return sums[0] + prod, sums[1] + bias_sum
            prod, bias_sum = lax.fori_loop(0, blocks, block, start, unroll=True)
            GB[slot] = -factor * (prod[:C, :C] + (prod[:C, C:] + prod[C:, :C]))
            column = jnp.sum(bias_sum, axis=1, keepdims=True)
            GB[MOST, pl.ds(slot, 1), :] = -factor * row_of(column, eye)
            return 0

        lax.fori_loop(0, MOST, layer, 0)
        for c in range(chunks):
            a_out[:, c * LANES : (c + 1) * LANES] = G[0, c + 1]
        GR[image] = GB[...]
        for o in range(1, images):
            grad_copy(o).start()

    def grad_copy(o):
        return copy(GB, GR.at[image], grad_s.at[o - 1], grad_r.at[o - 1], d, (image + o) % images)

    def turn(order, _):
        relay_at = jnp.where(chip < early, 0, jnp.where(chip < middle, 1, 2))
        start_at = jnp.where(jnp.logical_and(odd, chip < early), 1, 0)
        full_at = jnp.where(jnp.logical_and(odd, chip >= middle), 1, 2)
        here = jnp.logical_and(odd, order == relay_at)

        @pl.when(jnp.logical_and(here, chip < chips - 1))
        def _():
            relay(True)

        @pl.when(jnp.logical_and(here, chip == chips - 1))
        def _():
            relay(False)

        @pl.when(order == start_at)
        def _():
            backward_start()

        @pl.when(order == full_at)
        def _():
            backward_full()
        return 0

    lax.fori_loop(0, 3, turn, 0)

    for o in range(1, images):
        grad_copy(o).wait_recv()
    for i in range(MOST + 1):
        total = GR[0, i]
        for b in range(1, images):
            total = total + GR[b, i]
        if i < MOST:
            gw_out[i] = total
        else:
            gb_out[...] = total[:MOST]

    @pl.when(even)
    def _():
        def take(c, _):
            one_copy(c).wait_recv()
            s_out[:, at(c)] = S[c]
            return 0
        lax.fori_loop(0, chunks, take, 0)

    for o in range(1, images):
        grad_copy(o).wait_send()

    @pl.when(has_next)
    def _():
        for j in range(blocks):
            push_copy(j).wait_send()

    @pl.when(has_prev)
    def _():
        for j in range(blocks):
            lam_copy(j).wait_send()

    @pl.when(even)
    def _():
        weight_copy.wait_send()
        bias_copy.wait_send()
        for j in range(blocks + 1):
            tau_copy(j).wait_send()

    @pl.when(starts)
    def _():
        def sent(c, _):
            first_copy(c).wait_send()
            return 0
        lax.fori_loop(0, chunks, sent, 0)

    @pl.when(odd)
    def _():
        def sent(c, _):
            one_copy(c).wait_send()
            return 0
        lax.fori_loop(0, chunks, sent, 0)

    @pl.when(up2)
    def _():
        def sent(c, _):
            two_copy(c).wait_send()
            return 0
        lax.fori_loop(0, chunks, sent, 0)


def write_out(*refs):
    sems = refs[8]
    copies = [pltpu.make_async_copy(refs[i], refs[i + 4], sems.at[i]) for i in range(4)]
    for one in copies:
        one.start()
    for one in copies:
        one.wait()


def body(cpoint_guess, adjoint_guess, weights, biases, diffusion, section_len):
    pixels = cpoint_guess.shape[-1]
    images = lax.axis_size("batch")
    chunks = pixels // LANES
    NB = min(16, chunks)
    blocks = chunks // NB
    vmem = pl.BlockSpec(memory_space=pltpu.VMEM)
    image_shape = jax.ShapeDtypeStruct((C, pixels), F)
    dma = pltpu.SemaphoreType.DMA

    def stack(*lead):
        return pltpu.VMEM(lead + (C, LANES), F)

    outs = pl.pallas_call(
        kernel,
        out_shape=(
            image_shape, image_shape,
            jax.ShapeDtypeStruct((MOST, C, C), F), jax.ShapeDtypeStruct((MOST, C), F),
        ),
        in_specs=[vmem] * 5 + [pl.BlockSpec(memory_space=pltpu.SMEM)],
        out_specs=(vmem,) * 4,
        scratch_shapes=[
            stack(MOST + 1, chunks + 2), stack(MOST, chunks), stack(2, chunks + 2), stack(chunks + 2),
            stack(chunks), stack(chunks), stack(chunks), stack(chunks), stack(chunks + 1), stack(chunks + 1),
            pltpu.VMEM((MOST, C, 3 * C), BF), pltpu.VMEM((MOST, C, 3 * C), BF), stack(MOST), stack(MOST),
            pltpu.VMEM((C, C), F), pltpu.VMEM((MOST, C), F),
            stack(C), stack(C), stack(C), stack(C), stack(4),
            pltpu.VMEM((MOST + 1, C, C), F), pltpu.VMEM((images, MOST + 1, C, C), F),
            dma((blocks,)), dma((blocks,)), dma((blocks,)), dma((blocks,)), dma((blocks + 1,)), dma((blocks + 1,)),
            dma((2,)), dma((2,)), dma((chunks,)), dma((chunks,)), dma((chunks,)),
            dma((images - 1,)), dma((images - 1,)),
        ],
        compiler_params=pltpu.CompilerParams(
            collective_id=0, has_side_effects=True, vmem_limit_bytes=24 << 20
        ),
        name="mgrit_cycle",
    )(
        cpoint_guess.reshape(C, pixels), adjoint_guess.reshape(C, pixels), weights, biases,
        diffusion.reshape(1, C), section_len,
    )
    states_out, adjoint_out, grad_weights, grad_biases = pl.pallas_call(
        write_out,
        out_shape=tuple(jax.ShapeDtypeStruct(o.shape, o.dtype) for o in outs),
        in_specs=[vmem] * 4,
        out_specs=(pl.BlockSpec(memory_space=pltpu.HBM),) * 4,
        scratch_shapes=[dma((4,))],
        compiler_params=pltpu.CompilerParams(vmem_limit_bytes=8 << 20),
        name="write_out",
    )(*outs)
    return states_out[None, None], adjoint_out[None, None], grad_weights, grad_biases


def solution(mesh):
    placed = (
        P("depth", "batch", None, None), P("depth", "batch", None, None), P("depth", None, None),
        P("depth", None), P(), P(),
    )
    return jax.shard_map(
        body, mesh=mesh, in_specs=placed,
        out_specs=(
            P("depth", "batch", None, None), P("depth", "batch", None, None), P("depth", None, None),
            P("depth", None),
        ),
        check_vma=False,
    )
```

```python
import jax
import jax.numpy as jnp
from jax import lax
from jax.experimental import pallas as pl
from jax.experimental.pallas import tpu as pltpu
from jax.sharding import PartitionSpec as P

MOST = 8
C = 32
LANES = 128
F = jnp.float32
BF = jnp.bfloat16
NT = (((1,), (1,)), ((), ()))


def split2(x):
    hi = x.astype(BF)
    return hi, (x - hi.astype(F)).astype(BF)


def dot3(packed, x):
    hi, lo = split2(x)
    return jnp.dot(packed, jnp.concatenate([hi, lo, hi], axis=0), preferred_element_type=F)


def pack3(matrix):
    hi, lo = split2(matrix)
    return jnp.concatenate([hi, hi, lo], axis=1)


def lane_masks():
    lane = lax.broadcasted_iota(jnp.int32, (C, LANES), 1)
    return lane < 64, lane % 64 == 0, lane % 64 == 63


def beside(x, masks):
    zero = jnp.zeros_like(x)
    return jnp.where(masks[1], zero, pltpu.roll(x, 1, 1)) + jnp.where(masks[2], zero, pltpu.roll(x, 127, 1))


def chunk_laps(chunks, count, masks):
    turned = [pltpu.roll(x, 64, 1) for x in chunks]
    laps = []
    for k in range(1, count + 1):
        above_below = turned[k] + jnp.where(masks[0], turned[k - 1], turned[k + 1])
        laps.append((above_below + beside(chunks[k], masks)) - 4.0 * chunks[k])
    return laps


def column_of(row, eye):
    return jnp.sum(jnp.where(eye, jnp.broadcast_to(row, (C, C)), 0.0), axis=1, keepdims=True)


def row_of(column, eye):
    return jnp.sum(jnp.where(eye, jnp.broadcast_to(column, (C, C)), 0.0), axis=0, keepdims=True)


def spread(matrix, out_ref):
    for k in range(C):
        out_ref[k] = jnp.broadcast_to(matrix[:, k : k + 1], (C, LANES))


def mix(spread_ref, x, first):
    sums = [first, None]
    for k in range(C):
        term = spread_ref[k] * jnp.broadcast_to(x[k : k + 1, :], (C, LANES))
        sums[k % 2] = term if sums[k % 2] is None else sums[k % 2] + term
    return sums[0] + sums[1]


def kernel(
    guess_ref, adj_ref, w_hbm, b_hbm, d_hbm, n_hbm,
    s_out, a_out, gw_out, gb_out,
    A, T, G, LR, PUSH, LSEND, S, S2, TAU, TAU_A,
    WC, WT, BB, FD, WP, BP, SPA, SPAT, SPB, SPBT, CB, GB, GR,
    push_s, push_r, lam_s, lam_r, tau_s, tau_r, par_s, par_r, one_s, two_s, st_r, grad_s, grad_r,
    w_ref, b_ref, d_ref, n_ref, in_s, guess_s, adj_s, spare_s,
):
    sections, images = lax.axis_size("depth"), lax.axis_size("batch")
    d, image = lax.axis_index("depth"), lax.axis_index("batch")
    chunks = guess_ref.shape[1] // LANES
    NB = min(16, chunks)
    blocks = chunks // NB
    core, chip, chips = d % 2, d // 2, sections // 2
    has_prev, has_next = d > 0, d < sections - 1
    even = core == 0
    odd = core == 1
    early, middle = (3 * chips) // 16, chips // 2
    masks = lane_masks()
    eye = lax.broadcasted_iota(jnp.int32, (C, C), 0) == lax.broadcasted_iota(jnp.int32, (C, C), 1)

    def at(c):
        return pl.ds(pl.multiple_of(c * LANES, LANES), LANES)

    def copy(src, dst, ssem, rsem, depth_to, image_to=None):
        return pltpu.make_async_remote_copy(
            src_ref=src, dst_ref=dst, send_sem=ssem, recv_sem=rsem,
            device_id=(depth_to, image if image_to is None else image_to),
            device_id_type=pl.DeviceIdType.MESH,
        )

    def brought(src, dst, sem):
        return pltpu.make_async_copy(src, dst, sem)

    def guess_in(c):
        return brought(guess_ref.at[:, at(c)], G.at[0, c + 1], guess_s.at[c])

    def guess_start(c):
        return brought(guess_ref.at[:, at(c)], A.at[0, c + 1], spare_s.at[c])

    def adj_in(c):
        return brought(adj_ref.at[:, at(c)], G.at[0, c + 1], adj_s.at[c])

    def adj_end(c):
        return brought(adj_ref.at[:, at(c)], LR.at[c + 1], spare_s.at[c])

    def each_chunk(action):
        def one(c, _):
            action(c)
            return 0
        lax.fori_loop(0, chunks, one, 0)

    small = [
        brought(src, dst, in_s.at[i])
        for i, (src, dst) in enumerate(((n_hbm, n_ref), (w_hbm, w_ref), (b_hbm, b_ref), (d_hbm, d_ref)))
    ]
    for part in small:
        part.start()
    for c in range(chunks):
        guess_in(c).start()

    barrier = pltpu.get_barrier_semaphore()

    def greet(cond, depth_to, image_to):
        @pl.when(cond)
        def _():
            pl.semaphore_signal(barrier, inc=1, device_id=(depth_to, image_to), device_id_type=pl.DeviceIdType.MESH)

    up2, down2 = jnp.logical_and(odd, chip < chips - 1), jnp.logical_and(odd, chip > 0)
    greet(has_prev, d - 1, image)
    greet(has_next, d + 1, image)
    greet(up2, d + 2, image)
    greet(down2, d - 2, image)
    for o in range(1, images):
        pl.semaphore_signal(
            barrier, inc=1, device_id=(d, (image + o) % images), device_id_type=pl.DeviceIdType.MESH
        )
    partners = (
        has_prev.astype(jnp.int32) + has_next.astype(jnp.int32) + up2.astype(jnp.int32)
        + down2.astype(jnp.int32) + (images - 1)
    )

    starts, ends = jnp.logical_not(has_prev), jnp.logical_not(has_next)

    @pl.when(starts)
    def _():
        each_chunk(lambda c: guess_start(c).start())

    @pl.when(ends)
    def _():
        each_chunk(lambda c: adj_end(c).start())

    zero_chunk = jnp.zeros((C, LANES), F)
    for l in range(MOST + 1):
        A[l, 0] = zero_chunk
        A[l, chunks + 1] = zero_chunk
    for ref in (G.at[0], G.at[1], LR):
        ref[0] = zero_chunk
        ref[chunks + 1] = zero_chunk

    for part in small:
        part.wait()
    n = n_ref[d]
    diff_col = column_of(d_ref[...], eye)
    diff = jnp.broadcast_to(diff_col, (C, LANES))

    def prepare(i, _):
        factor = jnp.where(i < n, 1.0 / MOST, 0.0)
        WC[i] = pack3(w_ref[i])
        WT[i] = pack3(w_ref[i].T * factor)
        BB[i] = jnp.broadcast_to(column_of(b_ref[pl.ds(i, 1), :], eye), (C, LANES))
        FD[i] = diff * factor
        return 0

    lax.fori_loop(0, MOST, prepare, 0, unroll=True)
    for c in range(chunks):
        guess_in(c).wait()

    def forward_block(src, i, j, store, keep):
        u = [src[j * NB + k] for k in range(NB + 2)]
        laps = chunk_laps(u, NB, masks)
        bias = jnp.concatenate([BB[i]] * NB, axis=1)
        act = jnp.tanh(dot3(WC[i], jnp.concatenate(u[1:-1], axis=1)) + bias)
        mixed = dot3(WT[i], act)
        fd = FD[i]
        for k in range(NB):
            store(j * NB + k, u[k + 1] + fd * laps[k] - mixed[:, k * LANES : (k + 1) * LANES])
            if keep is not None:
                keep[j * NB + k] = act[:, k * LANES : (k + 1) * LANES]

    def into(ref, shift):
        def store(c, value):
            ref[c + shift] = value
        return store

    def forward_layer(src, i, store, keep=None, unroll=True):
        def block(j, _):
            forward_block(src, i, j, store, keep)
            return 0
        lax.fori_loop(0, blocks, block, 0, unroll=unroll)

    def first_pass(i, _):
        forward_layer(G.at[i % 2], i, into(G.at[(i + 1) % 2], 1))
        return 0

    lax.fori_loop(0, MOST - 1, first_pass, 0)
    pl.semaphore_wait(barrier, partners)

    def push_copy(j):
        return copy(
            PUSH.at[pl.ds(j * NB, NB)], A.at[0, pl.ds(1 + j * NB, NB)], push_s.at[j], push_r.at[j], d + 1
        )

    def push_block(j, _):
        forward_block(G.at[(MOST - 1) % 2], MOST - 1, j, into(PUSH, 0), None)

        @pl.when(has_next)
        def _():
            push_copy(j).start()
        return 0

    lax.fori_loop(0, blocks, push_block, 0)
    for c in range(chunks):
        adj_in(c).start()

    weight_copy = copy(w_ref.at[0], WP, par_s.at[0], par_r.at[0], d + 1)
    bias_copy = copy(b_ref, BP, par_s.at[1], par_r.at[1], d + 1)

    def first_copy(c):
        return copy(guess_ref.at[:, at(c)], S.at[c], one_s.at[c], st_r.at[c], d + 1)

    @pl.when(even)
    def _():
        weight_copy.start()
        bias_copy.start()

    @pl.when(starts)
    def _():
        def send(c, _):
            first_copy(c).start()
            return 0
        lax.fori_loop(0, chunks, send, 0)

    @pl.when(odd)
    def _():
        coarse_b = n.astype(F) / MOST
        spread(w_ref[0], SPB)
        spread(w_ref[0].T * -coarse_b, SPBT)
        CB[2] = BB[0]
        CB[3] = diff * coarse_b
        weight_copy.wait_recv()
        bias_copy.wait_recv()
        coarse_a = n_ref[d - core].astype(F) / MOST
        spread(WP[...], SPA)
        spread(WP[...].T * -coarse_a, SPAT)
        CB[0] = jnp.broadcast_to(column_of(BP[0:1, :], eye), (C, LANES))
        CB[1] = diff * coarse_a

    @pl.when(has_prev)
    def _():
        for j in range(blocks):
            push_copy(j).wait_recv()

    @pl.when(starts)
    def _():
        each_chunk(lambda c: guess_start(c).wait())

    def second_pass(i, _):
        forward_layer(A.at[i], i, into(A.at[i + 1], 1), T.at[i])
        return 0

    lax.fori_loop(0, MOST, second_pass, 0)

    layers = n.astype(F)

    def tau_of(c):
        start = A[0, c + 1]
        return A[MOST, c + 1] - (start + layers * (A[1, c + 1] - start))

    def tau_copy(j):
        part = pl.ds(j * NB, NB) if j < blocks else pl.ds(chunks, 1)
        return copy(TAU.at[part], TAU_A.at[part], tau_s.at[j], tau_r.at[j], d + 1)

    @pl.when(even)
    def _():
        before = zero_chunk
        for c in range(chunks):
            here = tau_of(c)
            TAU[c] = jnp.where(masks[0], here, before)
            before = here
            if c % NB == NB - 1:
                tau_copy(c // NB).start()
        TAU[chunks] = jnp.where(masks[0], 0.0, before)
        tau_copy(blocks).start()

    @pl.when(odd)
    def _():
        for c in range(chunks):
            TAU[c] = tau_of(c)

    def one_copy(c):
        return copy(S.at[c], S.at[c], one_s.at[c], st_r.at[c], d - 1)

    def two_copy(c):
        return copy(S2.at[c], S.at[c], two_s.at[c], st_r.at[c], d + 2)

    def relay(both):
        bias_a, fd_a, bias_b, fd_b = CB[0], CB[1], CB[2], CB[3]
        lower = masks[0]

        def step(c, carry, first=False, last=False):
            prev, one_prev = carry
            if last:
                now = zero_chunk
            else:
                two_copy(c).wait_recv()
                one_copy(c).start()
                now = S[c]
            mid = jnp.where(lower, now, prev)
            lap = (pltpu.roll(prev + now, 64, 1) + beside(mid, masks)) - 4.0 * mid
            act = jnp.tanh(mix(SPA, mid, bias_a))
            one = mix(SPAT, act, mid + fd_a * lap + TAU_A[c])
            if first:
                one = jnp.where(lower, one, 0.0)
            if last:
                one = jnp.where(lower, 0.0, one)
            if not first:
                mid_one = jnp.where(lower, one_prev, one)
                if both:
                    lap_b = (pltpu.roll(one_prev + one, 64, 1) + beside(mid_one, masks)) - 4.0 * mid_one
                    act_b = jnp.tanh(mix(SPB, mid_one, bias_b))
                    S2[c - 1] = mix(SPBT, act_b, mid_one + fd_b * lap_b + TAU[c - 1])
                    two_copy(c - 1).start()
                s_out[:, at(c - 1)] = mid_one
            return now, one

        tau_copy(0).wait_recv()
        carry = step(0, (zero_chunk,) * 2, first=True)
        for j in range(blocks):
            if j:
                tau_copy(j).wait_recv()
            carry = lax.fori_loop(max(1, j * NB), (j + 1) * NB, step, carry)
        tau_copy(blocks).wait_recv()
        step(chunks, carry, last=True)

    def backward_block(src, i, j, store, with_grads):
        g = [src[j * NB + k] for k in range(NB + 2)]
        laps = chunk_laps(g, NB, masks)
        act = jnp.concatenate([T[i, j * NB + k] for k in range(NB)], axis=1)
        g_hi, g_lo = split2(jnp.concatenate(g[1:-1], axis=1))
        pulled = jnp.dot(WC[i], jnp.concatenate([g_hi, g_lo, g_hi], axis=0), preferred_element_type=F)
        pre = (1.0 - act * act) * pulled
        p_hi, p_lo = split2(pre)
        back = jnp.dot(WT[i], jnp.concatenate([p_hi, p_lo, p_hi], axis=0), preferred_element_type=F)
        fd = FD[i]
        for k in range(NB):
            store(j * NB + k, g[k + 1] + fd * laps[k] - back[:, k * LANES : (k + 1) * LANES])
        if not with_grads:
            return None
        t_hi, t_lo = split2(act)
        u_hi, u_lo = split2(jnp.concatenate([A[i, j * NB + k + 1] for k in range(NB)], axis=1))
        left = jnp.concatenate(
            [jnp.concatenate([t_hi, p_hi], axis=1), jnp.concatenate([t_lo, p_lo], axis=1)], axis=0
        )
        right = jnp.concatenate(
            [jnp.concatenate([g_hi, u_hi], axis=1), jnp.concatenate([g_lo, u_lo], axis=1)], axis=0
        )
        prod = lax.dot_general(left, right, NT, preferred_element_type=F)
        bias_sum = pre[:, :LANES]
        for k in range(1, NB):
            bias_sum = bias_sum + pre[:, k * LANES : (k + 1) * LANES]
        return prod, bias_sum

    def lam_copy(j):
        return copy(LSEND.at[pl.ds(j * NB, NB)], LR.at[pl.ds(1 + j * NB, NB)], lam_s.at[j], lam_r.at[j], d - 1)

    def backward_start():
        for c in range(chunks):
            adj_in(c).wait()

        def layer(i, _):
            def block(j, _):
                backward_block(G.at[i % 2], MOST - 1 - i, j, into(G.at[(i + 1) % 2], 1), False)
                return 0
            lax.fori_loop(0, blocks, block, 0, unroll=True)
            return 0

        lax.fori_loop(0, MOST - 1, layer, 0)

        def block(j, _):
            backward_block(G.at[(MOST - 1) % 2], 0, j, into(LSEND, 0), False)

            @pl.when(has_prev)
            def _():
                lam_copy(j).start()
            return 0

        lax.fori_loop(0, blocks, block, 0)

    def backward_full():
        @pl.when(has_next)
        def _():
            for j in range(blocks):
                lam_copy(j).wait_recv()

        @pl.when(ends)
        def _():
            each_chunk(lambda c: adj_end(c).wait())

        for c in range(chunks):
            G[0, c + 1] = LR[c + 1]
        GB[MOST] = jnp.zeros((C, C), F)

        def layer(i, _):
            slot = MOST - 1 - i
            factor = jnp.where(slot < n, 1.0 / MOST, 0.0)
            start = (jnp.zeros((2 * C, 2 * C), F), jnp.zeros((C, LANES), F))

            def block(j, sums):
                prod, bias_sum = backward_block(G.at[i % 2], slot, j, into(G.at[(i + 1) % 2], 1), True)
                return sums[0] + prod, sums[1] + bias_sum
            prod, bias_sum = lax.fori_loop(0, blocks, block, start, unroll=True)
            GB[slot] = -factor * (prod[:C, :C] + (prod[:C, C:] + prod[C:, :C]))
            column = jnp.sum(bias_sum, axis=1, keepdims=True)
            GB[MOST, pl.ds(slot, 1), :] = -factor * row_of(column, eye)
            return 0

        lax.fori_loop(0, MOST, layer, 0)
        for c in range(chunks):
            a_out[:, c * LANES : (c + 1) * LANES] = G[0, c + 1]
        GR[image] = GB[...]
        for o in range(1, images):
            grad_copy(o).start()

    def grad_copy(o):
        return copy(GB, GR.at[image], grad_s.at[o - 1], grad_r.at[o - 1], d, (image + o) % images)

    def turn(order, _):
        relay_at = jnp.where(chip < early, 0, jnp.where(chip < middle, 1, 2))
        start_at = jnp.where(jnp.logical_and(odd, chip < early), 1, 0)
        full_at = jnp.where(jnp.logical_and(odd, chip >= middle), 1, 2)
        here = jnp.logical_and(odd, order == relay_at)

        @pl.when(jnp.logical_and(here, chip < chips - 1))
        def _():
            relay(True)

        @pl.when(jnp.logical_and(here, chip == chips - 1))
        def _():
            relay(False)

        @pl.when(order == start_at)
        def _():
            backward_start()

        @pl.when(order == full_at)
        def _():
            backward_full()
        return 0

    lax.fori_loop(0, 3, turn, 0)

    for o in range(1, images):
        grad_copy(o).wait_recv()
    for i in range(MOST + 1):
        total = GR[0, i]
        for b in range(1, images):
            total = total + GR[b, i]
        if i < MOST:
            gw_out[i] = total
        else:
            gb_out[...] = total[:MOST]

    @pl.when(even)
    def _():
        def take(c, _):
            one_copy(c).wait_recv()
            s_out[:, at(c)] = S[c]
            return 0
        lax.fori_loop(0, chunks, take, 0)

    for o in range(1, images):
        grad_copy(o).wait_send()

    @pl.when(has_next)
    def _():
        for j in range(blocks):
            push_copy(j).wait_send()

    @pl.when(has_prev)
    def _():
        for j in range(blocks):
            lam_copy(j).wait_send()

    @pl.when(even)
    def _():
        weight_copy.wait_send()
        bias_copy.wait_send()
        for j in range(blocks + 1):
            tau_copy(j).wait_send()

    @pl.when(starts)
    def _():
        def sent(c, _):
            first_copy(c).wait_send()
            return 0
        lax.fori_loop(0, chunks, sent, 0)

    @pl.when(odd)
    def _():
        def sent(c, _):
            one_copy(c).wait_send()
            return 0
        lax.fori_loop(0, chunks, sent, 0)

    @pl.when(up2)
    def _():
        def sent(c, _):
            two_copy(c).wait_send()
            return 0
        lax.fori_loop(0, chunks, sent, 0)


def write_out(*refs):
    sems = refs[8]
    copies = [pltpu.make_async_copy(refs[i], refs[i + 4], sems.at[i]) for i in range(4)]
    for one in copies:
        one.start()
    for one in copies:
        one.wait()


def body(cpoint_guess, adjoint_guess, weights, biases, diffusion, section_len):
    pixels = cpoint_guess.shape[-1]
    images = lax.axis_size("batch")
    chunks = pixels // LANES
    NB = min(16, chunks)
    blocks = chunks // NB
    vmem = pl.BlockSpec(memory_space=pltpu.VMEM)
    image_shape = jax.ShapeDtypeStruct((C, pixels), F)
    dma = pltpu.SemaphoreType.DMA

    def stack(*lead):
        return pltpu.VMEM(lead + (C, LANES), F)

    outs = pl.pallas_call(
        kernel,
        out_shape=(
            image_shape, image_shape,
            jax.ShapeDtypeStruct((MOST, C, C), F), jax.ShapeDtypeStruct((MOST, C), F),
        ),
        in_specs=[pl.BlockSpec(memory_space=pltpu.HBM)] * 6,
        out_specs=(vmem,) * 4,
        scratch_shapes=[
            stack(MOST + 1, chunks + 2), stack(MOST, chunks), stack(2, chunks + 2), stack(chunks + 2),
            stack(chunks), stack(chunks), stack(chunks), stack(chunks), stack(chunks + 1), stack(chunks + 1),
            pltpu.VMEM((MOST, C, 3 * C), BF), pltpu.VMEM((MOST, C, 3 * C), BF), stack(MOST), stack(MOST),
            pltpu.VMEM((C, C), F), pltpu.VMEM((MOST, C), F),
            stack(C), stack(C), stack(C), stack(C), stack(4),
            pltpu.VMEM((MOST + 1, C, C), F), pltpu.VMEM((images, MOST + 1, C, C), F),
            dma((blocks,)), dma((blocks,)), dma((blocks,)), dma((blocks,)), dma((blocks + 1,)), dma((blocks + 1,)),
            dma((2,)), dma((2,)), dma((chunks,)), dma((chunks,)), dma((chunks,)),
            dma((images - 1,)), dma((images - 1,)),
            pltpu.VMEM((MOST, C, C), F), pltpu.VMEM((MOST, C), F), pltpu.VMEM((1, C), F),
            pltpu.SMEM(section_len.shape, jnp.int32), dma((4,)), dma((chunks,)), dma((chunks,)), dma((chunks,)),
        ],
        compiler_params=pltpu.CompilerParams(
            collective_id=0, has_side_effects=True, vmem_limit_bytes=24 << 20
        ),
        name="mgrit_cycle",
    )(
        *(
            pltpu.with_memory_space_constraint(x, pltpu.HBM)
            for x in (
                cpoint_guess.reshape(C, pixels), adjoint_guess.reshape(C, pixels), weights, biases,
                diffusion.reshape(1, C), section_len,
            )
        )
    )
    states_out, adjoint_out, grad_weights, grad_biases = pl.pallas_call(
        write_out,
        out_shape=tuple(jax.ShapeDtypeStruct(o.shape, o.dtype) for o in outs),
        in_specs=[vmem] * 4,
        out_specs=(pl.BlockSpec(memory_space=pltpu.HBM),) * 4,
        scratch_shapes=[dma((4,))],
        compiler_params=pltpu.CompilerParams(vmem_limit_bytes=8 << 20),
        name="write_out",
    )(*outs)
    return states_out[None, None], adjoint_out[None, None], grad_weights, grad_biases


def solution(mesh):
    placed = (
        P("depth", "batch", None, None), P("depth", "batch", None, None), P("depth", None, None),
        P("depth", None), P(), P(),
    )
    return jax.shard_map(
        body, mesh=mesh, in_specs=placed,
        out_specs=(
            P("depth", "batch", None, None), P("depth", "batch", None, None), P("depth", None, None),
            P("depth", None),
        ),
        check_vma=False,
    )
```

```python
import jax
import jax.numpy as jnp
from jax import lax
from jax.experimental import pallas as pl
from jax.experimental.pallas import tpu as pltpu
from jax.sharding import PartitionSpec as P

MOST = 8
C = 32
LANES = 128
F = jnp.float32
BF = jnp.bfloat16
NT = (((1,), (1,)), ((), ()))


def split2(x):
    hi = x.astype(BF)
    return hi, (x - hi.astype(F)).astype(BF)


def dot3(packed, x):
    hi, lo = split2(x)
    return jnp.dot(packed, jnp.concatenate([hi, lo, hi], axis=0), preferred_element_type=F)


def pack3(matrix):
    hi, lo = split2(matrix)
    return jnp.concatenate([hi, hi, lo], axis=1)


def lane_masks():
    lane = lax.broadcasted_iota(jnp.int32, (C, LANES), 1)
    return lane < 64, lane % 64 == 0, lane % 64 == 63


def beside(x, masks):
    zero = jnp.zeros_like(x)
    return jnp.where(masks[1], zero, pltpu.roll(x, 1, 1)) + jnp.where(masks[2], zero, pltpu.roll(x, 127, 1))


def chunk_laps(chunks, count, masks):
    turned = [pltpu.roll(x, 64, 1) for x in chunks]
    laps = []
    for k in range(1, count + 1):
        above_below = turned[k] + jnp.where(masks[0], turned[k - 1], turned[k + 1])
        laps.append((above_below + beside(chunks[k], masks)) - 4.0 * chunks[k])
    return laps


def column_of(row, eye):
    return jnp.sum(jnp.where(eye, jnp.broadcast_to(row, (C, C)), 0.0), axis=1, keepdims=True)


def row_of(column, eye):
    return jnp.sum(jnp.where(eye, jnp.broadcast_to(column, (C, C)), 0.0), axis=0, keepdims=True)


def spread(matrix, out_ref):
    for k in range(C):
        out_ref[k] = jnp.broadcast_to(matrix[:, k : k + 1], (C, LANES))


def mix(spread_ref, x, first):
    sums = [first, None]
    for k in range(C):
        term = spread_ref[k] * jnp.broadcast_to(x[k : k + 1, :], (C, LANES))
        sums[k % 2] = term if sums[k % 2] is None else sums[k % 2] + term
    return sums[0] + sums[1]


def kernel(
    guess_ref, adj_ref, w_hbm, b_hbm, d_hbm, n_hbm,
    s_out, a_out, gw_out, gb_out,
    A, T, H, G, LR, LSEND, S, S2, TAU, TAU_A,
    WC, WT, BB, FD, WP, BP, SPA, SPAT, SPB, SPBT, CB, GB, GR,
    push_s, push_r, lam_s, lam_r, tau_s, tau_r, par_s, par_r, one_s, two_s, st_r, grad_s, grad_r,
    w_ref, b_ref, d_ref, n_ref, in_s, guess_s, adj_s, spare_s,
):
    sections, images = lax.axis_size("depth"), lax.axis_size("batch")
    d, image = lax.axis_index("depth"), lax.axis_index("batch")
    chunks = guess_ref.shape[1] // LANES
    blocks = 2
    NB = chunks // blocks
    halo = MOST // 2
    core, chip, chips = d % 2, d // 2, sections // 2
    has_prev, has_next = d > 0, d < sections - 1
    even = core == 0
    odd = core == 1
    early = (3 * chips) // 16
    ahead = jnp.where(even, MOST, jnp.where(chip >= (12 * chips) // 16, MOST, jnp.clip(2 * (chip - (9 * chips) // 16) - 1, 0, MOST)))
    masks = lane_masks()
    eye = lax.broadcasted_iota(jnp.int32, (C, C), 0) == lax.broadcasted_iota(jnp.int32, (C, C), 1)

    def at(c):
        return pl.ds(pl.multiple_of(c * LANES, LANES), LANES)

    def copy(src, dst, ssem, rsem, depth_to, image_to=None):
        return pltpu.make_async_remote_copy(
            src_ref=src, dst_ref=dst, send_sem=ssem, recv_sem=rsem,
            device_id=(depth_to, image if image_to is None else image_to),
            device_id_type=pl.DeviceIdType.MESH,
        )

    def brought(src, dst, sem):
        return pltpu.make_async_copy(src, dst, sem)

    def guess_in(c):
        return brought(guess_ref.at[:, at(c)], H.at[0, c + 1], guess_s.at[c])

    def guess_start(c):
        return brought(guess_ref.at[:, at(c)], A.at[0, c + 1], spare_s.at[c])

    def adj_in(c):
        return brought(adj_ref.at[:, at(c)], G.at[0, c + 1], adj_s.at[c])

    def adj_end(c):
        return brought(adj_ref.at[:, at(c)], LR.at[c + 1], spare_s.at[c])

    def each_chunk(action):
        def one(c, _):
            action(c)
            return 0
        lax.fori_loop(0, chunks, one, 0)

    small = [
        brought(src, dst, in_s.at[i])
        for i, (src, dst) in enumerate(((n_hbm, n_ref), (w_hbm, w_ref), (b_hbm, b_ref), (d_hbm, d_ref)))
    ]
    for part in small:
        part.start()
    for c in range(chunks):
        guess_in(c).start()
    for c in range(chunks):
        adj_in(c).start()

    barrier = pltpu.get_barrier_semaphore()

    def greet(cond, depth_to, image_to):
        @pl.when(cond)
        def _():
            pl.semaphore_signal(barrier, inc=1, device_id=(depth_to, image_to), device_id_type=pl.DeviceIdType.MESH)

    up2, down2 = jnp.logical_and(odd, chip < chips - 1), jnp.logical_and(odd, chip > 0)
    greet(has_prev, d - 1, image)
    greet(has_next, d + 1, image)
    greet(up2, d + 2, image)
    greet(down2, d - 2, image)
    for o in range(1, images):
        pl.semaphore_signal(
            barrier, inc=1, device_id=(d, (image + o) % images), device_id_type=pl.DeviceIdType.MESH
        )
    partners = (
        has_prev.astype(jnp.int32) + has_next.astype(jnp.int32) + up2.astype(jnp.int32)
        + down2.astype(jnp.int32) + (images - 1)
    )

    starts, ends = jnp.logical_not(has_prev), jnp.logical_not(has_next)

    @pl.when(starts)
    def _():
        each_chunk(lambda c: guess_start(c).start())

    @pl.when(ends)
    def _():
        each_chunk(lambda c: adj_end(c).start())

    zero_chunk = jnp.zeros((C, LANES), F)
    for l in range(MOST + 1):
        for ref in (A, H):
            ref[l, 0] = zero_chunk
            ref[l, chunks + 1] = zero_chunk
    for ref in (G.at[0], G.at[1], LR):
        ref[0] = zero_chunk
        ref[chunks + 1] = zero_chunk

    for part in small:
        part.wait()
    n = n_ref[d]
    diff_col = column_of(d_ref[...], eye)
    diff = jnp.broadcast_to(diff_col, (C, LANES))

    def prepare(i, _):
        factor = jnp.where(i < n, 1.0 / MOST, 0.0)
        WC[i] = pack3(w_ref[i])
        WT[i] = pack3(w_ref[i].T * factor)
        BB[i] = jnp.broadcast_to(column_of(b_ref[pl.ds(i, 1), :], eye), (C, LANES))
        FD[i] = diff * factor
        return 0

    lax.fori_loop(0, MOST, prepare, 0, unroll=True)
    for c in range(chunks):
        guess_in(c).wait()

    def forward_tile(src, i, lo, count, dst, keep, open_end):
        u = [src[lo + k] for k in range(count + 1)] + [zero_chunk if open_end else src[lo + count + 1]]
        laps = chunk_laps(u, count, masks)
        bias = jnp.concatenate([BB[i]] * count, axis=1)
        act = jnp.tanh(dot3(WC[i], jnp.concatenate(u[1:-1], axis=1)) + bias)
        mixed = dot3(WT[i], act)
        fd = FD[i]
        for k in range(count):
            dst[lo + k + 1] = u[k + 1] + fd * laps[k] - mixed[:, k * LANES : (k + 1) * LANES]
            if keep is not None:
                keep[lo + k] = act[:, k * LANES : (k + 1) * LANES]

    def into(ref, shift):
        def store(c, value):
            ref[c + shift] = value
        return store

    def sweep(stack, keeps, lo, count, open_end):
        def layer(i, _):
            keep = None if keeps is None else keeps.at[i]
            forward_tile(stack.at[i], i, lo, count, stack.at[i + 1], keep, open_end)
            return 0
        lax.fori_loop(0, MOST, layer, 0)

    upper = NB + halo

    def push_copy(j):
        part = pl.ds(1, upper) if j == 0 else pl.ds(1 + upper, chunks - upper)
        return copy(H.at[MOST, part], A.at[0, part], push_s.at[j], push_r.at[j], d + 1)

    def push(j):
        @pl.when(has_next)
        def _():
            push_copy(j).start()

    first = min(upper + halo, chunks)
    sweep(H, None, 0, first, first < chunks)
    pl.semaphore_wait(barrier, partners)
    push(0)
    sweep(H, None, upper, chunks - upper, False)
    push(1)

    weight_copy = copy(w_ref.at[0], WP, par_s.at[0], par_r.at[0], d + 1)
    bias_copy = copy(b_ref, BP, par_s.at[1], par_r.at[1], d + 1)

    def first_copy(c):
        return copy(guess_ref.at[:, at(c)], S.at[c], one_s.at[c], st_r.at[c], d + 1)

    @pl.when(even)
    def _():
        weight_copy.start()
        bias_copy.start()

    @pl.when(starts)
    def _():
        def send(c, _):
            first_copy(c).start()
            return 0
        lax.fori_loop(0, chunks, send, 0)

    @pl.when(odd)
    def _():
        coarse_b = n.astype(F) / MOST
        spread(w_ref[0], SPB)
        spread(w_ref[0].T * -coarse_b, SPBT)
        CB[2] = BB[0]
        CB[3] = diff * coarse_b
        weight_copy.wait_recv()
        bias_copy.wait_recv()
        coarse_a = n_ref[d - core].astype(F) / MOST
        spread(WP[...], SPA)
        spread(WP[...].T * -coarse_a, SPAT)
        CB[0] = jnp.broadcast_to(column_of(BP[0:1, :], eye), (C, LANES))
        CB[1] = diff * coarse_a

    layers = n.astype(F)

    def tau_of(c):
        start = A[0, c + 1]
        return A[MOST, c + 1] - (start + layers * (A[1, c + 1] - start))

    def tau_copy(j):
        part = pl.ds(0, NB) if j == 0 else pl.ds(NB, chunks + 1 - NB)
        return copy(TAU.at[part], TAU_A.at[part], tau_s.at[j], tau_r.at[j], d + 1)

    @pl.when(starts)
    def _():
        each_chunk(lambda c: guess_start(c).wait())

    for j in range(blocks):
        @pl.when(has_prev)
        def _():
            push_copy(j).wait_recv()

        if j == 0:
            sweep(A, T, 0, upper, True)
        else:
            sweep(A, T, NB, chunks - NB, False)

        @pl.when(even)
        def _():
            before = zero_chunk if j == 0 else tau_of(NB - 1)
            for c in range(j * NB, (j + 1) * NB):
                here = tau_of(c)
                TAU[c] = jnp.where(masks[0], here, before)
                before = here
            if j == blocks - 1:
                TAU[chunks] = jnp.where(masks[0], 0.0, before)
            tau_copy(j).start()

        @pl.when(odd)
        def _():
            for c in range(j * NB, (j + 1) * NB):
                TAU[c] = tau_of(c)

    def one_copy(c):
        return copy(S.at[c], S.at[c], one_s.at[c], st_r.at[c], d - 1)

    def two_copy(c):
        return copy(S2.at[c], S.at[c], two_s.at[c], st_r.at[c], d + 2)

    def relay(both):
        bias_a, fd_a, bias_b, fd_b = CB[0], CB[1], CB[2], CB[3]
        lower = masks[0]

        def step(c, carry, first=False, last=False):
            prev, one_prev = carry
            if last:
                now = zero_chunk
            else:
                two_copy(c).wait_recv()
                one_copy(c).start()
                now = S[c]
            mid = jnp.where(lower, now, prev)
            lap = (pltpu.roll(prev + now, 64, 1) + beside(mid, masks)) - 4.0 * mid
            act = jnp.tanh(mix(SPA, mid, bias_a))
            one = mix(SPAT, act, mid + fd_a * lap + TAU_A[c])
            if first:
                one = jnp.where(lower, one, 0.0)
            if last:
                one = jnp.where(lower, 0.0, one)
            if not first:
                mid_one = jnp.where(lower, one_prev, one)
                if both:
                    lap_b = (pltpu.roll(one_prev + one, 64, 1) + beside(mid_one, masks)) - 4.0 * mid_one
                    act_b = jnp.tanh(mix(SPB, mid_one, bias_b))
                    S2[c - 1] = mix(SPBT, act_b, mid_one + fd_b * lap_b + TAU[c - 1])
                    two_copy(c - 1).start()
                s_out[:, at(c - 1)] = mid_one
            return now, one

        tau_copy(0).wait_recv()
        carry = step(0, (zero_chunk,) * 2, first=True)
        for j in range(blocks):
            if j:
                tau_copy(j).wait_recv()
            carry = lax.fori_loop(max(1, j * NB), (j + 1) * NB, step, carry)
        step(chunks, carry, last=True)

    def backward_block(src, i, j, store, with_grads):
        g = [src[j * NB + k] for k in range(NB + 2)]
        laps = chunk_laps(g, NB, masks)
        act = jnp.concatenate([T[i, j * NB + k] for k in range(NB)], axis=1)
        g_hi, g_lo = split2(jnp.concatenate(g[1:-1], axis=1))
        pulled = jnp.dot(WC[i], jnp.concatenate([g_hi, g_lo, g_hi], axis=0), preferred_element_type=F)
        pre = (1.0 - act * act) * pulled
        p_hi, p_lo = split2(pre)
        back = jnp.dot(WT[i], jnp.concatenate([p_hi, p_lo, p_hi], axis=0), preferred_element_type=F)
        fd = FD[i]
        for k in range(NB):
            store(j * NB + k, g[k + 1] + fd * laps[k] - back[:, k * LANES : (k + 1) * LANES])
        if not with_grads:
            return None
        t_hi, t_lo = split2(act)
        u_hi, u_lo = split2(jnp.concatenate([A[i, j * NB + k + 1] for k in range(NB)], axis=1))
        left = jnp.concatenate(
            [jnp.concatenate([t_hi, p_hi], axis=1), jnp.concatenate([t_lo, p_lo], axis=1)], axis=0
        )
        right = jnp.concatenate(
            [jnp.concatenate([g_hi, u_hi], axis=1), jnp.concatenate([g_lo, u_lo], axis=1)], axis=0
        )
        prod = lax.dot_general(left, right, NT, preferred_element_type=F)
        bias_sum = pre[:, :LANES]
        for k in range(1, NB):
            bias_sum = bias_sum + pre[:, k * LANES : (k + 1) * LANES]
        return prod, bias_sum

    def lam_copy(j):
        return copy(LSEND.at[pl.ds(j * NB, NB)], LR.at[pl.ds(1 + j * NB, NB)], lam_s.at[j], lam_r.at[j], d - 1)

    def backward_start():
        for c in range(chunks):
            adj_in(c).wait()

        def layer(i, _):
            def block(j, _):
                backward_block(G.at[i % 2], MOST - 1 - i, j, into(G.at[(i + 1) % 2], 1), False)
                return 0
            lax.fori_loop(0, blocks, block, 0, unroll=True)
            return 0

        lax.fori_loop(0, MOST - 1, layer, 0)

        def block(j, _):
            backward_block(G.at[(MOST - 1) % 2], 0, j, into(LSEND, 0), False)

            @pl.when(has_prev)
            def _():
                lam_copy(j).start()
            return 0

        lax.fori_loop(0, blocks, block, 0)

    def full_ready():
        @pl.when(has_next)
        def _():
            for j in range(blocks):
                lam_copy(j).wait_recv()

        @pl.when(ends)
        def _():
            each_chunk(lambda c: adj_end(c).wait())

        for c in range(chunks):
            G[0, c + 1] = LR[c + 1]
        GB[MOST] = jnp.zeros((C, C), F)

    def full_layers(first_layer, end_layer):
        def layer(i, _):
            slot = MOST - 1 - i
            factor = jnp.where(slot < n, 1.0 / MOST, 0.0)
            start = (jnp.zeros((2 * C, 2 * C), F), jnp.zeros((C, LANES), F))

            def block(j, sums):
                prod, bias_sum = backward_block(G.at[i % 2], slot, j, into(G.at[(i + 1) % 2], 1), True)
                return sums[0] + prod, sums[1] + bias_sum
            prod, bias_sum = lax.fori_loop(0, blocks, block, start, unroll=True)
            GB[slot] = -factor * (prod[:C, :C] + (prod[:C, C:] + prod[C:, :C]))
            column = jnp.sum(bias_sum, axis=1, keepdims=True)
            GB[MOST, pl.ds(slot, 1), :] = -factor * row_of(column, eye)
            return 0

        lax.fori_loop(first_layer, end_layer, layer, 0)

    def grad_copy(o):
        return copy(GB, GR.at[image], grad_s.at[o - 1], grad_r.at[o - 1], d, (image + o) % images)

    def turn(order, _):
        here = jnp.logical_and(odd, order == jnp.where(chip < early, 0, 3))

        @pl.when(jnp.logical_and(here, chip < chips - 1))
        def _():
            relay(True)

        @pl.when(jnp.logical_and(here, chip == chips - 1))
        def _():
            relay(False)

        @pl.when(order == 1)
        def _():
            backward_start()

        @pl.when(order == jnp.where(ahead > 0, 2, 4))
        def _():
            full_ready()

        @pl.when(jnp.logical_or(order == 2, order == 4))
        def _():
            full_layers(jnp.where(order == 2, 0, ahead), jnp.where(order == 2, ahead, MOST))
        return 0

    lax.fori_loop(0, 5, turn, 0)
    GR[image] = GB[...]
    for o in range(1, images):
        grad_copy(o).start()
    for c in range(chunks):
        a_out[:, c * LANES : (c + 1) * LANES] = G[0, c + 1]
    for o in range(1, images):
        grad_copy(o).wait_recv()
    for i in range(MOST + 1):
        total = GR[0, i]
        for b in range(1, images):
            total = total + GR[b, i]
        if i < MOST:
            gw_out[i] = total
        else:
            gb_out[...] = total[:MOST]

    @pl.when(even)
    def _():
        def take(c, _):
            one_copy(c).wait_recv()
            s_out[:, at(c)] = S[c]
            return 0
        lax.fori_loop(0, chunks, take, 0)

    for o in range(1, images):
        grad_copy(o).wait_send()

    @pl.when(has_next)
    def _():
        for j in range(blocks):
            push_copy(j).wait_send()

    @pl.when(has_prev)
    def _():
        for j in range(blocks):
            lam_copy(j).wait_send()

    @pl.when(even)
    def _():
        weight_copy.wait_send()
        bias_copy.wait_send()
        for j in range(blocks):
            tau_copy(j).wait_send()

    @pl.when(starts)
    def _():
        def sent(c, _):
            first_copy(c).wait_send()
            return 0
        lax.fori_loop(0, chunks, sent, 0)

    @pl.when(odd)
    def _():
        def sent(c, _):
            one_copy(c).wait_send()
            return 0
        lax.fori_loop(0, chunks, sent, 0)

    @pl.when(up2)
    def _():
        def sent(c, _):
            two_copy(c).wait_send()
            return 0
        lax.fori_loop(0, chunks, sent, 0)


def write_out(*refs):
    sems = refs[8]
    copies = [pltpu.make_async_copy(refs[i], refs[i + 4], sems.at[i]) for i in range(4)]
    for one in copies:
        one.start()
    for one in copies:
        one.wait()


def body(cpoint_guess, adjoint_guess, weights, biases, diffusion, section_len):
    pixels = cpoint_guess.shape[-1]
    images = lax.axis_size("batch")
    chunks = pixels // LANES
    blocks = 2
    vmem = pl.BlockSpec(memory_space=pltpu.VMEM)
    image_shape = jax.ShapeDtypeStruct((C, pixels), F)
    dma = pltpu.SemaphoreType.DMA

    def stack(*lead):
        return pltpu.VMEM(lead + (C, LANES), F)

    outs = pl.pallas_call(
        kernel,
        out_shape=(
            image_shape, image_shape,
            jax.ShapeDtypeStruct((MOST, C, C), F), jax.ShapeDtypeStruct((MOST, C), F),
        ),
        in_specs=[pl.BlockSpec(memory_space=pltpu.HBM)] * 6,
        out_specs=(vmem,) * 4,
        scratch_shapes=[
            stack(MOST + 1, chunks + 2), stack(MOST, chunks), stack(MOST + 1, chunks + 2), stack(2, chunks + 2),
            stack(chunks + 2), stack(chunks), stack(chunks), stack(chunks), stack(chunks + 1), stack(chunks + 1),
            pltpu.VMEM((MOST, C, 3 * C), BF), pltpu.VMEM((MOST, C, 3 * C), BF), stack(MOST), stack(MOST),
            pltpu.VMEM((C, C), F), pltpu.VMEM((MOST, C), F),
            stack(C), stack(C), stack(C), stack(C), stack(4),
            pltpu.VMEM((MOST + 1, C, C), F), pltpu.VMEM((images, MOST + 1, C, C), F),
            dma((blocks,)), dma((blocks,)), dma((blocks,)), dma((blocks,)), dma((blocks,)), dma((blocks,)),
            dma((2,)), dma((2,)), dma((chunks,)), dma((chunks,)), dma((chunks,)),
            dma((images - 1,)), dma((images - 1,)),
            pltpu.VMEM((MOST, C, C), F), pltpu.VMEM((MOST, C), F), pltpu.VMEM((1, C), F),
            pltpu.SMEM(section_len.shape, jnp.int32), dma((4,)), dma((chunks,)), dma((chunks,)), dma((chunks,)),
        ],
        compiler_params=pltpu.CompilerParams(
            collective_id=0, has_side_effects=True, vmem_limit_bytes=32 << 20
        ),
        name="mgrit_cycle",
    )(
        *(
            pltpu.with_memory_space_constraint(x, pltpu.HBM)
            for x in (
                cpoint_guess.reshape(C, pixels), adjoint_guess.reshape(C, pixels), weights, biases,
                diffusion.reshape(1, C), section_len,
            )
        )
    )
    states_out, adjoint_out, grad_weights, grad_biases = pl.pallas_call(
        write_out,
        out_shape=tuple(jax.ShapeDtypeStruct(o.shape, o.dtype) for o in outs),
        in_specs=[vmem] * 4,
        out_specs=(pl.BlockSpec(memory_space=pltpu.HBM),) * 4,
        scratch_shapes=[dma((4,))],
        compiler_params=pltpu.CompilerParams(vmem_limit_bytes=8 << 20),
        name="write_out",
    )(*outs)
    return states_out[None, None], adjoint_out[None, None], grad_weights, grad_biases


def solution(mesh):
    placed = (
        P("depth", "batch", None, None), P("depth", "batch", None, None), P("depth", None, None),
        P("depth", None), P(), P(),
    )
    return jax.shard_map(
        body, mesh=mesh, in_specs=placed,
        out_specs=(
            P("depth", "batch", None, None), P("depth", "batch", None, None), P("depth", None, None),
            P("depth", None),
        ),
        check_vma=False,
    )
```

```python
import jax
import jax.numpy as jnp
from jax import lax
from jax.experimental import pallas as pl
from jax.experimental.pallas import tpu as pltpu
from jax.sharding import PartitionSpec as P

MOST = 8
C = 32
LANES = 128
F = jnp.float32
BF = jnp.bfloat16
NT = (((1,), (1,)), ((), ()))


def split2(x):
    hi = x.astype(BF)
    return hi, (x - hi.astype(F)).astype(BF)


def dot3(packed, x):
    hi, lo = split2(x)
    return jnp.dot(packed, jnp.concatenate([hi, lo, hi], axis=0), preferred_element_type=F)


def pack3(matrix):
    hi, lo = split2(matrix)
    return jnp.concatenate([hi, hi, lo], axis=1)


def lane_masks():
    lane = lax.broadcasted_iota(jnp.int32, (C, LANES), 1)
    return lane < 64, lane % 64 == 0, lane % 64 == 63


def beside(x, masks):
    zero = jnp.zeros_like(x)
    return jnp.where(masks[1], zero, pltpu.roll(x, 1, 1)) + jnp.where(masks[2], zero, pltpu.roll(x, 127, 1))


def chunk_laps(chunks, count, masks):
    turned = [pltpu.roll(x, 64, 1) for x in chunks]
    laps = []
    for k in range(1, count + 1):
        above_below = turned[k] + jnp.where(masks[0], turned[k - 1], turned[k + 1])
        laps.append((above_below + beside(chunks[k], masks)) - 4.0 * chunks[k])
    return laps


def column_of(row, eye):
    return jnp.sum(jnp.where(eye, jnp.broadcast_to(row, (C, C)), 0.0), axis=1, keepdims=True)


def row_of(column, eye):
    return jnp.sum(jnp.where(eye, jnp.broadcast_to(column, (C, C)), 0.0), axis=0, keepdims=True)


def spread(matrix, out_ref):
    for k in range(C):
        out_ref[k] = jnp.broadcast_to(matrix[:, k : k + 1], (C, LANES))


def mix(spread_ref, x, first):
    sums = [first, None]
    for k in range(C):
        term = spread_ref[k] * jnp.broadcast_to(x[k : k + 1, :], (C, LANES))
        sums[k % 2] = term if sums[k % 2] is None else sums[k % 2] + term
    return sums[0] + sums[1]


def kernel(
    guess_ref, adj_ref, w_hbm, b_hbm, d_hbm, n_hbm,
    s_out, a_out, gw_out, gb_out,
    A, T, H, G, LR, LSEND, S, S2, TAU, TAU_A,
    WC, WT, BB, FD, WP, BP, SPA, SPAT, SPB, SPBT, CB, GB, PK, GR,
    push_s, push_r, lam_s, lam_r, tau_s, tau_r, par_s, par_r, one_s, two_s, st_r, grad_s, grad_r,
    w_ref, b_ref, d_ref, n_ref, in_s, guess_s, adj_s, spare_s,
):
    sections, images = lax.axis_size("depth"), lax.axis_size("batch")
    d, image = lax.axis_index("depth"), lax.axis_index("batch")
    chunks = guess_ref.shape[1] // LANES
    blocks = 2
    NB = chunks // blocks
    halo = MOST // 2
    core, chip, chips = d % 2, d // 2, sections // 2
    has_prev, has_next = d > 0, d < sections - 1
    even = core == 0
    odd = core == 1
    early = (3 * chips) // 16
    ahead = jnp.where(even, MOST, jnp.where(chip >= (12 * chips) // 16, MOST, jnp.clip(2 * (chip - (9 * chips) // 16) - 1, 0, MOST)))
    masks = lane_masks()
    eye = lax.broadcasted_iota(jnp.int32, (C, C), 0) == lax.broadcasted_iota(jnp.int32, (C, C), 1)

    def at(c):
        return pl.ds(pl.multiple_of(c * LANES, LANES), LANES)

    def copy(src, dst, ssem, rsem, depth_to, image_to=None):
        return pltpu.make_async_remote_copy(
            src_ref=src, dst_ref=dst, send_sem=ssem, recv_sem=rsem,
            device_id=(depth_to, image if image_to is None else image_to),
            device_id_type=pl.DeviceIdType.MESH,
        )

    def brought(src, dst, sem):
        return pltpu.make_async_copy(src, dst, sem)

    def guess_in(c):
        return brought(guess_ref.at[:, at(c)], H.at[0, c + 1], guess_s.at[c])

    def guess_start(c):
        return brought(guess_ref.at[:, at(c)], A.at[0, c + 1], spare_s.at[c])

    def adj_in(c):
        return brought(adj_ref.at[:, at(c)], G.at[0, c + 1], adj_s.at[c])

    def adj_end(c):
        return brought(adj_ref.at[:, at(c)], LR.at[c + 1], spare_s.at[c])

    def each_chunk(action):
        def one(c, _):
            action(c)
            return 0
        lax.fori_loop(0, chunks, one, 0)

    small = [
        brought(src, dst, in_s.at[i])
        for i, (src, dst) in enumerate(((n_hbm, n_ref), (w_hbm, w_ref), (b_hbm, b_ref), (d_hbm, d_ref)))
    ]
    for part in small:
        part.start()
    for c in range(chunks):
        guess_in(c).start()
    for c in range(chunks):
        adj_in(c).start()

    barrier = pltpu.get_barrier_semaphore()

    def greet(cond, depth_to, image_to):
        @pl.when(cond)
        def _():
            pl.semaphore_signal(barrier, inc=1, device_id=(depth_to, image_to), device_id_type=pl.DeviceIdType.MESH)

    up2, down2 = jnp.logical_and(odd, chip < chips - 1), jnp.logical_and(odd, chip > 0)
    greet(has_prev, d - 1, image)
    greet(has_next, d + 1, image)
    greet(up2, d + 2, image)
    greet(down2, d - 2, image)
    for o in range(1, images):
        pl.semaphore_signal(
            barrier, inc=1, device_id=(d, (image + o) % images), device_id_type=pl.DeviceIdType.MESH
        )
    partners = (
        has_prev.astype(jnp.int32) + has_next.astype(jnp.int32) + up2.astype(jnp.int32)
        + down2.astype(jnp.int32) + (images - 1)
    )

    starts, ends = jnp.logical_not(has_prev), jnp.logical_not(has_next)

    @pl.when(starts)
    def _():
        each_chunk(lambda c: guess_start(c).start())

    @pl.when(ends)
    def _():
        each_chunk(lambda c: adj_end(c).start())

    zero_chunk = jnp.zeros((C, LANES), F)
    for l in range(MOST + 1):
        for ref in (A, H):
            ref[l, 0] = zero_chunk
            ref[l, chunks + 1] = zero_chunk
    for ref in (G.at[0], G.at[1], LR):
        ref[0] = zero_chunk
        ref[chunks + 1] = zero_chunk

    for part in small:
        part.wait()
    n = n_ref[d]
    diff_col = column_of(d_ref[...], eye)
    diff = jnp.broadcast_to(diff_col, (C, LANES))

    def prepare(i, _):
        factor = jnp.where(i < n, 1.0 / MOST, 0.0)
        WC[i] = pack3(w_ref[i])
        WT[i] = pack3(w_ref[i].T * factor)
        BB[i] = jnp.broadcast_to(column_of(b_ref[pl.ds(i, 1), :], eye), (C, LANES))
        FD[i] = diff * factor
        return 0

    lax.fori_loop(0, MOST, prepare, 0, unroll=True)
    for c in range(chunks):
        guess_in(c).wait()

    def forward_tile(src, i, lo, count, dst, keep, open_end):
        u = [src[lo + k] for k in range(count + 1)] + [zero_chunk if open_end else src[lo + count + 1]]
        laps = chunk_laps(u, count, masks)
        bias = jnp.concatenate([BB[i]] * count, axis=1)
        act = jnp.tanh(dot3(WC[i], jnp.concatenate(u[1:-1], axis=1)) + bias)
        mixed = dot3(WT[i], act)
        fd = FD[i]
        for k in range(count):
            dst[lo + k + 1] = u[k + 1] + fd * laps[k] - mixed[:, k * LANES : (k + 1) * LANES]
            if keep is not None:
                keep[lo + k] = act[:, k * LANES : (k + 1) * LANES]

    def into(ref, shift):
        def store(c, value):
            ref[c + shift] = value
        return store

    def sweep(stack, keeps, lo, count, open_end):
        def layer(i, _):
            keep = None if keeps is None else keeps.at[i]
            forward_tile(stack.at[i], i, lo, count, stack.at[i + 1], keep, open_end)
            return 0
        lax.fori_loop(0, MOST, layer, 0)

    upper = NB + halo

    def push_copy(j):
        part = pl.ds(1, upper) if j == 0 else pl.ds(1 + upper, chunks - upper)
        return copy(H.at[MOST, part], A.at[0, part], push_s.at[j], push_r.at[j], d + 1)

    def push(j):
        @pl.when(has_next)
        def _():
            push_copy(j).start()

    first = min(upper + halo, chunks)
    sweep(H, None, 0, first, first < chunks)
    pl.semaphore_wait(barrier, partners)
    push(0)
    sweep(H, None, upper, chunks - upper, False)
    push(1)

    weight_copy = copy(w_ref.at[0], WP, par_s.at[0], par_r.at[0], d + 1)
    bias_copy = copy(b_ref, BP, par_s.at[1], par_r.at[1], d + 1)

    def first_copy(c):
        return copy(guess_ref.at[:, at(c)], S.at[c], one_s.at[c], st_r.at[c], d + 1)

    @pl.when(even)
    def _():
        weight_copy.start()
        bias_copy.start()

    @pl.when(starts)
    def _():
        def send(c, _):
            first_copy(c).start()
            return 0
        lax.fori_loop(0, chunks, send, 0)

    @pl.when(odd)
    def _():
        coarse_b = n.astype(F) / MOST
        spread(w_ref[0], SPB)
        spread(w_ref[0].T * -coarse_b, SPBT)
        CB[2] = BB[0]
        CB[3] = diff * coarse_b
        weight_copy.wait_recv()
        bias_copy.wait_recv()
        coarse_a = n_ref[d - core].astype(F) / MOST
        spread(WP[...], SPA)
        spread(WP[...].T * -coarse_a, SPAT)
        CB[0] = jnp.broadcast_to(column_of(BP[0:1, :], eye), (C, LANES))
        CB[1] = diff * coarse_a

    layers = n.astype(F)

    def tau_of(c):
        start = A[0, c + 1]
        return A[MOST, c + 1] - (start + layers * (A[1, c + 1] - start))

    def tau_copy(j):
        part = pl.ds(0, NB) if j == 0 else pl.ds(NB, chunks + 1 - NB)
        return copy(TAU.at[part], TAU_A.at[part], tau_s.at[j], tau_r.at[j], d + 1)

    @pl.when(starts)
    def _():
        each_chunk(lambda c: guess_start(c).wait())

    for j in range(blocks):
        @pl.when(has_prev)
        def _():
            push_copy(j).wait_recv()

        if j == 0:
            sweep(A, T, 0, upper, True)
        else:
            sweep(A, T, NB, chunks - NB, False)

        @pl.when(even)
        def _():
            before = zero_chunk if j == 0 else tau_of(NB - 1)
            for c in range(j * NB, (j + 1) * NB):
                here = tau_of(c)
                TAU[c] = jnp.where(masks[0], here, before)
                before = here
            if j == blocks - 1:
                TAU[chunks] = jnp.where(masks[0], 0.0, before)
            tau_copy(j).start()

        @pl.when(odd)
        def _():
            for c in range(j * NB, (j + 1) * NB):
                TAU[c] = tau_of(c)

    def one_copy(c):
        return copy(S.at[c], S.at[c], one_s.at[c], st_r.at[c], d - 1)

    def two_copy(c):
        return copy(S2.at[c], S.at[c], two_s.at[c], st_r.at[c], d + 2)

    def relay(both):
        bias_a, fd_a, bias_b, fd_b = CB[0], CB[1], CB[2], CB[3]
        lower = masks[0]

        def step(c, carry, first=False, last=False):
            prev, one_prev = carry
            if last:
                now = zero_chunk
            else:
                two_copy(c).wait_recv()
                one_copy(c).start()
                now = S[c]
            mid = jnp.where(lower, now, prev)
            lap = (pltpu.roll(prev + now, 64, 1) + beside(mid, masks)) - 4.0 * mid
            act = jnp.tanh(mix(SPA, mid, bias_a))
            one = mix(SPAT, act, mid + fd_a * lap + TAU_A[c])
            if first:
                one = jnp.where(lower, one, 0.0)
            if last:
                one = jnp.where(lower, 0.0, one)
            if not first:
                mid_one = jnp.where(lower, one_prev, one)
                if both:
                    lap_b = (pltpu.roll(one_prev + one, 64, 1) + beside(mid_one, masks)) - 4.0 * mid_one
                    act_b = jnp.tanh(mix(SPB, mid_one, bias_b))
                    S2[c - 1] = mix(SPBT, act_b, mid_one + fd_b * lap_b + TAU[c - 1])
                    two_copy(c - 1).start()
                s_out[:, at(c - 1)] = mid_one
            return now, one

        tau_copy(0).wait_recv()
        carry = step(0, (zero_chunk,) * 2, first=True)
        for j in range(blocks):
            if j:
                tau_copy(j).wait_recv()
            carry = lax.fori_loop(max(1, j * NB), (j + 1) * NB, step, carry)
        step(chunks, carry, last=True)

    def backward_block(src, i, j, store, with_grads):
        g = [src[j * NB + k] for k in range(NB + 2)]
        laps = chunk_laps(g, NB, masks)
        act = jnp.concatenate([T[i, j * NB + k] for k in range(NB)], axis=1)
        g_hi, g_lo = split2(jnp.concatenate(g[1:-1], axis=1))
        pulled = jnp.dot(WC[i], jnp.concatenate([g_hi, g_lo, g_hi], axis=0), preferred_element_type=F)
        pre = (1.0 - act * act) * pulled
        p_hi, p_lo = split2(pre)
        back = jnp.dot(WT[i], jnp.concatenate([p_hi, p_lo, p_hi], axis=0), preferred_element_type=F)
        fd = FD[i]
        for k in range(NB):
            store(j * NB + k, g[k + 1] + fd * laps[k] - back[:, k * LANES : (k + 1) * LANES])
        if not with_grads:
            return None
        t_hi, t_lo = split2(act)
        u_hi, u_lo = split2(jnp.concatenate([A[i, j * NB + k + 1] for k in range(NB)], axis=1))
        left = jnp.concatenate(
            [jnp.concatenate([t_hi, p_hi], axis=1), jnp.concatenate([t_lo, p_lo], axis=1)], axis=0
        )
        right = jnp.concatenate(
            [jnp.concatenate([g_hi, u_hi], axis=1), jnp.concatenate([g_lo, u_lo], axis=1)], axis=0
        )
        prod = lax.dot_general(left, right, NT, preferred_element_type=F)
        bias_sum = pre[:, :LANES]
        for k in range(1, NB):
            bias_sum = bias_sum + pre[:, k * LANES : (k + 1) * LANES]
        return prod, bias_sum

    def lam_copy(j):
        return copy(LSEND.at[pl.ds(j * NB, NB)], LR.at[pl.ds(1 + j * NB, NB)], lam_s.at[j], lam_r.at[j], d - 1)

    def backward_start():
        for c in range(chunks):
            adj_in(c).wait()

        def layer(i, _):
            def block(j, _):
                backward_block(G.at[i % 2], MOST - 1 - i, j, into(G.at[(i + 1) % 2], 1), False)
                return 0
            lax.fori_loop(0, blocks, block, 0, unroll=True)
            return 0

        lax.fori_loop(0, MOST - 1, layer, 0)

        def block(j, _):
            backward_block(G.at[(MOST - 1) % 2], 0, j, into(LSEND, 0), False)

            @pl.when(has_prev)
            def _():
                lam_copy(j).start()
            return 0

        lax.fori_loop(0, blocks, block, 0)

    def full_ready():
        @pl.when(has_next)
        def _():
            for j in range(blocks):
                lam_copy(j).wait_recv()

        @pl.when(ends)
        def _():
            each_chunk(lambda c: adj_end(c).wait())

        for c in range(chunks):
            G[0, c + 1] = LR[c + 1]
        GB[MOST] = jnp.zeros((C, C), F)
        PK[...] = jnp.zeros_like(PK)

    def full_layers(first_layer, end_layer):
        def layer(i, _):
            slot = MOST - 1 - i
            factor = jnp.where(slot < n, 1.0 / MOST, 0.0)
            start = (jnp.zeros((2 * C, 2 * C), F), jnp.zeros((C, LANES), F))

            def block(j, sums):
                prod, bias_sum = backward_block(G.at[i % 2], slot, j, into(G.at[(i + 1) % 2], 1), True)
                return sums[0] + prod, sums[1] + bias_sum
            prod, bias_sum = lax.fori_loop(0, blocks, block, start, unroll=True)
            GB[slot] = -factor * (prod[:C, :C] + (prod[:C, C:] + prod[C:, :C]))
            column = jnp.sum(bias_sum, axis=1, keepdims=True)
            GB[MOST, pl.ds(slot, 1), :] = -factor * row_of(column, eye)
            return 0

        lax.fori_loop(first_layer, end_layer, layer, 0)

    side = LANES // C

    def share_grads():
        for g in range(MOST // side):
            PK[g * C : (g + 1) * C] = jnp.concatenate([GB[g * side + k] for k in range(side)], axis=1)
        PK[MOST // side * C :, :C] = GB[MOST, :MOST]
        GR[image] = PK[...]
        for o in range(1, images):
            grad_copy(o).start()
        for c in range(chunks):
            a_out[:, c * LANES : (c + 1) * LANES] = G[0, c + 1]

    def grad_copy(o):
        return copy(PK, GR.at[image], grad_s.at[o - 1], grad_r.at[o - 1], d, (image + o) % images)

    def turn(order, _):
        here = jnp.logical_and(odd, order == jnp.where(chip < early, 0, 3))

        @pl.when(jnp.logical_and(here, chip < chips - 1))
        def _():
            relay(True)

        @pl.when(jnp.logical_and(here, chip == chips - 1))
        def _():
            relay(False)

        @pl.when(order == 1)
        def _():
            backward_start()

        @pl.when(order == jnp.where(ahead > 0, 2, 4))
        def _():
            full_ready()

        @pl.when(jnp.logical_or(order == 2, order == 4))
        def _():
            full_layers(jnp.where(order == 2, 0, ahead), jnp.where(order == 2, ahead, MOST))

        @pl.when(order == jnp.where(ahead == MOST, 2, 4))
        def _():
            share_grads()
        return 0

    lax.fori_loop(0, 5, turn, 0)
    for o in range(1, images):
        grad_copy(o).wait_recv()
    total = GR[0]
    for b in range(1, images):
        total = total + GR[b]
    for i in range(MOST):
        row, lane = i // side * C, i % side * C
        gw_out[i] = total[row : row + C, lane : lane + C]
    gb_out[...] = total[MOST // side * C :, :C]

    @pl.when(even)
    def _():
        def take(c, _):
            one_copy(c).wait_recv()
            s_out[:, at(c)] = S[c]
            return 0
        lax.fori_loop(0, chunks, take, 0)

    for o in range(1, images):
        grad_copy(o).wait_send()

    @pl.when(has_next)
    def _():
        for j in range(blocks):
            push_copy(j).wait_send()

    @pl.when(has_prev)
    def _():
        for j in range(blocks):
            lam_copy(j).wait_send()

    @pl.when(even)
    def _():
        weight_copy.wait_send()
        bias_copy.wait_send()
        for j in range(blocks):
            tau_copy(j).wait_send()

    @pl.when(starts)
    def _():
        def sent(c, _):
            first_copy(c).wait_send()
            return 0
        lax.fori_loop(0, chunks, sent, 0)

    @pl.when(odd)
    def _():
        def sent(c, _):
            one_copy(c).wait_send()
            return 0
        lax.fori_loop(0, chunks, sent, 0)

    @pl.when(up2)
    def _():
        def sent(c, _):
            two_copy(c).wait_send()
            return 0
        lax.fori_loop(0, chunks, sent, 0)


def write_out(*refs):
    sems = refs[8]
    copies = [pltpu.make_async_copy(refs[i], refs[i + 4], sems.at[i]) for i in range(4)]
    for one in copies:
        one.start()
    for one in copies:
        one.wait()


def body(cpoint_guess, adjoint_guess, weights, biases, diffusion, section_len):
    pixels = cpoint_guess.shape[-1]
    images = lax.axis_size("batch")
    chunks = pixels // LANES
    blocks = 2
    vmem = pl.BlockSpec(memory_space=pltpu.VMEM)
    image_shape = jax.ShapeDtypeStruct((C, pixels), F)
    dma = pltpu.SemaphoreType.DMA

    def stack(*lead):
        return pltpu.VMEM(lead + (C, LANES), F)

    outs = pl.pallas_call(
        kernel,
        out_shape=(
            image_shape, image_shape,
            jax.ShapeDtypeStruct((MOST, C, C), F), jax.ShapeDtypeStruct((MOST, C), F),
        ),
        in_specs=[pl.BlockSpec(memory_space=pltpu.HBM)] * 6,
        out_specs=(vmem,) * 4,
        scratch_shapes=[
            stack(MOST + 1, chunks + 2), stack(MOST, chunks), stack(MOST + 1, chunks + 2), stack(2, chunks + 2),
            stack(chunks + 2), stack(chunks), stack(chunks), stack(chunks), stack(chunks + 1), stack(chunks + 1),
            pltpu.VMEM((MOST, C, 3 * C), BF), pltpu.VMEM((MOST, C, 3 * C), BF), stack(MOST), stack(MOST),
            pltpu.VMEM((C, C), F), pltpu.VMEM((MOST, C), F),
            stack(C), stack(C), stack(C), stack(C), stack(4),
            pltpu.VMEM((MOST + 1, C, C), F),
            pltpu.VMEM((MOST // 4 * C + MOST, LANES), F), pltpu.VMEM((images, MOST // 4 * C + MOST, LANES), F),
            dma((blocks,)), dma((blocks,)), dma((blocks,)), dma((blocks,)), dma((blocks,)), dma((blocks,)),
            dma((2,)), dma((2,)), dma((chunks,)), dma((chunks,)), dma((chunks,)),
            dma((images - 1,)), dma((images - 1,)),
            pltpu.VMEM((MOST, C, C), F), pltpu.VMEM((MOST, C), F), pltpu.VMEM((1, C), F),
            pltpu.SMEM(section_len.shape, jnp.int32), dma((4,)), dma((chunks,)), dma((chunks,)), dma((chunks,)),
        ],
        compiler_params=pltpu.CompilerParams(
            collective_id=0, has_side_effects=True, vmem_limit_bytes=32 << 20
        ),
        name="mgrit_cycle",
    )(
        *(
            pltpu.with_memory_space_constraint(x, pltpu.HBM)
            for x in (
                cpoint_guess.reshape(C, pixels), adjoint_guess.reshape(C, pixels), weights, biases,
                diffusion.reshape(1, C), section_len,
            )
        )
    )
    states_out, adjoint_out, grad_weights, grad_biases = pl.pallas_call(
        write_out,
        out_shape=tuple(jax.ShapeDtypeStruct(o.shape, o.dtype) for o in outs),
        in_specs=[vmem] * 4,
        out_specs=(pl.BlockSpec(memory_space=pltpu.HBM),) * 4,
        scratch_shapes=[dma((4,))],
        compiler_params=pltpu.CompilerParams(vmem_limit_bytes=8 << 20),
        name="write_out",
    )(*outs)
    return states_out[None, None], adjoint_out[None, None], grad_weights, grad_biases


def solution(mesh):
    placed = (
        P("depth", "batch", None, None), P("depth", "batch", None, None), P("depth", None, None),
        P("depth", None), P(), P(),
    )
    return jax.shard_map(
        body, mesh=mesh, in_specs=placed,
        out_specs=(
            P("depth", "batch", None, None), P("depth", "batch", None, None), P("depth", None, None),
            P("depth", None),
        ),
        check_vma=False,
    )
```

```python
import jax
import jax.numpy as jnp
from jax import lax
from jax.experimental import pallas as pl
from jax.experimental.pallas import tpu as pltpu
from jax.sharding import PartitionSpec as P

MOST = 8
C = 32
LANES = 128
F = jnp.float32
BF = jnp.bfloat16
NT = (((1,), (1,)), ((), ()))


def split2(x):
    hi = x.astype(BF)
    return hi, (x - hi.astype(F)).astype(BF)


def dot3(packed, x):
    hi, lo = split2(x)
    return jnp.dot(packed, jnp.concatenate([hi, lo, hi], axis=0), preferred_element_type=F)


def pack3(matrix):
    hi, lo = split2(matrix)
    return jnp.concatenate([hi, hi, lo], axis=1)


def lane_masks():
    lane = lax.broadcasted_iota(jnp.int32, (C, LANES), 1)
    return lane < 64, lane % 64 == 0, lane % 64 == 63


def beside(x, masks):
    zero = jnp.zeros_like(x)
    return jnp.where(masks[1], zero, pltpu.roll(x, 1, 1)) + jnp.where(masks[2], zero, pltpu.roll(x, 127, 1))


def chunk_laps(chunks, count, masks):
    turned = [pltpu.roll(x, 64, 1) for x in chunks]
    laps = []
    for k in range(1, count + 1):
        above_below = turned[k] + jnp.where(masks[0], turned[k - 1], turned[k + 1])
        laps.append((above_below + beside(chunks[k], masks)) - 4.0 * chunks[k])
    return laps


def column_of(row, eye):
    return jnp.sum(jnp.where(eye, jnp.broadcast_to(row, (C, C)), 0.0), axis=1, keepdims=True)


def row_of(column, eye):
    return jnp.sum(jnp.where(eye, jnp.broadcast_to(column, (C, C)), 0.0), axis=0, keepdims=True)


def spread(matrix, out_ref):
    for k in range(C):
        out_ref[k] = jnp.broadcast_to(matrix[:, k : k + 1], (C, LANES))


def mix(spread_ref, x, first):
    sums = [first, None]
    for k in range(C):
        term = spread_ref[k] * jnp.broadcast_to(x[k : k + 1, :], (C, LANES))
        sums[k % 2] = term if sums[k % 2] is None else sums[k % 2] + term
    return sums[0] + sums[1]


def kernel(
    guess_hbm, adj_hbm, w_hbm, b_hbm, d_hbm, n_hbm,
    s_out, a_out, gw_out, gb_out,
    A, T, H, G, LR, LSEND, S, S2, TAU, TAU_A,
    WC, WT, BB, FD, WP, BP, SPA, SPAT, SPB, SPBT, CB, GB, PK, GR,
    push_s, push_r, lam_s, lam_r, tau_s, tau_r, par_s, par_r, one_s, one_r, two_s, st_r, grad_s, grad_r,
    guess_ref, adj_ref, w_ref, b_ref, d_ref, n_ref, in_s,
):
    sections, images = lax.axis_size("depth"), lax.axis_size("batch")
    d, image = lax.axis_index("depth"), lax.axis_index("batch")
    chunks = guess_ref.shape[1] // LANES
    blocks = 2
    NB = chunks // blocks
    halo = MOST // 2
    cut = (3 * chunks) // 8
    parts = ((0, cut), (cut, chunks))
    core, chip, chips = d % 2, d // 2, sections // 2
    has_prev, has_next = d > 0, d < sections - 1
    even = core == 0
    odd = core == 1
    early = chips // 4
    ahead = jnp.where(even, MOST, jnp.where(chip >= (12 * chips) // 16, MOST, jnp.clip(2 * (chip - (9 * chips) // 16), 0, MOST)))
    masks = lane_masks()
    eye = lax.broadcasted_iota(jnp.int32, (C, C), 0) == lax.broadcasted_iota(jnp.int32, (C, C), 1)

    def at(c):
        return pl.ds(pl.multiple_of(c * LANES, LANES), LANES)

    def copy(src, dst, ssem, rsem, depth_to, image_to=None):
        return pltpu.make_async_remote_copy(
            src_ref=src, dst_ref=dst, send_sem=ssem, recv_sem=rsem,
            device_id=(depth_to, image if image_to is None else image_to),
            device_id_type=pl.DeviceIdType.MESH,
        )

    def brought(src, dst, sem):
        return pltpu.make_async_copy(src, dst, sem)

    small = [
        brought(src, dst, in_s.at[i])
        for i, (src, dst) in enumerate(((n_hbm, n_ref), (w_hbm, w_ref), (b_hbm, b_ref), (d_hbm, d_ref)))
    ]
    guess_in, adj_in = brought(guess_hbm, guess_ref, in_s.at[4]), brought(adj_hbm, adj_ref, in_s.at[5])
    for part in small:
        part.start()
    guess_in.start()
    adj_in.start()

    barrier = pltpu.get_barrier_semaphore()

    def greet(cond, depth_to, image_to):
        @pl.when(cond)
        def _():
            pl.semaphore_signal(barrier, inc=1, device_id=(depth_to, image_to), device_id_type=pl.DeviceIdType.MESH)

    up2, down2 = jnp.logical_and(odd, chip < chips - 1), jnp.logical_and(odd, chip > 0)
    greet(has_prev, d - 1, image)
    greet(has_next, d + 1, image)
    greet(up2, d + 2, image)
    greet(down2, d - 2, image)
    for o in range(1, images):
        pl.semaphore_signal(
            barrier, inc=1, device_id=(d, (image + o) % images), device_id_type=pl.DeviceIdType.MESH
        )
    partners = (
        has_prev.astype(jnp.int32) + has_next.astype(jnp.int32) + up2.astype(jnp.int32)
        + down2.astype(jnp.int32) + (images - 1)
    )

    starts, ends = jnp.logical_not(has_prev), jnp.logical_not(has_next)

    zero_chunk = jnp.zeros((C, LANES), F)
    for l in range(MOST + 1):
        for ref in (A, H):
            ref[l, 0] = zero_chunk
            ref[l, chunks + 1] = zero_chunk
    for ref in (G.at[0], G.at[1], LR):
        ref[0] = zero_chunk
        ref[chunks + 1] = zero_chunk

    for part in small:
        part.wait()
    n = n_ref[d]
    diff_col = column_of(d_ref[...], eye)
    diff = jnp.broadcast_to(diff_col, (C, LANES))

    def prepare(i, _):
        factor = jnp.where(i < n, 1.0 / MOST, 0.0)
        WC[i] = pack3(w_ref[i])
        WT[i] = pack3(w_ref[i].T * factor)
        BB[i] = jnp.broadcast_to(column_of(b_ref[pl.ds(i, 1), :], eye), (C, LANES))
        FD[i] = diff * factor
        return 0

    lax.fori_loop(0, MOST, prepare, 0, unroll=True)
    guess_in.wait()
    for c in range(chunks):
        H[0, c + 1] = guess_ref[:, c * LANES : (c + 1) * LANES]

    def forward_tile(src, i, lo, count, dst, keep, open_end):
        u = [src[lo + k] for k in range(count + 1)] + [zero_chunk if open_end else src[lo + count + 1]]
        laps = chunk_laps(u, count, masks)
        bias = jnp.concatenate([BB[i]] * count, axis=1)
        act = jnp.tanh(dot3(WC[i], jnp.concatenate(u[1:-1], axis=1)) + bias)
        mixed = dot3(WT[i], act)
        fd = FD[i]
        for k in range(count):
            dst[lo + k + 1] = u[k + 1] + fd * laps[k] - mixed[:, k * LANES : (k + 1) * LANES]
            if keep is not None:
                keep[lo + k] = act[:, k * LANES : (k + 1) * LANES]

    def into(ref, shift):
        def store(c, value):
            ref[c + shift] = value
        return store

    def sweep(stack, keeps, lo, count, open_end):
        def layer(i, _):
            keep = None if keeps is None else keeps.at[i]
            forward_tile(stack.at[i], i, lo, count, stack.at[i + 1], keep, open_end)
            return 0
        lax.fori_loop(0, MOST, layer, 0)

    upper = cut + halo

    def push_copy(j):
        part = pl.ds(1, upper) if j == 0 else pl.ds(1 + upper, chunks - upper)
        return copy(H.at[MOST, part], A.at[0, part], push_s.at[j], push_r.at[j], d + 1)

    def push(j):
        @pl.when(has_next)
        def _():
            push_copy(j).start()

    first = min(upper + halo, chunks)
    sweep(H, None, 0, first, first < chunks)
    pl.semaphore_wait(barrier, partners)
    push(0)
    sweep(H, None, upper, chunks - upper, False)
    push(1)

    weight_copy = copy(w_ref.at[0], WP, par_s.at[0], par_r.at[0], d + 1)
    bias_copy = copy(b_ref, BP, par_s.at[1], par_r.at[1], d + 1)

    def first_copy(c):
        return copy(guess_ref.at[:, at(c)], S.at[c], two_s.at[0], st_r.at[c], d + 1)

    @pl.when(even)
    def _():
        weight_copy.start()
        bias_copy.start()

    @pl.when(starts)
    def _():
        def send(c, _):
            first_copy(c).start()
            return 0
        lax.fori_loop(0, chunks, send, 0)

    @pl.when(odd)
    def _():
        coarse_b = n.astype(F) / MOST
        spread(w_ref[0], SPB)
        spread(w_ref[0].T * -coarse_b, SPBT)
        CB[2] = BB[0]
        CB[3] = diff * coarse_b
        weight_copy.wait_recv()
        bias_copy.wait_recv()
        coarse_a = n_ref[d - core].astype(F) / MOST
        spread(WP[...], SPA)
        spread(WP[...].T * -coarse_a, SPAT)
        CB[0] = jnp.broadcast_to(column_of(BP[0:1, :], eye), (C, LANES))
        CB[1] = diff * coarse_a

    layers = n.astype(F)

    def tau_of(c):
        start = A[0, c + 1]
        return A[MOST, c + 1] - (start + layers * (A[1, c + 1] - start))

    def tau_copy(j):
        part = pl.ds(0, cut) if j == 0 else pl.ds(cut, chunks + 1 - cut)
        return copy(TAU.at[part], TAU_A.at[part], tau_s.at[j], tau_r.at[j], d + 1)

    @pl.when(starts)
    def _():
        for c in range(chunks):
            A[0, c + 1] = guess_ref[:, c * LANES : (c + 1) * LANES]

    def push_arrived(j):
        @pl.when(has_prev)
        def _():
            push_copy(j).wait_recv()

    @pl.when(even)
    def _():
        for j, (lo, hi) in enumerate(parts):
            push_arrived(j)
            if j == 0:
                sweep(A, T, 0, upper, True)
            else:
                sweep(A, T, cut, chunks - cut, False)
            before = zero_chunk if j == 0 else tau_of(cut - 1)
            for c in range(lo, hi):
                here = tau_of(c)
                TAU[c] = jnp.where(masks[0], here, before)
                before = here
            if j == 1:
                TAU[chunks] = jnp.where(masks[0], 0.0, before)
            tau_copy(j).start()

    @pl.when(odd)
    def _():
        for j in range(2):
            push_arrived(j)
        sweep(A, T, 0, chunks, False)
        for c in range(chunks):
            TAU[c] = tau_of(c)

    hand = (0, cut, chunks - chunks // 8, chunks)

    def one_copy(p):
        part = pl.ds(hand[p], hand[p + 1] - hand[p])
        return copy(S.at[part], S.at[part], one_s.at[p], one_r.at[p], d - 1)

    def two_copy(c):
        return copy(S2.at[c], S.at[c], two_s.at[0], st_r.at[c], d + 2)

    def relay(both):
        bias_a, fd_a, bias_b, fd_b = CB[0], CB[1], CB[2], CB[3]
        lower = masks[0]

        def step(c, carry, first=False, last=False):
            prev, one_prev = carry
            if last:
                now = zero_chunk
            else:
                two_copy(c).wait_recv()
                now = S[c]
            mid = jnp.where(lower, now, prev)
            lap = (pltpu.roll(prev + now, 64, 1) + beside(mid, masks)) - 4.0 * mid
            act = jnp.tanh(mix(SPA, mid, bias_a))
            one = mix(SPAT, act, mid + fd_a * lap + TAU_A[c])
            if first:
                one = jnp.where(lower, one, 0.0)
            if last:
                one = jnp.where(lower, 0.0, one)
            if not first:
                mid_one = jnp.where(lower, one_prev, one)
                if both:
                    lap_b = (pltpu.roll(one_prev + one, 64, 1) + beside(mid_one, masks)) - 4.0 * mid_one
                    act_b = jnp.tanh(mix(SPB, mid_one, bias_b))
                    S2[c - 1] = mix(SPBT, act_b, mid_one + fd_b * lap_b + TAU[c - 1])
                    two_copy(c - 1).start()
                s_out[:, at(c - 1)] = mid_one
            return now, one

        tau_copy(0).wait_recv()
        carry = step(0, (zero_chunk,) * 2, first=True)
        for p in range(3):
            if p == 1:
                tau_copy(1).wait_recv()
            carry = lax.fori_loop(max(1, hand[p]), hand[p + 1], step, carry)
            one_copy(p).start()
        step(chunks, carry, last=True)

    def backward_block(src, i, j, store, with_grads):
        g = [src[j * NB + k] for k in range(NB + 2)]
        laps = chunk_laps(g, NB, masks)
        act = jnp.concatenate([T[i, j * NB + k] for k in range(NB)], axis=1)
        g_hi, g_lo = split2(jnp.concatenate(g[1:-1], axis=1))
        pulled = jnp.dot(WC[i], jnp.concatenate([g_hi, g_lo, g_hi], axis=0), preferred_element_type=F)
        pre = (1.0 - act * act) * pulled
        p_hi, p_lo = split2(pre)
        back = jnp.dot(WT[i], jnp.concatenate([p_hi, p_lo, p_hi], axis=0), preferred_element_type=F)
        fd = FD[i]
        for k in range(NB):
            store(j * NB + k, g[k + 1] + fd * laps[k] - back[:, k * LANES : (k + 1) * LANES])
        if not with_grads:
            return None
        t_hi, t_lo = split2(act)
        u_hi, u_lo = split2(jnp.concatenate([A[i, j * NB + k + 1] for k in range(NB)], axis=1))
        left = jnp.concatenate(
            [jnp.concatenate([t_hi, p_hi], axis=1), jnp.concatenate([t_lo, p_lo], axis=1)], axis=0
        )
        right = jnp.concatenate(
            [jnp.concatenate([g_hi, u_hi], axis=1), jnp.concatenate([g_lo, u_lo], axis=1)], axis=0
        )
        prod = lax.dot_general(left, right, NT, preferred_element_type=F)
        bias_sum = pre[:, :LANES]
        for k in range(1, NB):
            bias_sum = bias_sum + pre[:, k * LANES : (k + 1) * LANES]
        return prod, bias_sum

    def lam_copy(j):
        return copy(LSEND.at[pl.ds(j * NB, NB)], LR.at[pl.ds(1 + j * NB, NB)], lam_s.at[j], lam_r.at[j], d - 1)

    def backward_start():
        adj_in.wait()
        for c in range(chunks):
            G[0, c + 1] = adj_ref[:, c * LANES : (c + 1) * LANES]

        def layer(i, _):
            def block(j, _):
                backward_block(G.at[i % 2], MOST - 1 - i, j, into(G.at[(i + 1) % 2], 1), False)
                return 0
            lax.fori_loop(0, blocks, block, 0, unroll=True)
            return 0

        lax.fori_loop(0, MOST - 1, layer, 0)

        def block(j, _):
            backward_block(G.at[(MOST - 1) % 2], 0, j, into(LSEND, 0), False)

            @pl.when(has_prev)
            def _():
                lam_copy(j).start()
            return 0

        lax.fori_loop(0, blocks, block, 0)

    def full_ready():
        @pl.when(has_next)
        def _():
            for j in range(blocks):
                lam_copy(j).wait_recv()

        @pl.when(ends)
        def _():
            for c in range(chunks):
                LR[c + 1] = adj_ref[:, c * LANES : (c + 1) * LANES]

        for c in range(chunks):
            G[0, c + 1] = LR[c + 1]
        GB[MOST] = jnp.zeros((C, C), F)
        PK[...] = jnp.zeros_like(PK)

    def full_layers(first_layer, end_layer):
        def layer(i, _):
            slot = MOST - 1 - i
            factor = jnp.where(slot < n, 1.0 / MOST, 0.0)
            start = (jnp.zeros((2 * C, 2 * C), F), jnp.zeros((C, LANES), F))

            def block(j, sums):
                prod, bias_sum = backward_block(G.at[i % 2], slot, j, into(G.at[(i + 1) % 2], 1), True)
                return sums[0] + prod, sums[1] + bias_sum
            prod, bias_sum = lax.fori_loop(0, blocks, block, start, unroll=True)
            GB[slot] = -factor * (prod[:C, :C] + (prod[:C, C:] + prod[C:, :C]))
            column = jnp.sum(bias_sum, axis=1, keepdims=True)
            GB[MOST, pl.ds(slot, 1), :] = -factor * row_of(column, eye)
            return 0

        lax.fori_loop(first_layer, end_layer, layer, 0)

    side = LANES // C

    def share_grads():
        for g in range(MOST // side):
            PK[g * C : (g + 1) * C] = jnp.concatenate([GB[g * side + k] for k in range(side)], axis=1)
        PK[MOST // side * C :, :C] = GB[MOST, :MOST]
        GR[image] = PK[...]
        for o in range(1, images):
            grad_copy(o).start()
        for c in range(chunks):
            a_out[:, c * LANES : (c + 1) * LANES] = G[0, c + 1]

    def grad_copy(o):
        return copy(PK, GR.at[image], grad_s.at[o - 1], grad_r.at[o - 1], d, (image + o) % images)

    def turn(order, _):
        here = jnp.logical_and(odd, order == jnp.where(chip < early, 0, 3))

        @pl.when(jnp.logical_and(here, chip < chips - 1))
        def _():
            relay(True)

        @pl.when(jnp.logical_and(here, chip == chips - 1))
        def _():
            relay(False)

        @pl.when(order == 1)
        def _():
            backward_start()

        @pl.when(order == jnp.where(ahead > 0, 2, 4))
        def _():
            full_ready()

        @pl.when(jnp.logical_or(order == 2, order == 4))
        def _():
            full_layers(jnp.where(order == 2, 0, ahead), jnp.where(order == 2, ahead, MOST))

        @pl.when(order == jnp.where(ahead == MOST, 2, 4))
        def _():
            share_grads()
        return 0

    lax.fori_loop(0, 5, turn, 0)
    for o in range(1, images):
        grad_copy(o).wait_recv()
    total = GR[0]
    for b in range(1, images):
        total = total + GR[b]
    for i in range(MOST):
        row, lane = i // side * C, i % side * C
        gw_out[i] = total[row : row + C, lane : lane + C]
    gb_out[...] = total[MOST // side * C :, :C]

    @pl.when(even)
    def _():
        for p in range(3):
            one_copy(p).wait_recv()
            for c in range(hand[p], hand[p + 1]):
                s_out[:, c * LANES : (c + 1) * LANES] = S[c]

    for o in range(1, images):
        grad_copy(o).wait_send()

    @pl.when(has_next)
    def _():
        for j in range(blocks):
            push_copy(j).wait_send()

    @pl.when(has_prev)
    def _():
        for j in range(blocks):
            lam_copy(j).wait_send()

    @pl.when(even)
    def _():
        weight_copy.wait_send()
        bias_copy.wait_send()
        for j in range(blocks):
            tau_copy(j).wait_send()

    @pl.when(odd)
    def _():
        for p in range(3):
            one_copy(p).wait_send()

    @pl.when(jnp.logical_or(starts, up2))
    def _():
        part = pl.ds(0, chunks)
        copy(S2.at[part], S.at[part], two_s.at[0], st_r.at[0], d + 1).wait_send()


def write_out(*refs):
    sems = refs[8]
    copies = [pltpu.make_async_copy(refs[i], refs[i + 4], sems.at[i]) for i in range(4)]
    for one in copies:
        one.start()
    for one in copies:
        one.wait()


def body(cpoint_guess, adjoint_guess, weights, biases, diffusion, section_len):
    pixels = cpoint_guess.shape[-1]
    images = lax.axis_size("batch")
    chunks = pixels // LANES
    blocks = 2
    vmem = pl.BlockSpec(memory_space=pltpu.VMEM)
    image_shape = jax.ShapeDtypeStruct((C, pixels), F)
    dma = pltpu.SemaphoreType.DMA

    def stack(*lead):
        return pltpu.VMEM(lead + (C, LANES), F)

    outs = pl.pallas_call(
        kernel,
        out_shape=(
            image_shape, image_shape,
            jax.ShapeDtypeStruct((MOST, C, C), F), jax.ShapeDtypeStruct((MOST, C), F),
        ),
        in_specs=[pl.BlockSpec(memory_space=pltpu.HBM)] * 6,
        out_specs=(vmem,) * 4,
        scratch_shapes=[
            stack(MOST + 1, chunks + 2), stack(MOST, chunks), stack(MOST + 1, chunks + 2), stack(2, chunks + 2),
            stack(chunks + 2), stack(chunks), stack(chunks), stack(chunks), stack(chunks + 1), stack(chunks + 1),
            pltpu.VMEM((MOST, C, 3 * C), BF), pltpu.VMEM((MOST, C, 3 * C), BF), stack(MOST), stack(MOST),
            pltpu.VMEM((C, C), F), pltpu.VMEM((MOST, C), F),
            stack(C), stack(C), stack(C), stack(C), stack(4),
            pltpu.VMEM((MOST + 1, C, C), F),
            pltpu.VMEM((MOST // 4 * C + MOST, LANES), F), pltpu.VMEM((images, MOST // 4 * C + MOST, LANES), F),
            dma((blocks,)), dma((blocks,)), dma((blocks,)), dma((blocks,)), dma((blocks,)), dma((blocks,)),
            dma((2,)), dma((2,)), dma((3,)), dma((3,)), dma((1,)), dma((chunks,)),
            dma((images - 1,)), dma((images - 1,)),
            pltpu.VMEM((C, pixels), F), pltpu.VMEM((C, pixels), F),
            pltpu.VMEM((MOST, C, C), F), pltpu.VMEM((MOST, C), F), pltpu.VMEM((1, C), F),
            pltpu.SMEM(section_len.shape, jnp.int32), dma((6,)),
        ],
        compiler_params=pltpu.CompilerParams(
            collective_id=0, has_side_effects=True, vmem_limit_bytes=32 << 20
        ),
        name="mgrit_cycle",
    )(
        *(
            pltpu.with_memory_space_constraint(x, pltpu.HBM)
            for x in (
                cpoint_guess.reshape(C, pixels), adjoint_guess.reshape(C, pixels), weights, biases,
                diffusion.reshape(1, C), section_len,
            )
        )
    )
    states_out, adjoint_out, grad_weights, grad_biases = pl.pallas_call(
        write_out,
        out_shape=tuple(jax.ShapeDtypeStruct(o.shape, o.dtype) for o in outs),
        in_specs=[vmem] * 4,
        out_specs=(pl.BlockSpec(memory_space=pltpu.HBM),) * 4,
        scratch_shapes=[dma((4,))],
        compiler_params=pltpu.CompilerParams(vmem_limit_bytes=8 << 20),
        name="write_out",
    )(*outs)
    return states_out[None, None], adjoint_out[None, None], grad_weights, grad_biases


def solution(mesh):
    placed = (
        P("depth", "batch", None, None), P("depth", "batch", None, None), P("depth", None, None),
        P("depth", None), P(), P(),
    )
    return jax.shard_map(
        body, mesh=mesh, in_specs=placed,
        out_specs=(
            P("depth", "batch", None, None), P("depth", "batch", None, None), P("depth", None, None),
            P("depth", None),
        ),
        check_vma=False,
    )
```

```python
import jax
import jax.numpy as jnp
from jax import lax
from jax.experimental import pallas as pl
from jax.experimental.pallas import tpu as pltpu
from jax.sharding import PartitionSpec as P

MOST = 8
C = 32
LANES = 128
F = jnp.float32
BF = jnp.bfloat16
NT = (((1,), (1,)), ((), ()))


def split2(x):
    hi = x.astype(BF)
    return hi, (x - hi.astype(F)).astype(BF)


def dot3(packed, x):
    hi, lo = split2(x)
    return jnp.dot(packed, jnp.concatenate([hi, lo, hi], axis=0), preferred_element_type=F)


def pack3(matrix):
    hi, lo = split2(matrix)
    return jnp.concatenate([hi, hi, lo], axis=1)


def lane_masks():
    lane = lax.broadcasted_iota(jnp.int32, (C, LANES), 1)
    return lane < 64, lane % 64 == 0, lane % 64 == 63


def beside(x, masks):
    zero = jnp.zeros_like(x)
    return jnp.where(masks[1], zero, pltpu.roll(x, 1, 1)) + jnp.where(masks[2], zero, pltpu.roll(x, 127, 1))


def chunk_laps(chunks, count, masks):
    turned = [pltpu.roll(x, 64, 1) for x in chunks]
    laps = []
    for k in range(1, count + 1):
        above_below = turned[k] + jnp.where(masks[0], turned[k - 1], turned[k + 1])
        laps.append((above_below + beside(chunks[k], masks)) - 4.0 * chunks[k])
    return laps


def column_of(row, eye):
    return jnp.sum(jnp.where(eye, jnp.broadcast_to(row, (C, C)), 0.0), axis=1, keepdims=True)


def row_of(column, eye):
    return jnp.sum(jnp.where(eye, jnp.broadcast_to(column, (C, C)), 0.0), axis=0, keepdims=True)


def spread(matrix, out_ref):
    for k in range(C):
        out_ref[k] = jnp.broadcast_to(matrix[:, k : k + 1], (C, LANES))


def mix(spread_ref, x, first):
    sums = [first, None]
    for k in range(C):
        term = spread_ref[k] * jnp.broadcast_to(x[k : k + 1, :], (C, LANES))
        sums[k % 2] = term if sums[k % 2] is None else sums[k % 2] + term
    return sums[0] + sums[1]


def kernel(
    guess_hbm, adj_hbm, w_hbm, b_hbm, d_hbm, n_hbm,
    s_out, a_out, gw_out, gb_out,
    A, T, H, G, LR, LSEND, S, S2, TAU, TAU_A,
    WC, WT, BB, FD, SPA, SPAT, SPB, SPBT, CB, GB, PK, GR,
    push_s, push_r, lam_s, lam_r, tau_s, tau_r, par_s, par_r, one_s, one_r, two_s, st_r, grad_s, grad_r,
    guess_ref, adj_ref, w_ref, b_ref, d_ref, n_ref, in_s,
):
    sections, images = lax.axis_size("depth"), lax.axis_size("batch")
    d, image = lax.axis_index("depth"), lax.axis_index("batch")
    chunks = guess_ref.shape[1] // LANES
    blocks = 2
    NB = chunks // blocks
    halo = MOST // 2
    cut = (3 * chunks) // 8
    parts = ((0, cut), (cut, chunks))
    core, chip, chips = d % 2, d // 2, sections // 2
    has_prev, has_next = d > 0, d < sections - 1
    even = core == 0
    odd = core == 1
    early = chips // 4 + 1
    ahead = jnp.where(even, MOST, jnp.where(chip >= (12 * chips) // 16, MOST, jnp.clip(2 * (chip - (9 * chips) // 16), 0, MOST)))
    masks = lane_masks()
    eye = lax.broadcasted_iota(jnp.int32, (C, C), 0) == lax.broadcasted_iota(jnp.int32, (C, C), 1)

    def at(c):
        return pl.ds(pl.multiple_of(c * LANES, LANES), LANES)

    def copy(src, dst, ssem, rsem, depth_to, image_to=None):
        return pltpu.make_async_remote_copy(
            src_ref=src, dst_ref=dst, send_sem=ssem, recv_sem=rsem,
            device_id=(depth_to, image if image_to is None else image_to),
            device_id_type=pl.DeviceIdType.MESH,
        )

    def brought(src, dst, sem):
        return pltpu.make_async_copy(src, dst, sem)

    small = [
        brought(src, dst, in_s.at[i])
        for i, (src, dst) in enumerate(((n_hbm, n_ref), (w_hbm, w_ref), (b_hbm, b_ref), (d_hbm, d_ref)))
    ]
    guess_in, adj_in = brought(guess_hbm, guess_ref, in_s.at[4]), brought(adj_hbm, adj_ref, in_s.at[5])
    for part in small:
        part.start()
    guess_in.start()
    adj_in.start()

    barrier = pltpu.get_barrier_semaphore()

    def greet(cond, depth_to, image_to):
        @pl.when(cond)
        def _():
            pl.semaphore_signal(barrier, inc=1, device_id=(depth_to, image_to), device_id_type=pl.DeviceIdType.MESH)

    up2, down2 = jnp.logical_and(odd, chip < chips - 1), jnp.logical_and(odd, chip > 0)
    greet(has_prev, d - 1, image)
    greet(has_next, d + 1, image)
    greet(up2, d + 2, image)
    greet(down2, d - 2, image)
    for o in range(1, images):
        pl.semaphore_signal(
            barrier, inc=1, device_id=(d, (image + o) % images), device_id_type=pl.DeviceIdType.MESH
        )
    partners = (
        has_prev.astype(jnp.int32) + has_next.astype(jnp.int32) + up2.astype(jnp.int32)
        + down2.astype(jnp.int32) + (images - 1)
    )

    starts, ends = jnp.logical_not(has_prev), jnp.logical_not(has_next)

    zero_chunk = jnp.zeros((C, LANES), F)
    for l in range(MOST + 1):
        for ref in (A, H):
            ref[l, 0] = zero_chunk
            ref[l, chunks + 1] = zero_chunk
    for ref in (G.at[0], G.at[1], LR):
        ref[0] = zero_chunk
        ref[chunks + 1] = zero_chunk

    for part in small:
        part.wait()
    n = n_ref[d]
    diff_col = column_of(d_ref[...], eye)
    diff = jnp.broadcast_to(diff_col, (C, LANES))

    def prepare(i, _):
        factor = jnp.where(i < n, 1.0 / MOST, 0.0)
        WC[i] = pack3(w_ref[i])
        WT[i] = pack3(w_ref[i].T * factor)
        BB[i] = jnp.broadcast_to(column_of(b_ref[pl.ds(i, 1), :], eye), (C, LANES))
        FD[i] = diff * factor
        return 0

    lax.fori_loop(0, MOST, prepare, 0, unroll=True)
    guess_in.wait()
    for c in range(chunks):
        H[0, c + 1] = guess_ref[:, c * LANES : (c + 1) * LANES]

    def forward_tile(src, i, lo, count, dst, keep, open_end):
        u = [src[lo + k] for k in range(count + 1)] + [zero_chunk if open_end else src[lo + count + 1]]
        laps = chunk_laps(u, count, masks)
        bias = jnp.concatenate([BB[i]] * count, axis=1)
        act = jnp.tanh(dot3(WC[i], jnp.concatenate(u[1:-1], axis=1)) + bias)
        mixed = dot3(WT[i], act)
        fd = FD[i]
        for k in range(count):
            dst[lo + k + 1] = u[k + 1] + fd * laps[k] - mixed[:, k * LANES : (k + 1) * LANES]
            if keep is not None:
                keep[lo + k] = act[:, k * LANES : (k + 1) * LANES]

    def into(ref, shift):
        def store(c, value):
            ref[c + shift] = value
        return store

    def sweep(stack, keeps, lo, count, open_end):
        def layer(i, _):
            keep = None if keeps is None else keeps.at[i]
            forward_tile(stack.at[i], i, lo, wide, stack.at[i + 1], keep, open_end)
            return 0

        wide = count
        lax.fori_loop(0, MOST // 2, layer, 0)
        wide = count - halo // 2 if open_end else count
        lax.fori_loop(MOST // 2, MOST, layer, 0)

    upper = cut + halo

    def push_copy(j):
        part = pl.ds(1, upper) if j == 0 else pl.ds(1 + upper, chunks - upper)
        return copy(H.at[MOST, part], A.at[0, part], push_s.at[j], push_r.at[j], d + 1)

    def push(j):
        @pl.when(has_next)
        def _():
            push_copy(j).start()

    first = min(upper + halo, chunks)
    sweep(H, None, 0, first, first < chunks)
    pl.semaphore_wait(barrier, partners)
    push(0)
    sweep(H, None, upper, chunks - upper, False)
    push(1)

    part_copies = [
        copy(SPA, SPA, par_s.at[0], par_r.at[0], d + 1),
        copy(SPAT, SPAT, par_s.at[1], par_r.at[1], d + 1),
        copy(CB.at[0:2], CB.at[0:2], par_s.at[2], par_r.at[2], d + 1),
    ]

    def first_copy(c):
        return copy(guess_ref.at[:, at(c)], S.at[c], two_s.at[0], st_r.at[c], d + 1)

    @pl.when(starts)
    def _():
        def send(c, _):
            first_copy(c).start()
            return 0
        lax.fori_loop(0, chunks, send, 0)

    def propagator(matrix_ref, back_ref, row):
        spread(w_ref[0], matrix_ref)
        spread(w_ref[0].T * -coarse, back_ref)
        CB[row] = BB[0]
        CB[row + 1] = diff * coarse

    coarse = n.astype(F) / MOST

    @pl.when(even)
    def _():
        propagator(SPA, SPAT, 0)
        for part in part_copies:
            part.start()

    @pl.when(odd)
    def _():
        propagator(SPB, SPBT, 2)

    layers = n.astype(F)

    def tau_of(c):
        start = A[0, c + 1]
        return A[MOST, c + 1] - (start + layers * (A[1, c + 1] - start))

    def tau_copy(j):
        part = pl.ds(0, cut) if j == 0 else pl.ds(cut, chunks + 1 - cut)
        return copy(TAU.at[part], TAU_A.at[part], tau_s.at[j], tau_r.at[j], d + 1)

    @pl.when(starts)
    def _():
        for c in range(chunks):
            A[0, c + 1] = guess_ref[:, c * LANES : (c + 1) * LANES]

    def push_arrived(j):
        @pl.when(has_prev)
        def _():
            push_copy(j).wait_recv()

    @pl.when(even)
    def _():
        for j, (lo, hi) in enumerate(parts):
            push_arrived(j)
            if j == 0:
                sweep(A, T, 0, upper, True)
            else:
                sweep(A, T, cut, chunks - cut, False)
            before = zero_chunk if j == 0 else tau_of(cut - 1)
            for c in range(lo, hi):
                here = tau_of(c)
                TAU[c] = jnp.where(masks[0], here, before)
                before = here
            if j == 1:
                TAU[chunks] = jnp.where(masks[0], 0.0, before)
            tau_copy(j).start()

    @pl.when(odd)
    def _():
        for j in range(2):
            push_arrived(j)
        sweep(A, T, 0, chunks, False)
        for c in range(chunks):
            TAU[c] = tau_of(c)

    hand = (0, cut, chunks - chunks // 8, chunks)

    def one_copy(p):
        part = pl.ds(hand[p], hand[p + 1] - hand[p])
        return copy(S.at[part], S.at[part], one_s.at[p], one_r.at[p], d - 1)

    def two_copy(c):
        return copy(S2.at[c], S.at[c], two_s.at[0], st_r.at[c], d + 2)

    def relay(both):
        for part in part_copies:
            part.wait_recv()
        bias_a, fd_a, bias_b, fd_b = CB[0], CB[1], CB[2], CB[3]
        lower = masks[0]

        def step(c, carry, first=False, last=False):
            prev, one_prev = carry
            if last:
                now = zero_chunk
            else:
                two_copy(c).wait_recv()
                now = S[c]
            mid = jnp.where(lower, now, prev)
            lap = (pltpu.roll(prev + now, 64, 1) + beside(mid, masks)) - 4.0 * mid
            act = jnp.tanh(mix(SPA, mid, bias_a))
            one = mix(SPAT, act, mid + fd_a * lap + TAU_A[c])
            if first:
                one = jnp.where(lower, one, 0.0)
            if last:
                one = jnp.where(lower, 0.0, one)
            if not first:
                mid_one = jnp.where(lower, one_prev, one)
                if both:
                    lap_b = (pltpu.roll(one_prev + one, 64, 1) + beside(mid_one, masks)) - 4.0 * mid_one
                    act_b = jnp.tanh(mix(SPB, mid_one, bias_b))
                    S2[c - 1] = mix(SPBT, act_b, mid_one + fd_b * lap_b + TAU[c - 1])
                    two_copy(c - 1).start()
                s_out[:, at(c - 1)] = mid_one
            return now, one

        tau_copy(0).wait_recv()
        carry = step(0, (zero_chunk,) * 2, first=True)
        for p in range(3):
            if p == 1:
                tau_copy(1).wait_recv()
            carry = lax.fori_loop(max(1, hand[p]), hand[p + 1], step, carry)
            one_copy(p).start()
        step(chunks, carry, last=True)

    def backward_block(src, i, j, store, with_grads):
        g = [src[j * NB + k] for k in range(NB + 2)]
        laps = chunk_laps(g, NB, masks)
        act = jnp.concatenate([T[i, j * NB + k] for k in range(NB)], axis=1)
        g_hi, g_lo = split2(jnp.concatenate(g[1:-1], axis=1))
        pulled = jnp.dot(WC[i], jnp.concatenate([g_hi, g_lo, g_hi], axis=0), preferred_element_type=F)
        pre = (1.0 - act * act) * pulled
        p_hi, p_lo = split2(pre)
        back = jnp.dot(WT[i], jnp.concatenate([p_hi, p_lo, p_hi], axis=0), preferred_element_type=F)
        fd = FD[i]
        for k in range(NB):
            store(j * NB + k, g[k + 1] + fd * laps[k] - back[:, k * LANES : (k + 1) * LANES])
        if not with_grads:
            return None
        t_hi, t_lo = split2(act)
        u_hi, u_lo = split2(jnp.concatenate([A[i, j * NB + k + 1] for k in range(NB)], axis=1))
        left = jnp.concatenate(
            [jnp.concatenate([t_hi, p_hi], axis=1), jnp.concatenate([t_lo, p_lo], axis=1)], axis=0
        )
        right = jnp.concatenate(
            [jnp.concatenate([g_hi, u_hi], axis=1), jnp.concatenate([g_lo, u_lo], axis=1)], axis=0
        )
        prod = lax.dot_general(left, right, NT, preferred_element_type=F)
        bias_sum = pre[:, :LANES]
        for k in range(1, NB):
            bias_sum = bias_sum + pre[:, k * LANES : (k + 1) * LANES]
        return prod, bias_sum

    def lam_copy(j):
        return copy(LSEND.at[pl.ds(j * NB, NB)], LR.at[pl.ds(1 + j * NB, NB)], lam_s.at[j], lam_r.at[j], d - 1)

    def backward_start():
        adj_in.wait()
        for c in range(chunks):
            G[0, c + 1] = adj_ref[:, c * LANES : (c + 1) * LANES]

        def layer(i, _):
            def block(j, _):
                backward_block(G.at[i % 2], MOST - 1 - i, j, into(G.at[(i + 1) % 2], 1), False)
                return 0
            lax.fori_loop(0, blocks, block, 0, unroll=True)
            return 0

        lax.fori_loop(0, MOST - 1, layer, 0)

        def block(j, _):
            backward_block(G.at[(MOST - 1) % 2], 0, j, into(LSEND, 0), False)

            @pl.when(has_prev)
            def _():
                lam_copy(j).start()
            return 0

        lax.fori_loop(0, blocks, block, 0)

    def full_ready():
        @pl.when(has_next)
        def _():
            for j in range(blocks):
                lam_copy(j).wait_recv()

        @pl.when(ends)
        def _():
            for c in range(chunks):
                LR[c + 1] = adj_ref[:, c * LANES : (c + 1) * LANES]

        for c in range(chunks):
            G[0, c + 1] = LR[c + 1]
        GB[MOST] = jnp.zeros((C, C), F)
        PK[...] = jnp.zeros_like(PK)

    def full_layers(first_layer, end_layer):
        def layer(i, _):
            slot = MOST - 1 - i
            factor = jnp.where(slot < n, 1.0 / MOST, 0.0)
            start = (jnp.zeros((2 * C, 2 * C), F), jnp.zeros((C, LANES), F))

            def block(j, sums):
                prod, bias_sum = backward_block(G.at[i % 2], slot, j, into(G.at[(i + 1) % 2], 1), True)
                return sums[0] + prod, sums[1] + bias_sum
            prod, bias_sum = lax.fori_loop(0, blocks, block, start, unroll=True)
            GB[slot] = -factor * (prod[:C, :C] + (prod[:C, C:] + prod[C:, :C]))
            column = jnp.sum(bias_sum, axis=1, keepdims=True)
            GB[MOST, pl.ds(slot, 1), :] = -factor * row_of(column, eye)
            return 0

        lax.fori_loop(first_layer, end_layer, layer, 0)

    side = LANES // C

    def share_grads():
        for g in range(MOST // side):
            PK[g * C : (g + 1) * C] = jnp.concatenate([GB[g * side + k] for k in range(side)], axis=1)
        PK[MOST // side * C :, :C] = GB[MOST, :MOST]
        GR[image] = PK[...]
        for o in range(1, images):
            grad_copy(o).start()
        for c in range(chunks):
            a_out[:, c * LANES : (c + 1) * LANES] = G[0, c + 1]

    def grad_copy(o):
        return copy(PK, GR.at[image], grad_s.at[o - 1], grad_r.at[o - 1], d, (image + o) % images)

    def turn(order, _):
        here = jnp.logical_and(odd, order == jnp.where(chip < early, 0, 3))

        @pl.when(jnp.logical_and(here, chip < chips - 1))
        def _():
            relay(True)

        @pl.when(jnp.logical_and(here, chip == chips - 1))
        def _():
            relay(False)

        @pl.when(order == 1)
        def _():
            backward_start()

        @pl.when(order == jnp.where(ahead > 0, 2, 4))
        def _():
            full_ready()

        @pl.when(jnp.logical_or(order == 2, order == 4))
        def _():
            full_layers(jnp.where(order == 2, 0, ahead), jnp.where(order == 2, ahead, MOST))

        @pl.when(order == jnp.where(ahead == MOST, 2, 4))
        def _():
            share_grads()
        return 0

    lax.fori_loop(0, 5, turn, 0)
    for o in range(1, images):
        grad_copy(o).wait_recv()
    total = GR[0]
    for b in range(1, images):
        total = total + GR[b]
    for i in range(MOST):
        row, lane = i // side * C, i % side * C
        gw_out[i] = total[row : row + C, lane : lane + C]
    gb_out[...] = total[MOST // side * C :, :C]

    @pl.when(even)
    def _():
        for p in range(3):
            one_copy(p).wait_recv()
            for c in range(hand[p], hand[p + 1]):
                s_out[:, c * LANES : (c + 1) * LANES] = S[c]

    for o in range(1, images):
        grad_copy(o).wait_send()

    @pl.when(has_next)
    def _():
        for j in range(blocks):
            push_copy(j).wait_send()

    @pl.when(has_prev)
    def _():
        for j in range(blocks):
            lam_copy(j).wait_send()

    @pl.when(even)
    def _():
        for part in part_copies:
            part.wait_send()
        for j in range(blocks):
            tau_copy(j).wait_send()

    @pl.when(odd)
    def _():
        for p in range(3):
            one_copy(p).wait_send()

    @pl.when(jnp.logical_or(starts, up2))
    def _():
        part = pl.ds(0, chunks)
        copy(S2.at[part], S.at[part], two_s.at[0], st_r.at[0], d + 1).wait_send()


def write_out(*refs):
    sems = refs[8]
    copies = [pltpu.make_async_copy(refs[i], refs[i + 4], sems.at[i]) for i in range(4)]
    for one in copies:
        one.start()
    for one in copies:
        one.wait()


def body(cpoint_guess, adjoint_guess, weights, biases, diffusion, section_len):
    pixels = cpoint_guess.shape[-1]
    images = lax.axis_size("batch")
    chunks = pixels // LANES
    blocks = 2
    vmem = pl.BlockSpec(memory_space=pltpu.VMEM)
    image_shape = jax.ShapeDtypeStruct((C, pixels), F)
    dma = pltpu.SemaphoreType.DMA

    def stack(*lead):
        return pltpu.VMEM(lead + (C, LANES), F)

    outs = pl.pallas_call(
        kernel,
        out_shape=(
            image_shape, image_shape,
            jax.ShapeDtypeStruct((MOST, C, C), F), jax.ShapeDtypeStruct((MOST, C), F),
        ),
        in_specs=[pl.BlockSpec(memory_space=pltpu.HBM)] * 6,
        out_specs=(vmem,) * 4,
        scratch_shapes=[
            stack(MOST + 1, chunks + 2), stack(MOST, chunks), stack(MOST + 1, chunks + 2), stack(2, chunks + 2),
            stack(chunks + 2), stack(chunks), stack(chunks), stack(chunks), stack(chunks + 1), stack(chunks + 1),
            pltpu.VMEM((MOST, C, 3 * C), BF), pltpu.VMEM((MOST, C, 3 * C), BF), stack(MOST), stack(MOST),
            stack(C), stack(C), stack(C), stack(C), stack(4),
            pltpu.VMEM((MOST + 1, C, C), F),
            pltpu.VMEM((MOST // 4 * C + MOST, LANES), F), pltpu.VMEM((images, MOST // 4 * C + MOST, LANES), F),
            dma((blocks,)), dma((blocks,)), dma((blocks,)), dma((blocks,)), dma((blocks,)), dma((blocks,)),
            dma((3,)), dma((3,)), dma((3,)), dma((3,)), dma((1,)), dma((chunks,)),
            dma((images - 1,)), dma((images - 1,)),
            pltpu.VMEM((C, pixels), F), pltpu.VMEM((C, pixels), F),
            pltpu.VMEM((MOST, C, C), F), pltpu.VMEM((MOST, C), F), pltpu.VMEM((1, C), F),
            pltpu.SMEM(section_len.shape, jnp.int32), dma((6,)),
        ],
        compiler_params=pltpu.CompilerParams(
            collective_id=0, has_side_effects=True, vmem_limit_bytes=32 << 20
        ),
        name="mgrit_cycle",
    )(
        *(
            pltpu.with_memory_space_constraint(x, pltpu.HBM)
            for x in (
                cpoint_guess.reshape(C, pixels), adjoint_guess.reshape(C, pixels), weights, biases,
                diffusion.reshape(1, C), section_len,
            )
        )
    )
    states_out, adjoint_out, grad_weights, grad_biases = pl.pallas_call(
        write_out,
        out_shape=tuple(jax.ShapeDtypeStruct(o.shape, o.dtype) for o in outs),
        in_specs=[vmem] * 4,
        out_specs=(pl.BlockSpec(memory_space=pltpu.HBM),) * 4,
        scratch_shapes=[dma((4,))],
        compiler_params=pltpu.CompilerParams(vmem_limit_bytes=8 << 20),
        name="write_out",
    )(*outs)
    return states_out[None, None], adjoint_out[None, None], grad_weights, grad_biases


def solution(mesh):
    placed = (
        P("depth", "batch", None, None), P("depth", "batch", None, None), P("depth", None, None),
        P("depth", None), P(), P(),
    )
    return jax.shard_map(
        body, mesh=mesh, in_specs=placed,
        out_specs=(
            P("depth", "batch", None, None), P("depth", "batch", None, None), P("depth", None, None),
            P("depth", None),
        ),
        check_vma=False,
    )
```

```python
import jax
import jax.numpy as jnp
from jax import lax
from jax.experimental import pallas as pl
from jax.experimental.pallas import tpu as pltpu
from jax.sharding import PartitionSpec as P

MOST = 8
C = 32
LANES = 128
F = jnp.float32
BF = jnp.bfloat16
NT = (((1,), (1,)), ((), ()))


def split2(x):
    hi = x.astype(BF)
    return hi, (x - hi.astype(F)).astype(BF)


def dot3(packed, x):
    hi, lo = split2(x)
    return jnp.dot(packed, jnp.concatenate([hi, lo, hi], axis=0), preferred_element_type=F)


def pack3(matrix):
    hi, lo = split2(matrix)
    return jnp.concatenate([hi, hi, lo], axis=1)


def lane_masks():
    lane = lax.broadcasted_iota(jnp.int32, (C, LANES), 1)
    return lane < 64, lane % 64 == 0, lane % 64 == 63


def beside(x, masks):
    zero = jnp.zeros_like(x)
    return jnp.where(masks[1], zero, pltpu.roll(x, 1, 1)) + jnp.where(masks[2], zero, pltpu.roll(x, 127, 1))


def chunk_laps(chunks, count, masks):
    turned = [pltpu.roll(x, 64, 1) for x in chunks]
    laps = []
    for k in range(1, count + 1):
        above_below = turned[k] + jnp.where(masks[0], turned[k - 1], turned[k + 1])
        laps.append((above_below + beside(chunks[k], masks)) - 4.0 * chunks[k])
    return laps


def column_of(row, eye):
    return jnp.sum(jnp.where(eye, jnp.broadcast_to(row, (C, C)), 0.0), axis=1, keepdims=True)


def row_of(column, eye):
    return jnp.sum(jnp.where(eye, jnp.broadcast_to(column, (C, C)), 0.0), axis=0, keepdims=True)


def spread(matrix, out_ref):
    for k in range(C):
        out_ref[k] = jnp.broadcast_to(matrix[:, k : k + 1], (C, LANES))


def mix(spread_ref, x, first):
    sums = [first, None]
    for k in range(C):
        term = spread_ref[k] * jnp.broadcast_to(x[k : k + 1, :], (C, LANES))
        sums[k % 2] = term if sums[k % 2] is None else sums[k % 2] + term
    return sums[0] + sums[1]


def kernel(
    guess_hbm, adj_hbm, w_hbm, b_hbm, d_hbm, n_hbm,
    s_out, a_out, gw_out, gb_out,
    A, T, H, G, LR, LSEND, S, S2, TAU, TAU_A,
    WC, WT, BB, FD, SPA, SPAT, SPB, SPBT, CB, GB, PK, GR,
    push_s, push_r, lam_s, lam_r, tau_s, tau_r, par_s, par_r, one_s, one_r, two_s, st_r, grad_s, grad_r,
    guess_ref, adj_ref, w_ref, b_ref, d_ref, n_ref, in_s,
):
    sections, images = lax.axis_size("depth"), lax.axis_size("batch")
    d, image = lax.axis_index("depth"), lax.axis_index("batch")
    chunks = guess_ref.shape[1] // LANES
    blocks = 2
    NB = chunks // blocks
    halo = MOST // 2
    cut = (3 * chunks) // 8
    parts = ((0, cut), (cut, chunks))
    core, chip, chips = d % 2, d // 2, sections // 2
    has_prev, has_next = d > 0, d < sections - 1
    even = core == 0
    odd = core == 1
    early = chips // 4 + 1
    ahead = jnp.where(even, MOST, jnp.where(chip >= (12 * chips) // 16, MOST, jnp.clip(2 * (chip - (9 * chips) // 16), 0, MOST)))
    masks = lane_masks()
    eye = lax.broadcasted_iota(jnp.int32, (C, C), 0) == lax.broadcasted_iota(jnp.int32, (C, C), 1)

    def at(c):
        return pl.ds(pl.multiple_of(c * LANES, LANES), LANES)

    def copy(src, dst, ssem, rsem, depth_to, image_to=None):
        return pltpu.make_async_remote_copy(
            src_ref=src, dst_ref=dst, send_sem=ssem, recv_sem=rsem,
            device_id=(depth_to, image if image_to is None else image_to),
            device_id_type=pl.DeviceIdType.MESH,
        )

    def brought(src, dst, sem):
        return pltpu.make_async_copy(src, dst, sem)

    small = [
        brought(src, dst, in_s.at[i])
        for i, (src, dst) in enumerate(((n_hbm, n_ref), (w_hbm, w_ref), (b_hbm, b_ref), (d_hbm, d_ref)))
    ]
    guess_in, adj_in = brought(guess_hbm, guess_ref, in_s.at[4]), brought(adj_hbm, adj_ref, in_s.at[5])
    for part in small:
        part.start()
    guess_in.start()
    adj_in.start()

    barrier = pltpu.get_barrier_semaphore()

    def greet(cond, depth_to, image_to):
        @pl.when(cond)
        def _():
            pl.semaphore_signal(barrier, inc=1, device_id=(depth_to, image_to), device_id_type=pl.DeviceIdType.MESH)

    up2, down2 = jnp.logical_and(odd, chip < chips - 1), jnp.logical_and(odd, chip > 0)
    greet(has_prev, d - 1, image)
    greet(has_next, d + 1, image)
    greet(up2, d + 2, image)
    greet(down2, d - 2, image)
    for o in range(1, images):
        pl.semaphore_signal(
            barrier, inc=1, device_id=(d, (image + o) % images), device_id_type=pl.DeviceIdType.MESH
        )
    partners = (
        has_prev.astype(jnp.int32) + has_next.astype(jnp.int32) + up2.astype(jnp.int32)
        + down2.astype(jnp.int32) + (images - 1)
    )

    starts, ends = jnp.logical_not(has_prev), jnp.logical_not(has_next)

    zero_chunk = jnp.zeros((C, LANES), F)
    for l in range(MOST + 1):
        for ref in (A, H):
            ref[l, 0] = zero_chunk
            ref[l, chunks + 1] = zero_chunk
    for ref in (G.at[0], G.at[1], LR):
        ref[0] = zero_chunk
        ref[chunks + 1] = zero_chunk

    for part in small:
        part.wait()
    n = n_ref[d]
    diff_col = column_of(d_ref[...], eye)
    diff = jnp.broadcast_to(diff_col, (C, LANES))

    def prepare(i, _):
        factor = jnp.where(i < n, 1.0 / MOST, 0.0)
        WC[i] = pack3(w_ref[i])
        WT[i] = pack3(w_ref[i].T * factor)
        BB[i] = jnp.broadcast_to(column_of(b_ref[pl.ds(i, 1), :], eye), (C, LANES))
        FD[i] = diff * factor
        return 0

    lax.fori_loop(0, MOST, prepare, 0, unroll=True)
    guess_in.wait()
    for c in range(chunks):
        H[0, c + 1] = guess_ref[:, c * LANES : (c + 1) * LANES]

    def forward_tile(src, i, lo, count, dst, keep, open_end):
        u = [src[lo + k] for k in range(count + 1)] + [zero_chunk if open_end else src[lo + count + 1]]
        laps = chunk_laps(u, count, masks)
        bias = jnp.concatenate([BB[i]] * count, axis=1)
        act = jnp.tanh(dot3(WC[i], jnp.concatenate(u[1:-1], axis=1)) + bias)
        mixed = dot3(WT[i], act)
        fd = FD[i]
        for k in range(count):
            dst[lo + k + 1] = u[k + 1] + fd * laps[k] - mixed[:, k * LANES : (k + 1) * LANES]
            if keep is not None:
                keep[lo + k] = act[:, k * LANES : (k + 1) * LANES]

    def into(ref, shift):
        def store(c, value):
            ref[c + shift] = value
        return store

    def sweep(stack, keeps, lo, count, open_end):
        def layer(i, _):
            keep = None if keeps is None else keeps.at[i]
            forward_tile(stack.at[i], i, lo, wide, stack.at[i + 1], keep, open_end)
            return 0

        wide = count
        lax.fori_loop(0, MOST // 2, layer, 0)
        wide = count - halo // 2 if open_end else count
        lax.fori_loop(MOST // 2, MOST, layer, 0)

    upper = cut + halo

    def push_copy(j):
        part = pl.ds(1, upper) if j == 0 else pl.ds(1 + upper, chunks - upper)
        return copy(H.at[MOST, part], A.at[0, part], push_s.at[j], push_r.at[j], d + 1)

    def push(j):
        @pl.when(has_next)
        def _():
            push_copy(j).start()

    first = min(upper + halo, chunks)
    sweep(H, None, 0, first, first < chunks)
    pl.semaphore_wait(barrier, partners)
    push(0)
    sweep(H, None, upper, chunks - upper, False)
    push(1)

    part_copies = [
        copy(SPA, SPA, par_s.at[0], par_r.at[0], d + 1),
        copy(SPAT, SPAT, par_s.at[1], par_r.at[1], d + 1),
        copy(CB.at[0:2], CB.at[0:2], par_s.at[2], par_r.at[2], d + 1),
    ]

    def first_copy(c):
        return copy(guess_ref.at[:, at(c)], S.at[c], two_s.at[0], st_r.at[c], d + 1)

    @pl.when(starts)
    def _():
        def send(c, _):
            first_copy(c).start()
            return 0
        lax.fori_loop(0, chunks, send, 0)

    def propagator(matrix_ref, back_ref, row):
        spread(w_ref[0], matrix_ref)
        spread(w_ref[0].T * -coarse, back_ref)
        CB[row] = BB[0]
        CB[row + 1] = diff * coarse

    coarse = n.astype(F) / MOST

    @pl.when(even)
    def _():
        propagator(SPA, SPAT, 0)
        for part in part_copies:
            part.start()

    @pl.when(odd)
    def _():
        propagator(SPB, SPBT, 2)

    layers = n.astype(F)

    def tau_of(c):
        start = A[0, c + 1]
        return A[MOST, c + 1] - (start + layers * (A[1, c + 1] - start))

    def tau_copy(j):
        part = pl.ds(0, cut) if j == 0 else pl.ds(cut, chunks + 1 - cut)
        return copy(TAU.at[part], TAU_A.at[part], tau_s.at[j], tau_r.at[j], d + 1)

    @pl.when(starts)
    def _():
        for c in range(chunks):
            A[0, c + 1] = guess_ref[:, c * LANES : (c + 1) * LANES]

    def push_arrived(j):
        @pl.when(has_prev)
        def _():
            push_copy(j).wait_recv()

    @pl.when(even)
    def _():
        for j, (lo, hi) in enumerate(parts):
            push_arrived(j)
            if j == 0:
                sweep(A, T, 0, upper, True)
            else:
                sweep(A, T, cut, chunks - cut, False)
            before = zero_chunk if j == 0 else tau_of(cut - 1)
            for c in range(lo, hi):
                here = tau_of(c)
                TAU[c] = jnp.where(masks[0], here, before)
                before = here
            if j == 1:
                TAU[chunks] = jnp.where(masks[0], 0.0, before)
            tau_copy(j).start()

    @pl.when(odd)
    def _():
        for j in range(2):
            push_arrived(j)
        sweep(A, T, 0, chunks, False)
        for c in range(chunks):
            TAU[c] = tau_of(c)

    hand = (0, cut, chunks - chunks // 8, chunks)

    def one_copy(p):
        part = pl.ds(hand[p], hand[p + 1] - hand[p])
        return copy(S.at[part], S.at[part], one_s.at[p], one_r.at[p], d - 1)

    def two_copy(c):
        return copy(S2.at[c], S.at[c], two_s.at[0], st_r.at[c], d + 2)

    def relay(both):
        for part in part_copies:
            part.wait_recv()
        lower = masks[0]
        bias_a, fd_a, bias_b, fd_b = CB[0], CB[1], CB[2], CB[3]
        bias_ab, bias_ba = jnp.where(lower, bias_a, bias_b), jnp.where(lower, bias_b, bias_a)

        for k in range(C):
            for first_ref, second_ref in ((SPA, SPB), (SPAT, SPBT)):
                one, two = first_ref[k], second_ref[k]
                first_ref[k] = jnp.where(lower, one, two)
                second_ref[k] = jnp.where(lower, two, one)

        def pull(there_ref, back_ref, x, bias):
            return mix(back_ref, jnp.tanh(mix(there_ref, x, bias)), None)

        def step(c, carry, first=False, last=False):
            prev, one_prev, ready = carry
            if last:
                now = zero_chunk
            else:
                two_copy(c).wait_recv()
                now = S[c]
            mid = jnp.where(lower, now, prev)
            lap = (pltpu.roll(prev + now, 64, 1) + beside(mid, masks)) - 4.0 * mid
            base = mid + fd_a * lap + TAU_A[c]
            pulled = pull(SPA, SPAT, jnp.where(lower, now, base + ready), bias_ab)
            one = base + jnp.where(lower, pulled, ready)
            if first:
                one = jnp.where(lower, one, 0.0)
            if last:
                one = jnp.where(lower, 0.0, one)
            if not first:
                mid_one = jnp.where(lower, one_prev, one)
                if both:
                    lap_b = (pltpu.roll(one_prev + one, 64, 1) + beside(mid_one, masks)) - 4.0 * mid_one
                    S2[c - 1] = (mid_one + fd_b * lap_b + TAU[c - 1]) + jnp.where(lower, ready, pulled)
                    two_copy(c - 1).start()
                s_out[:, at(c - 1)] = mid_one
            if last:
                return None
            return now, one, pull(SPB, SPBT, jnp.where(lower, one, now), bias_ba)

        tau_copy(0).wait_recv()
        carry = step(0, (zero_chunk,) * 3, first=True)
        for p in range(3):
            if p == 1:
                tau_copy(1).wait_recv()
            carry = lax.fori_loop(max(1, hand[p]), hand[p + 1], step, carry)
            one_copy(p).start()
        step(chunks, carry, last=True)

    def backward_block(src, i, j, store, with_grads):
        g = [src[j * NB + k] for k in range(NB + 2)]
        laps = chunk_laps(g, NB, masks)
        act = jnp.concatenate([T[i, j * NB + k] for k in range(NB)], axis=1)
        g_hi, g_lo = split2(jnp.concatenate(g[1:-1], axis=1))
        pulled = jnp.dot(WC[i], jnp.concatenate([g_hi, g_lo, g_hi], axis=0), preferred_element_type=F)
        pre = (1.0 - act * act) * pulled
        p_hi, p_lo = split2(pre)
        back = jnp.dot(WT[i], jnp.concatenate([p_hi, p_lo, p_hi], axis=0), preferred_element_type=F)
        fd = FD[i]
        for k in range(NB):
            store(j * NB + k, g[k + 1] + fd * laps[k] - back[:, k * LANES : (k + 1) * LANES])
        if not with_grads:
            return None
        t_hi, t_lo = split2(act)
        u_hi, u_lo = split2(jnp.concatenate([A[i, j * NB + k + 1] for k in range(NB)], axis=1))
        left = jnp.concatenate(
            [jnp.concatenate([t_hi, p_hi], axis=1), jnp.concatenate([t_lo, p_lo], axis=1)], axis=0
        )
        right = jnp.concatenate(
            [jnp.concatenate([g_hi, u_hi], axis=1), jnp.concatenate([g_lo, u_lo], axis=1)], axis=0
        )
        prod = lax.dot_general(left, right, NT, preferred_element_type=F)
        bias_sum = pre[:, :LANES]
        for k in range(1, NB):
            bias_sum = bias_sum + pre[:, k * LANES : (k + 1) * LANES]
        return prod, bias_sum

    def lam_copy(j):
        return copy(LSEND.at[pl.ds(j * NB, NB)], LR.at[pl.ds(1 + j * NB, NB)], lam_s.at[j], lam_r.at[j], d - 1)

    def backward_start():
        adj_in.wait()
        for c in range(chunks):
            G[0, c + 1] = adj_ref[:, c * LANES : (c + 1) * LANES]

        def layer(i, _):
            def block(j, _):
                backward_block(G.at[i % 2], MOST - 1 - i, j, into(G.at[(i + 1) % 2], 1), False)
                return 0
            lax.fori_loop(0, blocks, block, 0, unroll=True)
            return 0

        lax.fori_loop(0, MOST - 1, layer, 0)

        def block(j, _):
            backward_block(G.at[(MOST - 1) % 2], 0, j, into(LSEND, 0), False)

            @pl.when(has_prev)
            def _():
                lam_copy(j).start()
            return 0

        lax.fori_loop(0, blocks, block, 0)

    def full_ready():
        @pl.when(has_next)
        def _():
            for j in range(blocks):
                lam_copy(j).wait_recv()

        @pl.when(ends)
        def _():
            for c in range(chunks):
                LR[c + 1] = adj_ref[:, c * LANES : (c + 1) * LANES]

        for c in range(chunks):
            G[0, c + 1] = LR[c + 1]
        GB[MOST] = jnp.zeros((C, C), F)
        PK[...] = jnp.zeros_like(PK)

    def full_layers(first_layer, end_layer):
        def layer(i, _):
            slot = MOST - 1 - i
            factor = jnp.where(slot < n, 1.0 / MOST, 0.0)
            start = (jnp.zeros((2 * C, 2 * C), F), jnp.zeros((C, LANES), F))

            def block(j, sums):
                prod, bias_sum = backward_block(G.at[i % 2], slot, j, into(G.at[(i + 1) % 2], 1), True)
                return sums[0] + prod, sums[1] + bias_sum
            prod, bias_sum = lax.fori_loop(0, blocks, block, start, unroll=True)
            GB[slot] = -factor * (prod[:C, :C] + (prod[:C, C:] + prod[C:, :C]))
            column = jnp.sum(bias_sum, axis=1, keepdims=True)
            GB[MOST, pl.ds(slot, 1), :] = -factor * row_of(column, eye)
            return 0

        lax.fori_loop(first_layer, end_layer, layer, 0)

    side = LANES // C

    def share_grads():
        for g in range(MOST // side):
            PK[g * C : (g + 1) * C] = jnp.concatenate([GB[g * side + k] for k in range(side)], axis=1)
        PK[MOST // side * C :, :C] = GB[MOST, :MOST]
        GR[image] = PK[...]
        for o in range(1, images):
            grad_copy(o).start()
        for c in range(chunks):
            a_out[:, c * LANES : (c + 1) * LANES] = G[0, c + 1]

    def grad_copy(o):
        return copy(PK, GR.at[image], grad_s.at[o - 1], grad_r.at[o - 1], d, (image + o) % images)

    def turn(order, _):
        here = jnp.logical_and(odd, order == jnp.where(chip < early, 0, 3))

        @pl.when(jnp.logical_and(here, chip < chips - 1))
        def _():
            relay(True)

        @pl.when(jnp.logical_and(here, chip == chips - 1))
        def _():
            relay(False)

        @pl.when(order == 1)
        def _():
            backward_start()

        @pl.when(order == jnp.where(ahead > 0, 2, 4))
        def _():
            full_ready()

        @pl.when(jnp.logical_or(order == 2, order == 4))
        def _():
            full_layers(jnp.where(order == 2, 0, ahead), jnp.where(order == 2, ahead, MOST))

        @pl.when(order == jnp.where(ahead == MOST, 2, 4))
        def _():
            share_grads()
        return 0

    lax.fori_loop(0, 5, turn, 0)
    for o in range(1, images):
        grad_copy(o).wait_recv()
    total = GR[0]
    for b in range(1, images):
        total = total + GR[b]
    for i in range(MOST):
        row, lane = i // side * C, i % side * C
        gw_out[i] = total[row : row + C, lane : lane + C]
    gb_out[...] = total[MOST // side * C :, :C]

    @pl.when(even)
    def _():
        for p in range(3):
            one_copy(p).wait_recv()
            for c in range(hand[p], hand[p + 1]):
                s_out[:, c * LANES : (c + 1) * LANES] = S[c]

    for o in range(1, images):
        grad_copy(o).wait_send()

    @pl.when(has_next)
    def _():
        for j in range(blocks):
            push_copy(j).wait_send()

    @pl.when(has_prev)
    def _():
        for j in range(blocks):
            lam_copy(j).wait_send()

    @pl.when(even)
    def _():
        for part in part_copies:
            part.wait_send()
        for j in range(blocks):
            tau_copy(j).wait_send()

    @pl.when(odd)
    def _():
        for p in range(3):
            one_copy(p).wait_send()

    @pl.when(jnp.logical_or(starts, up2))
    def _():
        part = pl.ds(0, chunks)
        copy(S2.at[part], S.at[part], two_s.at[0], st_r.at[0], d + 1).wait_send()


def write_out(*refs):
    sems = refs[8]
    copies = [pltpu.make_async_copy(refs[i], refs[i + 4], sems.at[i]) for i in range(4)]
    for one in copies:
        one.start()
    for one in copies:
        one.wait()


def body(cpoint_guess, adjoint_guess, weights, biases, diffusion, section_len):
    pixels = cpoint_guess.shape[-1]
    images = lax.axis_size("batch")
    chunks = pixels // LANES
    blocks = 2
    vmem = pl.BlockSpec(memory_space=pltpu.VMEM)
    image_shape = jax.ShapeDtypeStruct((C, pixels), F)
    dma = pltpu.SemaphoreType.DMA

    def stack(*lead):
        return pltpu.VMEM(lead + (C, LANES), F)

    outs = pl.pallas_call(
        kernel,
        out_shape=(
            image_shape, image_shape,
            jax.ShapeDtypeStruct((MOST, C, C), F), jax.ShapeDtypeStruct((MOST, C), F),
        ),
        in_specs=[pl.BlockSpec(memory_space=pltpu.HBM)] * 6,
        out_specs=(vmem,) * 4,
        scratch_shapes=[
            stack(MOST + 1, chunks + 2), stack(MOST, chunks), stack(MOST + 1, chunks + 2), stack(2, chunks + 2),
            stack(chunks + 2), stack(chunks), stack(chunks), stack(chunks), stack(chunks + 1), stack(chunks + 1),
            pltpu.VMEM((MOST, C, 3 * C), BF), pltpu.VMEM((MOST, C, 3 * C), BF), stack(MOST), stack(MOST),
            stack(C), stack(C), stack(C), stack(C), stack(4),
            pltpu.VMEM((MOST + 1, C, C), F),
            pltpu.VMEM((MOST // 4 * C + MOST, LANES), F), pltpu.VMEM((images, MOST // 4 * C + MOST, LANES), F),
            dma((blocks,)), dma((blocks,)), dma((blocks,)), dma((blocks,)), dma((blocks,)), dma((blocks,)),
            dma((3,)), dma((3,)), dma((3,)), dma((3,)), dma((1,)), dma((chunks,)),
            dma((images - 1,)), dma((images - 1,)),
            pltpu.VMEM((C, pixels), F), pltpu.VMEM((C, pixels), F),
            pltpu.VMEM((MOST, C, C), F), pltpu.VMEM((MOST, C), F), pltpu.VMEM((1, C), F),
            pltpu.SMEM(section_len.shape, jnp.int32), dma((6,)),
        ],
        compiler_params=pltpu.CompilerParams(
            collective_id=0, has_side_effects=True, vmem_limit_bytes=32 << 20
        ),
        name="mgrit_cycle",
    )(
        *(
            pltpu.with_memory_space_constraint(x, pltpu.HBM)
            for x in (
                cpoint_guess.reshape(C, pixels), adjoint_guess.reshape(C, pixels), weights, biases,
                diffusion.reshape(1, C), section_len,
            )
        )
    )
    states_out, adjoint_out, grad_weights, grad_biases = pl.pallas_call(
        write_out,
        out_shape=tuple(jax.ShapeDtypeStruct(o.shape, o.dtype) for o in outs),
        in_specs=[vmem] * 4,
        out_specs=(pl.BlockSpec(memory_space=pltpu.HBM),) * 4,
        scratch_shapes=[dma((4,))],
        compiler_params=pltpu.CompilerParams(vmem_limit_bytes=8 << 20),
        name="write_out",
    )(*outs)
    return states_out[None, None], adjoint_out[None, None], grad_weights, grad_biases


def solution(mesh):
    placed = (
        P("depth", "batch", None, None), P("depth", "batch", None, None), P("depth", None, None),
        P("depth", None), P(), P(),
    )
    return jax.shard_map(
        body, mesh=mesh, in_specs=placed,
        out_specs=(
            P("depth", "batch", None, None), P("depth", "batch", None, None), P("depth", None, None),
            P("depth", None),
        ),
        check_vma=False,
    )
```

```python
import jax
import jax.numpy as jnp
from jax import lax
from jax.experimental import pallas as pl
from jax.experimental.pallas import tpu as pltpu
from jax.sharding import PartitionSpec as P

MOST = 8
C = 32
LANES = 128
F = jnp.float32
BF = jnp.bfloat16
NT = (((1,), (1,)), ((), ()))


def split2(x):
    hi = x.astype(BF)
    return hi, (x - hi.astype(F)).astype(BF)


def dot3(packed, x):
    hi, lo = split2(x)
    return jnp.dot(packed, jnp.concatenate([hi, lo, hi], axis=0), preferred_element_type=F)


def pack3(matrix):
    hi, lo = split2(matrix)
    return jnp.concatenate([hi, hi, lo], axis=1)


def lane_masks():
    lane = lax.broadcasted_iota(jnp.int32, (C, LANES), 1)
    return lane < 64, lane % 64 == 0, lane % 64 == 63


def beside(x, masks):
    zero = jnp.zeros_like(x)
    return jnp.where(masks[1], zero, pltpu.roll(x, 1, 1)) + jnp.where(masks[2], zero, pltpu.roll(x, 127, 1))


def chunk_laps(chunks, count, masks):
    turned = [pltpu.roll(x, 64, 1) for x in chunks]
    laps = []
    for k in range(1, count + 1):
        above_below = turned[k] + jnp.where(masks[0], turned[k - 1], turned[k + 1])
        laps.append((above_below + beside(chunks[k], masks)) - 4.0 * chunks[k])
    return laps


def column_of(row, eye):
    return jnp.sum(jnp.where(eye, jnp.broadcast_to(row, (C, C)), 0.0), axis=1, keepdims=True)


def row_of(column, eye):
    return jnp.sum(jnp.where(eye, jnp.broadcast_to(column, (C, C)), 0.0), axis=0, keepdims=True)


def spread(matrix, out_ref):
    for k in range(C):
        out_ref[k] = jnp.broadcast_to(matrix[:, k : k + 1], (C, LANES))


def mix(spread_ref, x, first):
    sums = [first, None]
    for k in range(C):
        term = spread_ref[k] * jnp.broadcast_to(x[k : k + 1, :], (C, LANES))
        sums[k % 2] = term if sums[k % 2] is None else sums[k % 2] + term
    return sums[0] + sums[1]


def kernel(
    guess_hbm, adj_hbm, w_hbm, b_hbm, d_hbm, n_hbm,
    s_out, a_out, gw_out, gb_out,
    A, T, H, G, LR, LSEND, S, S2, TAU, TAU_A,
    WC, WT, BB, FD, SPA, SPAT, SPB, SPBT, CB, GB, PK, GR,
    push_s, push_r, lam_s, lam_r, tau_s, tau_r, par_s, par_r, one_s, one_r, two_s, st_r, grad_s, grad_r,
    guess_ref, adj_ref, w_ref, b_ref, d_ref, n_ref, in_s,
):
    sections, images = lax.axis_size("depth"), lax.axis_size("batch")
    d, image = lax.axis_index("depth"), lax.axis_index("batch")
    chunks = guess_ref.shape[1] // LANES
    blocks = 2
    NB = chunks // blocks
    halo = MOST // 2
    cut = (3 * chunks) // 8
    parts = ((0, cut), (cut, chunks))
    core, chip, chips = d % 2, d // 2, sections // 2
    has_prev, has_next = d > 0, d < sections - 1
    even = core == 0
    odd = core == 1
    early = chips // 4 + 1
    ahead = jnp.where(even, MOST, jnp.where(chip >= (12 * chips) // 16, MOST, jnp.clip(2 * (chip - (9 * chips) // 16), 0, MOST)))
    masks = lane_masks()
    eye = lax.broadcasted_iota(jnp.int32, (C, C), 0) == lax.broadcasted_iota(jnp.int32, (C, C), 1)

    def at(c):
        return pl.ds(pl.multiple_of(c * LANES, LANES), LANES)

    def copy(src, dst, ssem, rsem, depth_to, image_to=None):
        return pltpu.make_async_remote_copy(
            src_ref=src, dst_ref=dst, send_sem=ssem, recv_sem=rsem,
            device_id=(depth_to, image if image_to is None else image_to),
            device_id_type=pl.DeviceIdType.MESH,
        )

    def brought(src, dst, sem):
        return pltpu.make_async_copy(src, dst, sem)

    small = [
        brought(src, dst, in_s.at[i])
        for i, (src, dst) in enumerate(((n_hbm, n_ref), (w_hbm, w_ref), (b_hbm, b_ref), (d_hbm, d_ref)))
    ]
    guess_in, adj_in = brought(guess_hbm, guess_ref, in_s.at[4]), brought(adj_hbm, adj_ref, in_s.at[5])
    for part in small:
        part.start()
    guess_in.start()
    adj_in.start()

    barrier = pltpu.get_barrier_semaphore()

    def greet(cond, depth_to, image_to):
        @pl.when(cond)
        def _():
            pl.semaphore_signal(barrier, inc=1, device_id=(depth_to, image_to), device_id_type=pl.DeviceIdType.MESH)

    up2, down2 = jnp.logical_and(odd, chip < chips - 1), jnp.logical_and(odd, chip > 0)
    greet(has_prev, d - 1, image)
    greet(has_next, d + 1, image)
    greet(up2, d + 2, image)
    greet(down2, d - 2, image)
    for o in range(1, images):
        pl.semaphore_signal(
            barrier, inc=1, device_id=(d, (image + o) % images), device_id_type=pl.DeviceIdType.MESH
        )
    partners = (
        has_prev.astype(jnp.int32) + has_next.astype(jnp.int32) + up2.astype(jnp.int32)
        + down2.astype(jnp.int32) + (images - 1)
    )

    starts, ends = jnp.logical_not(has_prev), jnp.logical_not(has_next)

    zero_chunk = jnp.zeros((C, LANES), F)
    for l in range(MOST + 1):
        for ref in (A, H):
            ref[l, 0] = zero_chunk
            ref[l, chunks + 1] = zero_chunk
    for ref in (G.at[0], G.at[1], LR):
        ref[0] = zero_chunk
        ref[chunks + 1] = zero_chunk

    for part in small:
        part.wait()
    n = n_ref[d]
    diff_col = column_of(d_ref[...], eye)
    diff = jnp.broadcast_to(diff_col, (C, LANES))

    def prepare(i, _):
        factor = jnp.where(i < n, 1.0 / MOST, 0.0)
        WC[i] = pack3(w_ref[i])
        WT[i] = pack3(w_ref[i].T * factor)
        BB[i] = jnp.broadcast_to(column_of(b_ref[pl.ds(i, 1), :], eye), (C, LANES))
        FD[i] = diff * factor
        return 0

    lax.fori_loop(0, MOST, prepare, 0, unroll=True)
    guess_in.wait()
    for c in range(chunks):
        H[0, c + 1] = guess_ref[:, c * LANES : (c + 1) * LANES]

    def forward_tile(src, i, lo, count, dst, keep, open_end):
        u = [src[lo + k] for k in range(count + 1)] + [zero_chunk if open_end else src[lo + count + 1]]
        laps = chunk_laps(u, count, masks)
        bias = jnp.concatenate([BB[i]] * count, axis=1)
        act = jnp.tanh(dot3(WC[i], jnp.concatenate(u[1:-1], axis=1)) + bias)
        mixed = dot3(WT[i], act)
        fd = FD[i]
        for k in range(count):
            dst[lo + k + 1] = u[k + 1] + fd * laps[k] - mixed[:, k * LANES : (k + 1) * LANES]
            if keep is not None:
                keep[lo + k] = act[:, k * LANES : (k + 1) * LANES]

    def into(ref, shift):
        def store(c, value):
            ref[c + shift] = value
        return store

    def sweep(stack, keeps, lo, count, open_end):
        def layer(i, _):
            keep = None if keeps is None else keeps.at[i]
            forward_tile(stack.at[i], i, lo, wide, stack.at[i + 1], keep, open_end)
            return 0

        wide = count
        lax.fori_loop(0, MOST // 2, layer, 0)
        wide = count - halo // 2 if open_end else count
        lax.fori_loop(MOST // 2, MOST, layer, 0)

    upper = cut + halo

    def push_copy(j):
        part = pl.ds(1, upper) if j == 0 else pl.ds(1 + upper, chunks - upper)
        return copy(H.at[MOST, part], A.at[0, part], push_s.at[j], push_r.at[j], d + 1)

    def push(j):
        @pl.when(has_next)
        def _():
            push_copy(j).start()

    first = min(upper + halo, chunks)
    sweep(H, None, 0, first, first < chunks)
    pl.semaphore_wait(barrier, partners)
    push(0)
    sweep(H, None, upper, chunks - upper, False)
    push(1)

    part_copies = [
        copy(SPA, SPA, par_s.at[0], par_r.at[0], d + 1),
        copy(SPAT, SPAT, par_s.at[1], par_r.at[1], d + 1),
        copy(CB.at[0:2], CB.at[0:2], par_s.at[2], par_r.at[2], d + 1),
    ]

    def first_copy(c):
        return copy(guess_ref.at[:, at(c)], S.at[c], two_s.at[0], st_r.at[c], d + 1)

    @pl.when(starts)
    def _():
        def send(c, _):
            first_copy(c).start()
            return 0
        lax.fori_loop(0, chunks, send, 0)

    def propagator(matrix_ref, back_ref, row):
        spread(w_ref[0], matrix_ref)
        spread(w_ref[0].T * -coarse, back_ref)
        CB[row] = BB[0]
        CB[row + 1] = diff * coarse

    coarse = n.astype(F) / MOST

    @pl.when(even)
    def _():
        propagator(SPA, SPAT, 0)
        for part in part_copies:
            part.start()

    @pl.when(odd)
    def _():
        propagator(SPB, SPBT, 2)

    layers = n.astype(F)

    def tau_of(c):
        start = A[0, c + 1]
        return A[MOST, c + 1] - (start + layers * (A[1, c + 1] - start))

    def tau_copy(j):
        part = pl.ds(0, cut) if j == 0 else pl.ds(cut, chunks + 1 - cut)
        return copy(TAU.at[part], TAU_A.at[part], tau_s.at[j], tau_r.at[j], d + 1)

    @pl.when(starts)
    def _():
        for c in range(chunks):
            A[0, c + 1] = guess_ref[:, c * LANES : (c + 1) * LANES]

    def push_arrived(j):
        @pl.when(has_prev)
        def _():
            push_copy(j).wait_recv()

    @pl.when(even)
    def _():
        for j, (lo, hi) in enumerate(parts):
            push_arrived(j)
            if j == 0:
                sweep(A, T, 0, upper, True)
            else:
                sweep(A, T, cut, chunks - cut, False)
            before = zero_chunk if j == 0 else tau_of(cut - 1)
            for c in range(lo, hi):
                here = tau_of(c)
                TAU[c] = jnp.where(masks[0], here, before)
                before = here
            if j == 1:
                TAU[chunks] = jnp.where(masks[0], 0.0, before)
            tau_copy(j).start()

    @pl.when(odd)
    def _():
        for j in range(2):
            push_arrived(j)
        sweep(A, T, 0, chunks, False)
        for c in range(chunks):
            TAU[c] = tau_of(c)

    hand = (0, cut, chunks - chunks // 8, chunks)

    def one_copy(p):
        part = pl.ds(hand[p], hand[p + 1] - hand[p])
        return copy(S.at[part], S.at[part], one_s.at[p], one_r.at[p], d - 1)

    def two_copy(c):
        return copy(S2.at[c], S.at[c], two_s.at[0], st_r.at[c], d + 2)

    def relay(both):
        for part in part_copies:
            part.wait_recv()
        bias_a, fd_a, bias_b, fd_b = CB[0], CB[1], CB[2], CB[3]
        lower = masks[0]

        def step(c, carry, first=False, last=False):
            prev, one_prev = carry
            if last:
                now = zero_chunk
            else:
                two_copy(c).wait_recv()
                now = S[c]
            mid = jnp.where(lower, now, prev)
            lap = (pltpu.roll(prev + now, 64, 1) + beside(mid, masks)) - 4.0 * mid
            act = jnp.tanh(mix(SPA, mid, bias_a))
            one = mix(SPAT, act, mid + fd_a * lap + TAU_A[c])
            if first:
                one = jnp.where(lower, one, 0.0)
            if last:
                one = jnp.where(lower, 0.0, one)
            if not first:
                mid_one = jnp.where(lower, one_prev, one)
                if both:
                    lap_b = (pltpu.roll(one_prev + one, 64, 1) + beside(mid_one, masks)) - 4.0 * mid_one
                    act_b = jnp.tanh(mix(SPB, mid_one, bias_b))
                    S2[c - 1] = mix(SPBT, act_b, mid_one + fd_b * lap_b + TAU[c - 1])
                    two_copy(c - 1).start()
                s_out[:, at(c - 1)] = mid_one
            return now, one

        tau_copy(0).wait_recv()
        carry = step(0, (zero_chunk,) * 2, first=True)
        for p in range(3):
            if p == 1:
                tau_copy(1).wait_recv()
            if p == 0:
                carry = step(1, carry)
            carry = lax.fori_loop(max(2, hand[p]), hand[p + 1], step, carry, unroll=2)
            one_copy(p).start()
        step(chunks, carry, last=True)

    def backward_block(src, i, j, store, with_grads):
        g = [src[j * NB + k] for k in range(NB + 2)]
        laps = chunk_laps(g, NB, masks)
        act = jnp.concatenate([T[i, j * NB + k] for k in range(NB)], axis=1)
        g_hi, g_lo = split2(jnp.concatenate(g[1:-1], axis=1))
        pulled = jnp.dot(WC[i], jnp.concatenate([g_hi, g_lo, g_hi], axis=0), preferred_element_type=F)
        pre = (1.0 - act * act) * pulled
        p_hi, p_lo = split2(pre)
        back = jnp.dot(WT[i], jnp.concatenate([p_hi, p_lo, p_hi], axis=0), preferred_element_type=F)
        fd = FD[i]
        for k in range(NB):
            store(j * NB + k, g[k + 1] + fd * laps[k] - back[:, k * LANES : (k + 1) * LANES])
        if not with_grads:
            return None
        t_hi, t_lo = split2(act)
        u_hi, u_lo = split2(jnp.concatenate([A[i, j * NB + k + 1] for k in range(NB)], axis=1))
        left = jnp.concatenate(
            [jnp.concatenate([t_hi, p_hi], axis=1), jnp.concatenate([t_lo, p_lo], axis=1)], axis=0
        )
        right = jnp.concatenate(
            [jnp.concatenate([g_hi, u_hi], axis=1), jnp.concatenate([g_lo, u_lo], axis=1)], axis=0
        )
        prod = lax.dot_general(left, right, NT, preferred_element_type=F)
        bias_sum = pre[:, :LANES]
        for k in range(1, NB):
            bias_sum = bias_sum + pre[:, k * LANES : (k + 1) * LANES]
        return prod, bias_sum

    def lam_copy(j):
        return copy(LSEND.at[pl.ds(j * NB, NB)], LR.at[pl.ds(1 + j * NB, NB)], lam_s.at[j], lam_r.at[j], d - 1)

    def backward_start():
        adj_in.wait()
        for c in range(chunks):
            G[0, c + 1] = adj_ref[:, c * LANES : (c + 1) * LANES]

        def layer(i, _):
            def block(j, _):
                backward_block(G.at[i % 2], MOST - 1 - i, j, into(G.at[(i + 1) % 2], 1), False)
                return 0
            lax.fori_loop(0, blocks, block, 0, unroll=True)
            return 0

        lax.fori_loop(0, MOST - 1, layer, 0)

        def block(j, _):
            backward_block(G.at[(MOST - 1) % 2], 0, j, into(LSEND, 0), False)

            @pl.when(has_prev)
            def _():
                lam_copy(j).start()
            return 0

        lax.fori_loop(0, blocks, block, 0)

    def full_ready():
        @pl.when(has_next)
        def _():
            for j in range(blocks):
                lam_copy(j).wait_recv()

        @pl.when(ends)
        def _():
            for c in range(chunks):
                LR[c + 1] = adj_ref[:, c * LANES : (c + 1) * LANES]

        for c in range(chunks):
            G[0, c + 1] = LR[c + 1]
        GB[MOST] = jnp.zeros((C, C), F)
        PK[...] = jnp.zeros_like(PK)

    def full_layers(first_layer, end_layer):
        def layer(i, _):
            slot = MOST - 1 - i
            factor = jnp.where(slot < n, 1.0 / MOST, 0.0)
            start = (jnp.zeros((2 * C, 2 * C), F), jnp.zeros((C, LANES), F))

            def block(j, sums):
                prod, bias_sum = backward_block(G.at[i % 2], slot, j, into(G.at[(i + 1) % 2], 1), True)
                return sums[0] + prod, sums[1] + bias_sum
            prod, bias_sum = lax.fori_loop(0, blocks, block, start, unroll=True)
            GB[slot] = -factor * (prod[:C, :C] + (prod[:C, C:] + prod[C:, :C]))
            column = jnp.sum(bias_sum, axis=1, keepdims=True)
            GB[MOST, pl.ds(slot, 1), :] = -factor * row_of(column, eye)
            return 0

        lax.fori_loop(first_layer, end_layer, layer, 0)

    side = LANES // C

    def share_grads():
        for g in range(MOST // side):
            PK[g * C : (g + 1) * C] = jnp.concatenate([GB[g * side + k] for k in range(side)], axis=1)
        PK[MOST // side * C :, :C] = GB[MOST, :MOST]
        GR[image] = PK[...]
        for o in range(1, images):
            grad_copy(o).start()
        for c in range(chunks):
            a_out[:, c * LANES : (c + 1) * LANES] = G[0, c + 1]

    def grad_copy(o):
        return copy(PK, GR.at[image], grad_s.at[o - 1], grad_r.at[o - 1], d, (image + o) % images)

    def turn(order, _):
        here = jnp.logical_and(odd, order == jnp.where(chip < early, 0, 3))

        @pl.when(jnp.logical_and(here, chip < chips - 1))
        def _():
            relay(True)

        @pl.when(jnp.logical_and(here, chip == chips - 1))
        def _():
            relay(False)

        @pl.when(order == 1)
        def _():
            backward_start()

        @pl.when(order == jnp.where(ahead > 0, 2, 4))
        def _():
            full_ready()

        @pl.when(jnp.logical_or(order == 2, order == 4))
        def _():
            full_layers(jnp.where(order == 2, 0, ahead), jnp.where(order == 2, ahead, MOST))

        @pl.when(order == jnp.where(ahead == MOST, 2, 4))
        def _():
            share_grads()
        return 0

    lax.fori_loop(0, 5, turn, 0)
    for o in range(1, images):
        grad_copy(o).wait_recv()
    total = GR[0]
    for b in range(1, images):
        total = total + GR[b]
    for i in range(MOST):
        row, lane = i // side * C, i % side * C
        gw_out[i] = total[row : row + C, lane : lane + C]
    gb_out[...] = total[MOST // side * C :, :C]

    @pl.when(even)
    def _():
        for p in range(3):
            one_copy(p).wait_recv()
            for c in range(hand[p], hand[p + 1]):
                s_out[:, c * LANES : (c + 1) * LANES] = S[c]

    for o in range(1, images):
        grad_copy(o).wait_send()

    @pl.when(has_next)
    def _():
        for j in range(blocks):
            push_copy(j).wait_send()

    @pl.when(has_prev)
    def _():
        for j in range(blocks):
            lam_copy(j).wait_send()

    @pl.when(even)
    def _():
        for part in part_copies:
            part.wait_send()
        for j in range(blocks):
            tau_copy(j).wait_send()

    @pl.when(odd)
    def _():
        for p in range(3):
            one_copy(p).wait_send()

    @pl.when(jnp.logical_or(starts, up2))
    def _():
        part = pl.ds(0, chunks)
        copy(S2.at[part], S.at[part], two_s.at[0], st_r.at[0], d + 1).wait_send()


def write_out(*refs):
    sems = refs[8]
    copies = [pltpu.make_async_copy(refs[i], refs[i + 4], sems.at[i]) for i in range(4)]
    for one in copies:
        one.start()
    for one in copies:
        one.wait()


def body(cpoint_guess, adjoint_guess, weights, biases, diffusion, section_len):
    pixels = cpoint_guess.shape[-1]
    images = lax.axis_size("batch")
    chunks = pixels // LANES
    blocks = 2
    vmem = pl.BlockSpec(memory_space=pltpu.VMEM)
    image_shape = jax.ShapeDtypeStruct((C, pixels), F)
    dma = pltpu.SemaphoreType.DMA

    def stack(*lead):
        return pltpu.VMEM(lead + (C, LANES), F)

    outs = pl.pallas_call(
        kernel,
        out_shape=(
            image_shape, image_shape,
            jax.ShapeDtypeStruct((MOST, C, C), F), jax.ShapeDtypeStruct((MOST, C), F),
        ),
        in_specs=[pl.BlockSpec(memory_space=pltpu.HBM)] * 6,
        out_specs=(vmem,) * 4,
        scratch_shapes=[
            stack(MOST + 1, chunks + 2), stack(MOST, chunks), stack(MOST + 1, chunks + 2), stack(2, chunks + 2),
            stack(chunks + 2), stack(chunks), stack(chunks), stack(chunks), stack(chunks + 1), stack(chunks + 1),
            pltpu.VMEM((MOST, C, 3 * C), BF), pltpu.VMEM((MOST, C, 3 * C), BF), stack(MOST), stack(MOST),
            stack(C), stack(C), stack(C), stack(C), stack(4),
            pltpu.VMEM((MOST + 1, C, C), F),
            pltpu.VMEM((MOST // 4 * C + MOST, LANES), F), pltpu.VMEM((images, MOST // 4 * C + MOST, LANES), F),
            dma((blocks,)), dma((blocks,)), dma((blocks,)), dma((blocks,)), dma((blocks,)), dma((blocks,)),
            dma((3,)), dma((3,)), dma((3,)), dma((3,)), dma((1,)), dma((chunks,)),
            dma((images - 1,)), dma((images - 1,)),
            pltpu.VMEM((C, pixels), F), pltpu.VMEM((C, pixels), F),
            pltpu.VMEM((MOST, C, C), F), pltpu.VMEM((MOST, C), F), pltpu.VMEM((1, C), F),
            pltpu.SMEM(section_len.shape, jnp.int32), dma((6,)),
        ],
        compiler_params=pltpu.CompilerParams(
            collective_id=0, has_side_effects=True, vmem_limit_bytes=32 << 20
        ),
        name="mgrit_cycle",
    )(
        *(
            pltpu.with_memory_space_constraint(x, pltpu.HBM)
            for x in (
                cpoint_guess.reshape(C, pixels), adjoint_guess.reshape(C, pixels), weights, biases,
                diffusion.reshape(1, C), section_len,
            )
        )
    )
    states_out, adjoint_out, grad_weights, grad_biases = pl.pallas_call(
        write_out,
        out_shape=tuple(jax.ShapeDtypeStruct(o.shape, o.dtype) for o in outs),
        in_specs=[vmem] * 4,
        out_specs=(pl.BlockSpec(memory_space=pltpu.HBM),) * 4,
        scratch_shapes=[dma((4,))],
        compiler_params=pltpu.CompilerParams(vmem_limit_bytes=8 << 20),
        name="write_out",
    )(*outs)
    return states_out[None, None], adjoint_out[None, None], grad_weights, grad_biases


def solution(mesh):
    placed = (
        P("depth", "batch", None, None), P("depth", "batch", None, None), P("depth", None, None),
        P("depth", None), P(), P(),
    )
    return jax.shard_map(
        body, mesh=mesh, in_specs=placed,
        out_specs=(
            P("depth", "batch", None, None), P("depth", "batch", None, None), P("depth", None, None),
            P("depth", None),
        ),
        check_vma=False,
    )
```

```python
import jax
import jax.numpy as jnp
from jax import lax
from jax.experimental import pallas as pl
from jax.experimental.pallas import tpu as pltpu
from jax.sharding import PartitionSpec as P

MOST = 8
C = 32
LANES = 128
F = jnp.float32
BF = jnp.bfloat16
NT = (((1,), (1,)), ((), ()))


def split2(x):
    hi = x.astype(BF)
    return hi, (x - hi.astype(F)).astype(BF)


def dot3(packed, x):
    hi, lo = split2(x)
    return jnp.dot(packed, jnp.concatenate([hi, lo, hi], axis=0), preferred_element_type=F)


def pack3(matrix):
    hi, lo = split2(matrix)
    return jnp.concatenate([hi, hi, lo], axis=1)


def lane_masks():
    lane = lax.broadcasted_iota(jnp.int32, (C, LANES), 1)
    return lane < 64, lane % 64 == 0, lane % 64 == 63


def beside(x, masks):
    zero = jnp.zeros_like(x)
    return jnp.where(masks[1], zero, pltpu.roll(x, 1, 1)) + jnp.where(masks[2], zero, pltpu.roll(x, 127, 1))


def chunk_laps(chunks, count, masks):
    turned = [pltpu.roll(x, 64, 1) for x in chunks]
    laps = []
    for k in range(1, count + 1):
        above_below = turned[k] + jnp.where(masks[0], turned[k - 1], turned[k + 1])
        laps.append((above_below + beside(chunks[k], masks)) - 4.0 * chunks[k])
    return laps


def column_of(row, eye):
    return jnp.sum(jnp.where(eye, jnp.broadcast_to(row, (C, C)), 0.0), axis=1, keepdims=True)


def row_of(column, eye):
    return jnp.sum(jnp.where(eye, jnp.broadcast_to(column, (C, C)), 0.0), axis=0, keepdims=True)


def spread(matrix, out_ref):
    for k in range(C):
        out_ref[k] = jnp.broadcast_to(matrix[:, k : k + 1], (C, LANES))


def mix(spread_ref, x, first):
    sums = [first, None]
    for step in range(C):
        k = step % 4 * 8 + step // 4
        term = spread_ref[k] * jnp.broadcast_to(x[k : k + 1, :], (C, LANES))
        sums[step % 2] = term if sums[step % 2] is None else sums[step % 2] + term
    return sums[0] + sums[1]


def kernel(
    guess_hbm, adj_hbm, w_hbm, b_hbm, d_hbm, n_hbm,
    s_out, a_out, gw_out, gb_out,
    A, T, H, G, LR, LSEND, S, S2, TAU, TAU_A,
    WC, WT, BB, FD, SPA, SPAT, SPB, SPBT, CB, GB, PK, GR,
    push_s, push_r, lam_s, lam_r, tau_s, tau_r, par_s, par_r, one_s, one_r, two_s, st_r, grad_s, grad_r,
    guess_ref, adj_ref, w_ref, b_ref, d_ref, n_ref, in_s,
):
    sections, images = lax.axis_size("depth"), lax.axis_size("batch")
    d, image = lax.axis_index("depth"), lax.axis_index("batch")
    chunks = guess_ref.shape[1] // LANES
    blocks = 2
    NB = chunks // blocks
    halo = MOST // 2
    cut = (3 * chunks) // 8
    parts = ((0, cut), (cut, chunks))
    core, chip, chips = d % 2, d // 2, sections // 2
    has_prev, has_next = d > 0, d < sections - 1
    even = core == 0
    odd = core == 1
    early = chips // 4 + 1
    ahead = jnp.where(even, MOST, jnp.where(chip >= (12 * chips) // 16, MOST, jnp.clip(2 * (chip - (9 * chips) // 16), 0, MOST)))
    masks = lane_masks()
    eye = lax.broadcasted_iota(jnp.int32, (C, C), 0) == lax.broadcasted_iota(jnp.int32, (C, C), 1)

    def at(c):
        return pl.ds(pl.multiple_of(c * LANES, LANES), LANES)

    def copy(src, dst, ssem, rsem, depth_to, image_to=None):
        return pltpu.make_async_remote_copy(
            src_ref=src, dst_ref=dst, send_sem=ssem, recv_sem=rsem,
            device_id=(depth_to, image if image_to is None else image_to),
            device_id_type=pl.DeviceIdType.MESH,
        )

    def brought(src, dst, sem):
        return pltpu.make_async_copy(src, dst, sem)

    small = [
        brought(src, dst, in_s.at[i])
        for i, (src, dst) in enumerate(((n_hbm, n_ref), (w_hbm, w_ref), (b_hbm, b_ref), (d_hbm, d_ref)))
    ]
    guess_in, adj_in = brought(guess_hbm, guess_ref, in_s.at[4]), brought(adj_hbm, adj_ref, in_s.at[5])
    for part in small:
        part.start()
    guess_in.start()
    adj_in.start()

    barrier = pltpu.get_barrier_semaphore()

    def greet(cond, depth_to, image_to):
        @pl.when(cond)
        def _():
            pl.semaphore_signal(barrier, inc=1, device_id=(depth_to, image_to), device_id_type=pl.DeviceIdType.MESH)

    up2, down2 = jnp.logical_and(odd, chip < chips - 1), jnp.logical_and(odd, chip > 0)
    greet(has_prev, d - 1, image)
    greet(has_next, d + 1, image)
    greet(up2, d + 2, image)
    greet(down2, d - 2, image)
    for o in range(1, images):
        pl.semaphore_signal(
            barrier, inc=1, device_id=(d, (image + o) % images), device_id_type=pl.DeviceIdType.MESH
        )
    partners = (
        has_prev.astype(jnp.int32) + has_next.astype(jnp.int32) + up2.astype(jnp.int32)
        + down2.astype(jnp.int32) + (images - 1)
    )

    starts, ends = jnp.logical_not(has_prev), jnp.logical_not(has_next)

    zero_chunk = jnp.zeros((C, LANES), F)
    for l in range(MOST + 1):
        for ref in (A, H):
            ref[l, 0] = zero_chunk
            ref[l, chunks + 1] = zero_chunk
    for ref in (G.at[0], G.at[1], LR):
        ref[0] = zero_chunk
        ref[chunks + 1] = zero_chunk

    for part in small:
        part.wait()
    n = n_ref[d]
    diff_col = column_of(d_ref[...], eye)
    diff = jnp.broadcast_to(diff_col, (C, LANES))

    def prepare(i, _):
        factor = jnp.where(i < n, 1.0 / MOST, 0.0)
        WC[i] = pack3(w_ref[i])
        WT[i] = pack3(w_ref[i].T * factor)
        BB[i] = jnp.broadcast_to(column_of(b_ref[pl.ds(i, 1), :], eye), (C, LANES))
        FD[i] = diff * factor
        return 0

    lax.fori_loop(0, MOST, prepare, 0, unroll=True)
    guess_in.wait()
    for c in range(chunks):
        H[0, c + 1] = guess_ref[:, c * LANES : (c + 1) * LANES]

    def forward_tile(src, i, lo, count, dst, keep, open_end):
        u = [src[lo + k] for k in range(count + 1)] + [zero_chunk if open_end else src[lo + count + 1]]
        laps = chunk_laps(u, count, masks)
        bias = jnp.concatenate([BB[i]] * count, axis=1)
        act = jnp.tanh(dot3(WC[i], jnp.concatenate(u[1:-1], axis=1)) + bias)
        mixed = dot3(WT[i], act)
        fd = FD[i]
        for k in range(count):
            dst[lo + k + 1] = u[k + 1] + fd * laps[k] - mixed[:, k * LANES : (k + 1) * LANES]
            if keep is not None:
                keep[lo + k] = act[:, k * LANES : (k + 1) * LANES]

    def into(ref, shift):
        def store(c, value):
            ref[c + shift] = value
        return store

    def sweep(stack, keeps, lo, count, open_end):
        def layer(i, _):
            keep = None if keeps is None else keeps.at[i]
            forward_tile(stack.at[i], i, lo, wide, stack.at[i + 1], keep, open_end)
            return 0

        wide = count
        lax.fori_loop(0, MOST // 2, layer, 0)
        wide = count - halo // 2 if open_end else count
        lax.fori_loop(MOST // 2, MOST, layer, 0)

    upper = cut + halo

    def push_copy(j):
        part = pl.ds(1, upper) if j == 0 else pl.ds(1 + upper, chunks - upper)
        return copy(H.at[MOST, part], A.at[0, part], push_s.at[j], push_r.at[j], d + 1)

    def push(j):
        @pl.when(has_next)
        def _():
            push_copy(j).start()

    first = min(upper + halo, chunks)
    sweep(H, None, 0, first, first < chunks)
    pl.semaphore_wait(barrier, partners)
    push(0)
    sweep(H, None, upper, chunks - upper, False)
    push(1)

    part_copies = [
        copy(SPA, SPA, par_s.at[0], par_r.at[0], d + 1),
        copy(SPAT, SPAT, par_s.at[1], par_r.at[1], d + 1),
        copy(CB.at[0:2], CB.at[0:2], par_s.at[2], par_r.at[2], d + 1),
    ]

    def first_copy(c):
        return copy(guess_ref.at[:, at(c)], S.at[c], two_s.at[0], st_r.at[c], d + 1)

    @pl.when(starts)
    def _():
        for c in range(chunks):
            first_copy(c).start()

    def propagator(matrix_ref, back_ref, row):
        spread(w_ref[0], matrix_ref)
        spread(w_ref[0].T * -coarse, back_ref)
        CB[row] = BB[0]
        CB[row + 1] = diff * coarse

    coarse = n.astype(F) / MOST

    @pl.when(even)
    def _():
        propagator(SPA, SPAT, 0)
        for part in part_copies:
            part.start()

    @pl.when(odd)
    def _():
        propagator(SPB, SPBT, 2)

    layers = n.astype(F)

    def tau_of(c):
        start = A[0, c + 1]
        return A[MOST, c + 1] - (start + layers * (A[1, c + 1] - start))

    def tau_copy(j):
        part = pl.ds(0, cut) if j == 0 else pl.ds(cut, chunks + 1 - cut)
        return copy(TAU.at[part], TAU_A.at[part], tau_s.at[j], tau_r.at[j], d + 1)

    @pl.when(starts)
    def _():
        for c in range(chunks):
            A[0, c + 1] = guess_ref[:, c * LANES : (c + 1) * LANES]

    def push_arrived(j):
        @pl.when(has_prev)
        def _():
            push_copy(j).wait_recv()

    @pl.when(even)
    def _():
        for j, (lo, hi) in enumerate(parts):
            push_arrived(j)
            if j == 0:
                sweep(A, T, 0, upper, True)
            else:
                sweep(A, T, cut, chunks - cut, False)
            before = zero_chunk if j == 0 else tau_of(cut - 1)
            for c in range(lo, hi):
                here = tau_of(c)
                TAU[c] = jnp.where(masks[0], here, before)
                before = here
            if j == 1:
                TAU[chunks] = jnp.where(masks[0], 0.0, before)
            tau_copy(j).start()

    @pl.when(odd)
    def _():
        for j in range(2):
            push_arrived(j)
        sweep(A, T, 0, chunks, False)
        for c in range(chunks):
            TAU[c] = tau_of(c)

    hand = (0, cut, chunks - chunks // 8, chunks)

    def one_copy(p):
        part = pl.ds(hand[p], hand[p + 1] - hand[p])
        return copy(S.at[part], S.at[part], one_s.at[p], one_r.at[p], d - 1)

    def two_copy(c):
        return copy(S2.at[c], S.at[c], two_s.at[0], st_r.at[c], d + 2)

    def relay(both):
        for part in part_copies:
            part.wait_recv()
        bias_a, fd_a, bias_b, fd_b = CB[0], CB[1], CB[2], CB[3]
        lower = masks[0]

        def step(c, carry, first=False, last=False):
            prev, one_prev = carry
            if last:
                now = zero_chunk
            else:
                two_copy(c).wait_recv()
                now = S[c]
            mid = jnp.where(lower, now, prev)
            lap = (pltpu.roll(prev + now, 64, 1) + beside(mid, masks)) - 4.0 * mid
            act = jnp.tanh(mix(SPA, mid, bias_a))
            one = mix(SPAT, act, mid + fd_a * lap + TAU_A[c])
            if first:
                one = jnp.where(lower, one, 0.0)
            if last:
                one = jnp.where(lower, 0.0, one)
            if not first:
                mid_one = jnp.where(lower, one_prev, one)
                if both:
                    lap_b = (pltpu.roll(one_prev + one, 64, 1) + beside(mid_one, masks)) - 4.0 * mid_one
                    act_b = jnp.tanh(mix(SPB, mid_one, bias_b))
                    S2[c - 1] = mix(SPBT, act_b, mid_one + fd_b * lap_b + TAU[c - 1])
                    two_copy(c - 1).start()
                s_out[:, at(c - 1)] = mid_one
            return now, one

        tau_copy(0).wait_recv()
        carry = step(0, (zero_chunk,) * 2, first=True)
        for p in range(3):
            if p == 1:
                tau_copy(1).wait_recv()
            carry = lax.fori_loop(max(1, hand[p]), hand[p + 1], step, carry)
            one_copy(p).start()
        step(chunks, carry, last=True)

    def backward_block(src, i, j, store, with_grads):
        g = [src[j * NB + k] for k in range(NB + 2)]
        laps = chunk_laps(g, NB, masks)
        act = jnp.concatenate([T[i, j * NB + k] for k in range(NB)], axis=1)
        g_hi, g_lo = split2(jnp.concatenate(g[1:-1], axis=1))
        pulled = jnp.dot(WC[i], jnp.concatenate([g_hi, g_lo, g_hi], axis=0), preferred_element_type=F)
        pre = (1.0 - act * act) * pulled
        p_hi, p_lo = split2(pre)
        back = jnp.dot(WT[i], jnp.concatenate([p_hi, p_lo, p_hi], axis=0), preferred_element_type=F)
        fd = FD[i]
        for k in range(NB):
            store(j * NB + k, g[k + 1] + fd * laps[k] - back[:, k * LANES : (k + 1) * LANES])
        if not with_grads:
            return None
        t_hi, t_lo = split2(act)
        u_hi, u_lo = split2(jnp.concatenate([A[i, j * NB + k + 1] for k in range(NB)], axis=1))
        left = jnp.concatenate(
            [jnp.concatenate([t_hi, p_hi], axis=1), jnp.concatenate([t_lo, p_lo], axis=1)], axis=0
        )
        right = jnp.concatenate(
            [jnp.concatenate([g_hi, u_hi], axis=1), jnp.concatenate([g_lo, u_lo], axis=1)], axis=0
        )
        prod = lax.dot_general(left, right, NT, preferred_element_type=F)
        bias_sum = pre[:, :LANES]
        for k in range(1, NB):
            bias_sum = bias_sum + pre[:, k * LANES : (k + 1) * LANES]
        return prod, bias_sum

    def lam_copy(j):
        return copy(LSEND.at[pl.ds(j * NB, NB)], LR.at[pl.ds(1 + j * NB, NB)], lam_s.at[j], lam_r.at[j], d - 1)

    def backward_start():
        adj_in.wait()
        for c in range(chunks):
            G[0, c + 1] = adj_ref[:, c * LANES : (c + 1) * LANES]

        def layer(i, _):
            def block(j, _):
                backward_block(G.at[i % 2], MOST - 1 - i, j, into(G.at[(i + 1) % 2], 1), False)
                return 0
            lax.fori_loop(0, blocks, block, 0, unroll=True)
            return 0

        lax.fori_loop(0, MOST - 1, layer, 0)

        def block(j, _):
            backward_block(G.at[(MOST - 1) % 2], 0, j, into(LSEND, 0), False)

            @pl.when(has_prev)
            def _():
                lam_copy(j).start()
            return 0

        lax.fori_loop(0, blocks, block, 0)

    def full_ready():
        @pl.when(has_next)
        def _():
            for j in range(blocks):
                lam_copy(j).wait_recv()

        @pl.when(ends)
        def _():
            for c in range(chunks):
                LR[c + 1] = adj_ref[:, c * LANES : (c + 1) * LANES]

        for c in range(chunks):
            G[0, c + 1] = LR[c + 1]
        GB[MOST] = jnp.zeros((C, C), F)
        PK[...] = jnp.zeros_like(PK)

    def full_layers(first_layer, end_layer):
        def layer(i, _):
            slot = MOST - 1 - i
            factor = jnp.where(slot < n, 1.0 / MOST, 0.0)
            start = (jnp.zeros((2 * C, 2 * C), F), jnp.zeros((C, LANES), F))

            def block(j, sums):
                prod, bias_sum = backward_block(G.at[i % 2], slot, j, into(G.at[(i + 1) % 2], 1), True)
                return sums[0] + prod, sums[1] + bias_sum
            prod, bias_sum = lax.fori_loop(0, blocks, block, start, unroll=True)
            GB[slot] = -factor * (prod[:C, :C] + (prod[:C, C:] + prod[C:, :C]))
            column = jnp.sum(bias_sum, axis=1, keepdims=True)
            GB[MOST, pl.ds(slot, 1), :] = -factor * row_of(column, eye)
            return 0

        lax.fori_loop(first_layer, end_layer, layer, 0)

    side = LANES // C

    def share_grads():
        for g in range(MOST // side):
            PK[g * C : (g + 1) * C] = jnp.concatenate([GB[g * side + k] for k in range(side)], axis=1)
        PK[MOST // side * C :, :C] = GB[MOST, :MOST]
        GR[image] = PK[...]
        for o in range(1, images):
            grad_copy(o).start()
        for c in range(chunks):
            a_out[:, c * LANES : (c + 1) * LANES] = G[0, c + 1]

    def grad_copy(o):
        return copy(PK, GR.at[image], grad_s.at[o - 1], grad_r.at[o - 1], d, (image + o) % images)

    def turn(order, _):
        here = jnp.logical_and(odd, order == jnp.where(chip < early, 0, 3))

        @pl.when(jnp.logical_and(here, chip < chips - 1))
        def _():
            relay(True)

        @pl.when(jnp.logical_and(here, chip == chips - 1))
        def _():
            relay(False)

        @pl.when(order == 1)
        def _():
            backward_start()

        @pl.when(order == jnp.where(ahead > 0, 2, 4))
        def _():
            full_ready()

        @pl.when(jnp.logical_or(order == 2, order == 4))
        def _():
            full_layers(jnp.where(order == 2, 0, ahead), jnp.where(order == 2, ahead, MOST))

        @pl.when(order == jnp.where(ahead == MOST, 2, 4))
        def _():
            share_grads()
        return 0

    lax.fori_loop(0, 5, turn, 0)
    for o in range(1, images):
        grad_copy(o).wait_recv()
    total = GR[0]
    for b in range(1, images):
        total = total + GR[b]
    for i in range(MOST):
        row, lane = i // side * C, i % side * C
        gw_out[i] = total[row : row + C, lane : lane + C]
    gb_out[...] = total[MOST // side * C :, :C]

    @pl.when(even)
    def _():
        for p in range(3):
            one_copy(p).wait_recv()
            for c in range(hand[p], hand[p + 1]):
                s_out[:, c * LANES : (c + 1) * LANES] = S[c]

    for o in range(1, images):
        grad_copy(o).wait_send()

    @pl.when(has_next)
    def _():
        for j in range(blocks):
            push_copy(j).wait_send()

    @pl.when(has_prev)
    def _():
        for j in range(blocks):
            lam_copy(j).wait_send()

    @pl.when(even)
    def _():
        for part in part_copies:
            part.wait_send()
        for j in range(blocks):
            tau_copy(j).wait_send()

    @pl.when(odd)
    def _():
        for p in range(3):
            one_copy(p).wait_send()

    @pl.when(jnp.logical_or(starts, up2))
    def _():
        part = pl.ds(0, chunks)
        copy(S2.at[part], S.at[part], two_s.at[0], st_r.at[0], d + 1).wait_send()


def write_out(*refs):
    sems = refs[8]
    copies = [pltpu.make_async_copy(refs[i], refs[i + 4], sems.at[i]) for i in range(4)]
    for one in copies:
        one.start()
    for one in copies:
        one.wait()


def body(cpoint_guess, adjoint_guess, weights, biases, diffusion, section_len):
    pixels = cpoint_guess.shape[-1]
    images = lax.axis_size("batch")
    chunks = pixels // LANES
    blocks = 2
    vmem = pl.BlockSpec(memory_space=pltpu.VMEM)
    image_shape = jax.ShapeDtypeStruct((C, pixels), F)
    dma = pltpu.SemaphoreType.DMA

    def stack(*lead):
        return pltpu.VMEM(lead + (C, LANES), F)

    outs = pl.pallas_call(
        kernel,
        out_shape=(
            image_shape, image_shape,
            jax.ShapeDtypeStruct((MOST, C, C), F), jax.ShapeDtypeStruct((MOST, C), F),
        ),
        in_specs=[pl.BlockSpec(memory_space=pltpu.HBM)] * 6,
        out_specs=(vmem,) * 4,
        scratch_shapes=[
            stack(MOST + 1, chunks + 2), stack(MOST, chunks), stack(MOST + 1, chunks + 2), stack(2, chunks + 2),
            stack(chunks + 2), stack(chunks), stack(chunks), stack(chunks), stack(chunks + 1), stack(chunks + 1),
            pltpu.VMEM((MOST, C, 3 * C), BF), pltpu.VMEM((MOST, C, 3 * C), BF), stack(MOST), stack(MOST),
            stack(C), stack(C), stack(C), stack(C), stack(4),
            pltpu.VMEM((MOST + 1, C, C), F),
            pltpu.VMEM((MOST // 4 * C + MOST, LANES), F), pltpu.VMEM((images, MOST // 4 * C + MOST, LANES), F),
            dma((blocks,)), dma((blocks,)), dma((blocks,)), dma((blocks,)), dma((blocks,)), dma((blocks,)),
            dma((3,)), dma((3,)), dma((3,)), dma((3,)), dma((1,)), dma((chunks,)),
            dma((images - 1,)), dma((images - 1,)),
            pltpu.VMEM((C, pixels), F), pltpu.VMEM((C, pixels), F),
            pltpu.VMEM((MOST, C, C), F), pltpu.VMEM((MOST, C), F), pltpu.VMEM((1, C), F),
            pltpu.SMEM(section_len.shape, jnp.int32), dma((6,)),
        ],
        compiler_params=pltpu.CompilerParams(
            collective_id=0, has_side_effects=True, vmem_limit_bytes=32 << 20
        ),
        name="mgrit_cycle",
    )(
        *(
            pltpu.with_memory_space_constraint(x, pltpu.HBM)
            for x in (
                cpoint_guess.reshape(C, pixels), adjoint_guess.reshape(C, pixels), weights, biases,
                diffusion.reshape(1, C), section_len,
            )
        )
    )
    states_out, adjoint_out, grad_weights, grad_biases = pl.pallas_call(
        write_out,
        out_shape=tuple(jax.ShapeDtypeStruct(o.shape, o.dtype) for o in outs),
        in_specs=[vmem] * 4,
        out_specs=(pl.BlockSpec(memory_space=pltpu.HBM),) * 4,
        scratch_shapes=[dma((4,))],
        compiler_params=pltpu.CompilerParams(vmem_limit_bytes=8 << 20),
        name="write_out",
    )(*outs)
    return states_out[None, None], adjoint_out[None, None], grad_weights, grad_biases


def solution(mesh):
    placed = (
        P("depth", "batch", None, None), P("depth", "batch", None, None), P("depth", None, None),
        P("depth", None), P(), P(),
    )
    return jax.shard_map(
        body, mesh=mesh, in_specs=placed,
        out_specs=(
            P("depth", "batch", None, None), P("depth", "batch", None, None), P("depth", None, None),
            P("depth", None),
        ),
        check_vma=False,
    )
```
